32 devices in a mesh: frames: 8 (over z, core), heads: 4 (over y, x).
Axes of the slice: x: 2, y: 2, z: 4, core: 2. Of those that a mesh axis runs over, the one named last changes fastest.
Arguments:
- clip: bfloat16 [16, 8, 128, 320], P('frames', 'heads'), may hold values from -6 to 6
- w_time: bfloat16 [3, 320, 320], replicated, may hold values from -0.1875 to 0.1875
- w_down: bfloat16 [320, 1280], replicated, may hold values from -0.3125 to 0.3125
- w_embed: bfloat16 [320, 1280], replicated, may hold values from -0.3125 to 0.3125
- w_qkv: bfloat16 [1280, 3840], P(None, 'heads'), may hold values from -0.15625 to 0.15625
- w_out: bfloat16 [1280, 1280], P('heads'), may hold values from -0.15625 to 0.15625
- w_up: bfloat16 [1280, 320], replicated, may hold values from -0.15625 to 0.15625
- timestep: int32 [1], replicated, may hold values from 0 to 999
- cotangent: bfloat16 [16, 8, 128, 320], P('frames', 'heads'), may hold values from -6 to 6
Outputs:
- output: bfloat16 [16, 8, 128, 320], P('frames', 'heads')
- grad_clip: float32 [16, 8, 128, 320], P('frames', 'heads')
- grad_time: float32 [3, 320, 320], replicated
- grad_down: float32 [320, 1280], replicated
- grad_embed: float32 [320, 1280], replicated
- grad_qkv: float32 [1280, 3840], P(None, 'heads')
- grad_out: float32 [1280, 1280], P('heads')
- grad_up: float32 [1280, 320], replicated
The draws below stay inside these ranges and needn't reach their ends.
All inputs are finite; a program needn't handle non-finite values.
Results may differ from the reference program's by a relative error of at most 0.024.
Values may be sent and summed in bfloat16 or wider, within the bound.
No kernel may reach another device: no remote copies, remote signals or barrier semaphores. Data moves between devices by JAX's collectives and lax.ppermute only.
A program may use at most 128 MiB of HBM per device.

```python
import math
import jax
import jax.numpy as jnp
from jax import lax

C = 320
CC = 1280
HEADS = 16
HD = 80
TEMB = 320
COLS = 128
F = 16
ROWS = 8


def steps_of(own_key, shape, cuts, least, largest):
    gain = 1.0
    for position, blocks in cuts:
        draws = jax.random.uniform(jax.random.fold_in(jax.random.fold_in(own_key, 6), position), (blocks,), jnp.float32, least / len(cuts), largest / len(cuts))
        gain = gain * jnp.repeat(jnp.exp(draws), shape[position] // blocks).reshape((-1,) + (1,) * (len(shape) - 1 - position))
    return gain


def scatter_about(key, extent, scale, limit, cuts=(), held_as=jnp.bfloat16):
    level = steps_of(key, extent, cuts, -0.22, 0.18) if cuts else 1.0
    entries = jax.random.normal(key, extent, jnp.float32) * scale * level
    return jnp.minimum(jnp.maximum(entries, -limit), limit).astype(held_as)


def setup_inputs(seed: int = 0) -> dict:
    splits = jax.random.split(jax.random.key(seed), 10)
    return {
        "clip": scatter_about(splits[0], (F, ROWS, COLS, C), 1.0, 6.0, ((0, 8), (1, 4))),
        "w_time": scatter_about(splits[1], (3, C, C), (3 * C) ** -0.5, 0.1875),
        "w_down": scatter_about(splits[2], (C, CC), C ** -0.5, 0.3125),
        "w_embed": scatter_about(splits[3], (TEMB, CC), TEMB ** -0.5, 0.3125),
        "w_qkv": scatter_about(splits[4], (CC, 3 * CC), CC ** -0.5, 0.15625, ((1, 4),)),
        "w_out": scatter_about(splits[5], (CC, CC), CC ** -0.5, 0.15625, ((0, 4),)),
        "w_up": scatter_about(splits[6], (CC, C), CC ** -0.5, 0.15625),
        "timestep": jax.random.randint(splits[7], (1,), 0, 1000).astype(jnp.int32),
        "cotangent": scatter_about(splits[8], (F, ROWS, COLS, C), 1.0, 6.0, ((0, 8), (1, 4))),
    }


def matmul(left, right):
    return jnp.dot(left, right, preferred_element_type=jnp.float32)

def upsample(field):
    return jnp.repeat(jnp.repeat(jnp.repeat(field, 2, 0), 2, 1), 2, 2)

def time_embed(timestep, width):
    half = width // 2
    freqs = jnp.exp(-math.log(10000.0) * jnp.arange(half, dtype=jnp.float32) / half)
    angle = timestep.astype(jnp.float32)[0] * freqs
    return jax.nn.silu(jnp.concatenate([jnp.cos(angle), jnp.sin(angle)])).astype(jnp.bfloat16)

def reference(clip, w_time, w_down, w_embed, w_qkv, w_out, w_up, timestep, cotangent):
    frames, rows, columns, chans = clip.shape
    width = w_down.shape[1]
    half_f, half_r, half_c = (frames // 2, rows // 2, columns // 2)
    places = half_r * half_c
    scale = 1.0 / math.sqrt(HD)
    padded = jnp.pad(clip, ((1, 1), (0, 0), (0, 0), (0, 0)))
    branch = jnp.zeros((frames * rows * columns, chans), jnp.float32)
    for tap in range(3):
        branch = branch + matmul(padded[tap:tap + frames].reshape(-1, chans), w_time[tap])
    hidden = (clip.astype(jnp.float32).reshape(-1, chans) + branch).astype(jnp.bfloat16)
    hidden_f = hidden.astype(jnp.float32).reshape(frames, rows, columns, chans)
    pooled = hidden_f.reshape(half_f, 2, half_r, 2, half_c, 2, chans).mean(axis=(1, 3, 5))
    pooled = pooled.astype(jnp.bfloat16).reshape(-1, chans)
    embed = time_embed(timestep, w_embed.shape[0])
    shift = matmul(embed[None, :], w_embed)
    coarse = (matmul(pooled, w_down) + shift).astype(jnp.bfloat16)
    qkv = matmul(coarse, w_qkv).astype(jnp.bfloat16).reshape(half_f, places, HEADS, 3, HD)
    query = qkv[:, :, :, 0].astype(jnp.float32)
    keys = qkv[:, :, :, 1].astype(jnp.float32)
    values = qkv[:, :, :, 2].astype(jnp.float32)
    scores = jnp.einsum('tpnd,spnd->ntsp', query, keys) * scale
    probs = jax.nn.softmax(scores, axis=2)
    weights = probs.astype(jnp.bfloat16)
    attended = jnp.einsum('ntsp,spnd->tpnd', weights.astype(jnp.float32), values)
    attended = attended.astype(jnp.bfloat16).reshape(-1, width)
    coarse_out = (coarse.astype(jnp.float32) + matmul(attended, w_out)).astype(jnp.bfloat16)
    lifted = matmul(coarse_out, w_up).reshape(half_f, half_r, half_c, chans)
    output = (hidden_f + upsample(lifted)).astype(jnp.bfloat16)
    upstream = cotangent.astype(jnp.float32)
    pooled_grad = upstream.reshape(half_f, 2, half_r, 2, half_c, 2, chans).sum(axis=(1, 3, 5))
    pooled_grad = pooled_grad.astype(jnp.bfloat16).reshape(-1, chans)
    grad_up = matmul(coarse_out.T, pooled_grad)
    back_in = matmul(pooled_grad, w_up.T).astype(jnp.bfloat16)
    grad_out = matmul(attended.T, back_in)
    attend_grad = matmul(back_in, w_out.T).astype(jnp.bfloat16).reshape(half_f, places, HEADS, HD)
    attend_f = attend_grad.astype(jnp.float32)
    weight_grad = jnp.einsum('tpnd,spnd->ntsp', attend_f, values)
    score_grad = probs * (weight_grad - lax.optimization_barrier(jnp.sum(probs * weight_grad, axis=2, keepdims=True))) * scale
    score_f = score_grad.astype(jnp.bfloat16).astype(jnp.float32)
    query_grad = jnp.einsum('ntsp,spnd->tpnd', score_f, keys)
    keys_grad = jnp.einsum('ntsp,tpnd->spnd', score_f, query)
    values_grad = jnp.einsum('ntsp,tpnd->spnd', weights.astype(jnp.float32), attend_f)
    qkv_grad = jnp.stack([query_grad, keys_grad, values_grad], axis=3).astype(jnp.bfloat16)
    qkv_grad = qkv_grad.reshape(-1, 3 * width)
    grad_qkv = matmul(coarse.T, qkv_grad)
    coarse_grad = (matmul(qkv_grad, w_qkv.T) + back_in.astype(jnp.float32)).astype(jnp.bfloat16)
    column_sum = lax.optimization_barrier(jnp.sum(coarse_grad.astype(jnp.float32), axis=0))
    grad_embed = embed.astype(jnp.float32)[:, None] * column_sum[None, :]
    grad_down = matmul(pooled.T, coarse_grad)
    spread = matmul(coarse_grad, w_down.T).reshape(half_f, half_r, half_c, chans)
    hidden_grad = (upstream + upsample(spread) * 0.125).astype(jnp.bfloat16)
    grad_padded = jnp.pad(hidden_grad, ((1, 1), (0, 0), (0, 0), (0, 0)))
    flat_grad = hidden_grad.reshape(-1, chans)
    grad_clip = flat_grad.astype(jnp.float32)
    taps = []
    for tap in range(3):
        grad_clip = grad_clip + matmul(grad_padded[2 - tap:2 - tap + frames].reshape(-1, chans), w_time[tap].T)
        taps.append(matmul(padded[tap:tap + frames].reshape(-1, chans).T, flat_grad))
    grad_clip = grad_clip.reshape(frames, rows, columns, chans)
    grad_time = jnp.stack(taps)
    return (output, grad_clip, grad_time, grad_down, grad_embed, grad_qkv, grad_out, grad_up)
```

```python
import functools
import math

import jax
import jax.numpy as jnp
from jax import lax
from jax.experimental import pallas as pl
from jax.experimental.pallas import tpu as pltpu
from jax.sharding import PartitionSpec as P

HD = 80
SLOT = 128
BF = jnp.bfloat16
F32 = jnp.float32


def nn(a, b):
    return lax.dot_general(a, b, (((1,), (0,)), ((), ())), preferred_element_type=F32)


def nt(a, b):
    return lax.dot_general(a, b, (((1,), (1,)), ((), ())), preferred_element_type=F32)


def tn(a, b):
    return lax.dot_general(a, b, (((0,), (0,)), ((), ())), preferred_element_type=F32)


def round_up(value, step):
    return -(-value // step) * step


def call(kernel, out_shape, **kw):
    return pl.pallas_call(
        kernel,
        out_shape=out_shape,
        compiler_params=pltpu.CompilerParams(vmem_limit_bytes=56 * 1024 * 1024),
        **kw,
    )


def smem():
    return pl.BlockSpec(memory_space=pltpu.SMEM)


def vmem():
    return pl.BlockSpec(memory_space=pltpu.VMEM)


def sds(shape, dtype):
    return jax.ShapeDtypeStruct(shape, dtype)


def bit_list(count):
    bits = []
    while (1 << len(bits)) < count:
        bits.append(1 << len(bits))
    return bits


def reversed_bits(value, count):
    n = len(bit_list(count))
    out = 0
    for i in range(n):
        out = out + (((value >> i) & 1) << (n - 1 - i))
    return out


def swap(x, axis, bit):
    n = lax.axis_size(axis)
    return lax.ppermute(x, axis, [(i, i ^ bit) for i in range(n)])


def time_embed(timestep, width):
    half = width // 2
    freqs = jnp.exp(-math.log(10000.0) * jnp.arange(half, dtype=F32) / half)
    angle = timestep.astype(F32)[0] * freqs
    return jax.nn.silu(jnp.concatenate([jnp.cos(angle), jnp.sin(angle)])).astype(BF)


def pool_matrix(half_c, columns):
    row = lax.broadcasted_iota(jnp.int32, (half_c, 2 * columns), 0)
    col = lax.broadcasted_iota(jnp.int32, (half_c, 2 * columns), 1)
    col = jnp.where(col >= columns, col - columns, col)
    return jnp.where((col >> 1) == row, 1.0, 0.0).astype(BF)


def lift_matrix(half_c, columns):
    row = lax.broadcasted_iota(jnp.int32, (2 * columns, half_c), 0)
    col = lax.broadcasted_iota(jnp.int32, (2 * columns, half_c), 1)
    row = jnp.where(row >= columns, row - columns, row)
    return jnp.where((row >> 1) == col, 1.0, 0.0).astype(BF)


def pool_kernel(me, clip, cot, keep, send, tmp):
    half_c = tmp.shape[1]
    half = half_c // 2
    quart = half // 2
    columns = clip.shape[1] // 2
    pool = pool_matrix(half_c, columns)
    tmp[0] = nn(pool, clip[0]) * 0.25
    tmp[1] = nn(pool, clip[1]) * 0.25
    tmp[2] = nn(pool, cot[0]) + nn(pool, cot[1])
    core = me[0] & 1
    for color in range(2):
        for item in range(3):
            base = pl.multiple_of(core * half + color * quart, quart)
            keep[color, item] = tmp[item, pl.ds(base, quart), :].astype(BF)
            base = pl.multiple_of((1 - core) * half + color * quart, quart)
            send[color, item] = tmp[item, pl.ds(base, quart), :].astype(BF)


def weight_kernel(w_down, w_embed, embed, w_qkv, w_out, w_up, down, mix, out_mix, direct):
    chans = w_down.shape[0]
    padded = down.shape[0]
    shift = nn(embed[...], w_embed[...])
    high = shift.astype(BF)
    low = (shift - high.astype(F32)).astype(BF)
    down[0:chans, :] = w_down[...]
    row = lax.broadcasted_iota(jnp.int32, (padded - chans, shift.shape[1]), 0)
    tail = jnp.where(row == 0, high.astype(F32), jnp.where(row == 1, low.astype(F32), 0.0))
    down[chans:padded, :] = tail.astype(BF)
    full = down[...]
    pieces = w_qkv.shape[1] // HD
    prod = nn(full, w_qkv[...])
    mix[...] = jnp.zeros(mix.shape, BF)
    for i in range(pieces):
        mix[:, i * SLOT : i * SLOT + HD] = prod[:, i * HD : (i + 1) * HD].astype(BF)
    up = w_up[...]
    small = nn(w_out[...], up)
    out_mix[...] = jnp.zeros(out_mix.shape, BF)
    for i in range(pieces // 3):
        out_mix[i * SLOT : i * SLOT + HD, :] = small[i * HD : (i + 1) * HD, :].astype(BF)
    direct[...] = nn(full, up).astype(BF)


def fine_kernel(clip, clip_lo, clip_hi, cot, cot_lo, cot_hi, w_time, hidden, base, taps):
    frames = clip.shape[0]

    def pick(body, lo, hi, t):
        return lo[...] if t < 0 else (hi[...] if t >= frames else body[t])

    chans = w_time.shape[1]
    taps[3 * chans :, :] = jnp.zeros((taps.shape[0] - 3 * chans, chans), BF)
    for tap in range(3):
        acc = None
        for t in range(frames):
            part = tn(pick(clip, clip_lo, clip_hi, t + tap - 1), cot[t])
            acc = part if acc is None else acc + part
        taps[tap * chans : (tap + 1) * chans, :] = acc.astype(BF)
    for t in range(frames):
        acc = clip[t].astype(F32)
        grad = cot[t].astype(F32)
        for tap in range(3):
            acc = acc + nn(pick(clip, clip_lo, clip_hi, t + tap - 1), w_time[tap])
            grad = grad + nt(pick(cot, cot_lo, cot_hi, t + 1 - tap), w_time[tap])
        hidden[t] = acc.astype(BF)
        base[t] = grad


def coarse_kernel(
    me, first, second, w_time, mix, out_mix, direct, local, grad_mix, grad_att, gram, tap_keep, tap_send,
    shifted, centre, pooled, upper, qkv, att_grad, att, qkv_grad, fields, mix_acc, att_acc, gram_acc, tap_acc,
    *, coarse_frames, heads_axis,
):
    step = pl.program_id(0)
    frame = me[0]
    quart = first.shape[2]
    chans = first.shape[3]
    padded = pooled.shape[1]
    tokens = coarse_frames * quart
    chips = coarse_frames // 2
    heads = att.shape[1] // SLOT
    scale = 1.0 / math.sqrt(HD)
    part = 1.0 / heads_axis

    @pl.when(step == 0)
    def _():
        mix_acc[...] = jnp.zeros(mix_acc.shape, F32)
        att_acc[...] = jnp.zeros(att_acc.shape, F32)
        gram_acc[...] = jnp.zeros(gram_acc.shape, F32)
        tap_acc[...] = jnp.zeros(tap_acc.shape, F32)
        lane = lax.broadcasted_iota(jnp.int32, (2 * tokens, padded - chans), 1)
        pooled[:, chans:padded] = jnp.where(lane < 2, 1.0, 0.0).astype(BF)

    def entry(index):
        gap = index ^ frame
        return (reversed_bits(gap >> 1, chips) * 2 + (gap & 1)) * 3

    for color, source in ((0, first), (1, second)):
        before = jnp.zeros((quart, chans), F32)
        here = source[0, entry(0)].astype(F32)
        for u in range(coarse_frames):
            at = entry(u)
            last = source[0, at + 1].astype(F32)
            after = source[0, entry(u + 1)].astype(F32) if u + 1 < coarse_frames else jnp.zeros((quart, chans), F32)
            rows = pl.ds(color * tokens + u * quart, quart)
            mid = 0.5 * (here + last)
            shifted[0, rows, :] = (0.5 * (before + here)).astype(BF)
            shifted[1, rows, :] = mid.astype(BF)
            shifted[2, rows, :] = (0.5 * (last + after)).astype(BF)
            centre[rows, :] = mid
            upper[rows, :] = source[0, at + 2]
            before, here = last, after
    acc = centre[...]
    for tap in range(3):
        acc = acc + nn(shifted[tap], w_time[tap])
    pooled[:, 0:chans] = acc.astype(BF)
    qkv[...] = nn(pooled[...], mix[...]).astype(BF)
    att_grad[...] = nt(upper[...], out_mix[...]).astype(BF)
    row = lax.broadcasted_iota(jnp.int32, (tokens, tokens), 0)
    col = lax.broadcasted_iota(jnp.int32, (tokens, tokens), 1)
    same = (row & (quart - 1)) == (col & (quart - 1))
    for color in range(2):
        rows = slice(color * tokens, (color + 1) * tokens)
        for n in range(heads):
            q = qkv[rows, (3 * n) * SLOT : (3 * n + 1) * SLOT]
            k = qkv[rows, (3 * n + 1) * SLOT : (3 * n + 2) * SLOT]
            v = qkv[rows, (3 * n + 2) * SLOT : (3 * n + 3) * SLOT]
            da = att_grad[rows, n * SLOT : (n + 1) * SLOT]
            scores = jnp.where(same, nt(q, k) * scale, -jnp.inf)
            peak = jnp.max(scores, axis=1, keepdims=True)
            ex = jnp.exp(scores - peak)
            probs = ex / jnp.sum(ex, axis=1, keepdims=True)
            weights = probs.astype(BF)
            att[rows, n * SLOT : (n + 1) * SLOT] = nn(weights, v).astype(BF)
            dw = nt(da, v)
            inner = jnp.sum(probs * dw, axis=1, keepdims=True)
            ds = (probs * (dw - inner) * scale).astype(BF)
            qkv_grad[rows, (3 * n) * SLOT : (3 * n + 1) * SLOT] = nn(ds, k).astype(BF)
            qkv_grad[rows, (3 * n + 1) * SLOT : (3 * n + 2) * SLOT] = tn(ds, q).astype(BF)
            qkv_grad[rows, (3 * n + 2) * SLOT : (3 * n + 3) * SLOT] = tn(weights, da).astype(BF)
    lifted = nn(att[...], out_mix[...]) + nn(pooled[...], direct[...]) * part
    spread = nt(qkv_grad[...], mix[...]) + nt(upper[...], direct[...]) * part
    spread = spread[:, 0:chans]
    fields[0] = lifted.astype(BF).reshape(2 * coarse_frames, quart, chans)
    fields[1] = spread.astype(BF).reshape(2 * coarse_frames, quart, chans)
    mine = (frame >> 1) * 2
    for color in range(2):
        for i in range(2):
            local[0, i, color] = fields[0, color * coarse_frames + mine + i]
        for i in range(4):
            at = jnp.clip(mine + i - 1, 0, coarse_frames - 1)
            local[0, 2 + i, color] = fields[1, color * coarse_frames + at]
    mix_acc[...] += tn(pooled[...], qkv_grad[...])
    att_acc[...] += tn(att[...], upper[...])
    gram_acc[...] += tn(pooled[...], upper[...])
    spread16 = spread.astype(BF)
    for tap in range(3):
        tap_acc[tap * chans : (tap + 1) * chans, :] += tn(shifted[tap], spread16)

    @pl.when(step == heads_axis - 1)
    def _():
        for i in range(3 * heads):
            grad_mix[:, i * HD : (i + 1) * HD] = mix_acc[:, i * SLOT : i * SLOT + HD].astype(BF)
        for n in range(heads):
            grad_att[n * HD : (n + 1) * HD, :] = att_acc[n * SLOT : n * SLOT + HD, :].astype(BF)
        gram[...] = gram_acc[...].astype(BF)
        rows = tap_keep.shape[0]
        tap_keep[...] = tap_acc[pl.ds(pl.multiple_of(frame * rows, rows), rows), :].astype(BF)
        tap_send[...] = tap_acc[pl.ds(pl.multiple_of((frame ^ 1) * rows, rows), rows), :].astype(BF)


def slice_kernel(
    me, mix_a, mix_b, att_a, att_b, gram_a, gram_b, tap_a, tap_b, tap_c, w_qkv, w_up, w_out, down,
    grad_mix, grad_att, down_t, up, taps, *, heads_axis,
):
    del me
    chans = gram_a.shape[1]
    part = 1.0 / heads_axis
    g = (mix_a[...].astype(F32) + mix_b[...].astype(F32)).astype(BF)
    a = (att_a[...].astype(F32) + att_b[...].astype(F32)).astype(BF)
    s = (gram_a[...].astype(F32) + gram_b[...].astype(F32)).astype(BF)
    grad_mix[...] = g
    grad_att[...] = a
    down_t[...] = nt(w_qkv[...], g) + nt(w_up[...], s) * part
    up[:, 0:chans] = tn(w_out[...], a) + tn(down[...], s) * part
    up[:, chans:] = jnp.zeros((up.shape[0], up.shape[1] - chans), F32)
    taps[:, 0:chans] = tap_a[...].astype(F32) + tap_b[...].astype(F32) + tap_c[...].astype(F32)
    taps[:, chans:] = jnp.zeros((taps.shape[0], taps.shape[1] - chans), F32)


def split_grad_kernel(down, grad_mix, grad_att, w_up, qkv_out, att_out):
    qkv_out[...] = tn(down[...], grad_mix[...])
    att_out[...] = nt(grad_att[...], w_up[...])


def finish_kernel(me, hidden, base, own, other, w_time, output, grad_clip, rows, *, coarse_frames):
    frame = me[0]
    core = frame & 1
    half = own.shape[1]
    columns = hidden.shape[1] // 2
    for i in range(4):
        rows[i, pl.ds(pl.multiple_of(core * half, half), half), :] = own[i].astype(F32)
        rows[i, pl.ds(pl.multiple_of((1 - core) * half, half), half), :] = other[i].astype(F32)
    lift = lift_matrix(2 * half, columns)
    fine = nn(lift, rows[0].astype(BF))
    for t in range(2):
        output[t] = (hidden[t].astype(F32) + fine).astype(BF)
    before = (rows[1] * jnp.where(frame == 0, 0.0, 1.0)).astype(BF)
    here = rows[2].astype(BF)
    after = (rows[3] * jnp.where(frame == coarse_frames - 1, 0.0, 1.0)).astype(BF)
    mid = rows[2] + nt(here, w_time[1])
    even = mid + nt(here, w_time[0]) + nt(before, w_time[2])
    odd = mid + nt(after, w_time[0]) + nt(here, w_time[2])
    for t, value in ((0, even), (1, odd)):
        high = value.astype(BF)
        low = (value - high.astype(F32)).astype(BF)
        grad_clip[t] = base[t] + (nn(lift, high) + nn(lift, low)) * 0.125


def gather_kernel(me, embed, *refs, layout, aligned):
    pieces = refs[:4]
    refs = refs[4:]
    time_out, up_out = refs[0], refs[1]
    frame, head = me[0], me[1]
    chips, heads_axis, r1, p1, r3, split = layout
    chans = up_out.shape[2]
    down_rows = refs[-1] if aligned else refs[2]
    devices = 2 * chips * heads_axis
    for core in range(2):
        for idx in range(chips * heads_axis):
            hi, zi = idx // chips, idx % chips
            colors = []
            for color in range(2):
                src = pieces[2 * core + color]
                off = hi if color == 0 else reversed_bits(hi, heads_axis)
                colors.append(src[off, zi].astype(F32))
            value = jnp.concatenate(colors, axis=0)
            owner = (frame ^ (reversed_bits(zi, chips) * 2 + core)) * heads_axis + (head ^ hi)
            down_rows[owner] = value[0:r1]
            up_out[owner] = value[p1 : p1 + r1, 0:chans]

            @pl.when(owner < time_out.shape[0])
            def _():
                time_out[owner] = value[2 * p1 : 2 * p1 + r3, 0:chans]

    if aligned:
        down_out, embed_out = refs[2], refs[3]
        table = down_rows[...].reshape(devices * r1, down_rows.shape[2]).astype(BF)
        lanes = table.shape[1]
        eye = (lax.broadcasted_iota(jnp.int32, (lanes, lanes), 0) == lax.broadcasted_iota(jnp.int32, (lanes, lanes), 1))
        flipped = nt(eye.astype(F32).astype(BF), table)
        down_out[...] = flipped[0:chans]
        embed_out[...] = embed[...] * flipped[chans : chans + 1]


def double(x, axis, bits, dim):
    for bit in bits:
        x = jnp.concatenate([x, swap(x, axis, bit)], axis=dim)
    return x


def shards(clip, w_time, w_down, w_embed, w_qkv, w_out, w_up, timestep, cotangent):
    nf = lax.axis_size("frames")
    nh = lax.axis_size("heads")
    f = lax.axis_index("frames")
    h = lax.axis_index("heads")
    me = jnp.stack([f, h]).astype(jnp.int32)
    frames, rows, columns, chans = clip.shape
    width = w_down.shape[1]
    half_c = columns // 2
    half = half_c // 2
    quart = half // 2
    chips = nf // 2
    padded = round_up(chans + 2, 128)
    pieces = w_qkv.shape[1] // HD
    heads = pieces // 3
    chip_bits = [2 * b for b in reversed(bit_list(chips))]
    head_bits = bit_list(nh)

    clip2 = clip.reshape(frames, rows * columns, chans)
    cot2 = cotangent.reshape(frames, rows * columns, chans)

    keep, send = call(
        pool_kernel,
        [sds((2, 3, quart, chans), BF)] * 2,
        in_specs=[smem(), vmem(), vmem()],
        out_specs=[vmem()] * 2,
        scratch_shapes=[pltpu.VMEM((3, half_c, chans), F32)],
    )(me, clip2, cot2)
    block = jnp.concatenate([keep, swap(send, "frames", 1)], axis=1)
    block = double(block, "frames", chip_bits, 1)
    first = block[0]
    second = block[1]
    first = first[None]
    second = second[None]
    for a, b in zip(head_bits, reversed(head_bits)):
        first_in = swap(first, "heads", a)
        second_in = swap(second, "heads", b)
        first = jnp.concatenate([first, first_in], axis=0)
        second = jnp.concatenate([second, second_in], axis=0)

    embed = time_embed(timestep, w_embed.shape[0])
    down, mix, out_mix, direct = call(
        weight_kernel,
        [
            sds((padded, width), BF),
            sds((padded, pieces * SLOT), BF),
            sds((heads * SLOT, chans), BF),
            sds((padded, chans), BF),
        ],
    )(w_down, w_embed, embed[None, :], w_qkv, w_out, w_up)

    tail = jnp.stack([clip2[-1], cot2[-1]])
    head = jnp.stack([clip2[0], cot2[0]])
    lo = lax.ppermute(tail, "frames", [(i, i + 1) for i in range(nf - 1)])
    hi = lax.ppermute(head, "frames", [(i + 1, i) for i in range(nf - 1)])
    tap_rows = round_up(3 * chans, nf * nh * 8)
    hidden, base, taps = call(
        fine_kernel,
        [
            sds(clip2.shape, BF),
            sds(clip2.shape, F32),
            sds((tap_rows, chans), BF),
        ],
    )(clip2, lo[0], hi[0], cot2, lo[1], hi[1], w_time)
    share = tap_rows // nf
    bits = bit_list(nf)
    taps = taps.reshape([2] * len(bits) + [share, chans])
    for i in range(len(bits)):
        axis = len(bits) - 1 - i
        mine = (f >> i) & 1
        other = lax.dynamic_index_in_dim(taps, 1 - mine, axis, keepdims=False)
        same = lax.dynamic_index_in_dim(taps, mine, axis, keepdims=False)
        got = swap(other, "frames", 1 << i)
        taps = (same.astype(F32) + got.astype(F32)).astype(BF)

    blk = pl.BlockSpec((1, nf * 3, quart, chans), lambda g: (g, 0, 0, 0))
    mirrored = pl.BlockSpec((1, nf * 3, quart, chans), lambda g: (reversed_bits(g, nh), 0, 0, 0))
    total = 2 * nf * quart

    def whole(*shape):
        return pl.BlockSpec(shape, lambda g: (0,) * len(shape))

    local, mix_g, att_g, gram, tap_keep, tap_send = call(
        functools.partial(coarse_kernel, coarse_frames=nf, heads_axis=nh),
        [
            sds((nh, 6, 2, quart, chans), BF),
            sds((padded, pieces * HD), BF),
            sds((heads * HD, chans), BF),
            sds((padded, chans), BF),
            sds((share, chans), BF),
            sds((share, chans), BF),
        ],
        grid=(nh,),
        in_specs=[
            smem(),
            blk,
            mirrored,
            whole(*w_time.shape),
            whole(*mix.shape),
            whole(*out_mix.shape),
            whole(*direct.shape),
        ],
        out_specs=[
            pl.BlockSpec((1, 6, 2, quart, chans), lambda g: (g, 0, 0, 0, 0)),
            whole(padded, pieces * HD),
            whole(heads * HD, chans),
            whole(padded, chans),
            whole(share, chans),
            whole(share, chans),
        ],
        scratch_shapes=[
            pltpu.VMEM((3, total, chans), BF),
            pltpu.VMEM((total, chans), F32),
            pltpu.VMEM((total, padded), BF),
            pltpu.VMEM((total, chans), BF),
            pltpu.VMEM((total, pieces * SLOT), BF),
            pltpu.VMEM((total, heads * SLOT), BF),
            pltpu.VMEM((total, heads * SLOT), BF),
            pltpu.VMEM((total, pieces * SLOT), BF),
            pltpu.VMEM((2, 2 * nf, quart, chans), BF),
            pltpu.VMEM((padded, pieces * SLOT), F32),
            pltpu.VMEM((heads * SLOT, chans), F32),
            pltpu.VMEM((padded, chans), F32),
            pltpu.VMEM((tap_rows, chans), F32),
        ],
    )(me, first, second, w_time, mix, out_mix, direct)

    mix_o = swap(mix_g, "frames", 1)
    att_o = swap(att_g, "frames", 1)
    gram_o = swap(gram, "frames", 1)
    tap_o = swap(tap_send, "frames", 1)

    rows_here = width // nf
    out_cols = lax.dynamic_slice_in_dim(w_out, f * rows_here, rows_here, axis=1)
    down_cols = lax.dynamic_slice_in_dim(down, f * rows_here, rows_here, axis=1)
    grid_spec = pltpu.PrefetchScalarGridSpec(
        num_scalar_prefetch=1,
        grid=(1,),
        in_specs=[pl.BlockSpec(x.shape, lambda g, m: (0, 0)) for x in (mix_g, mix_o, att_g, att_o, gram, gram_o, tap_keep, tap_o, taps)]
        + [
            pl.BlockSpec((rows_here, w_qkv.shape[1]), lambda g, m: (m[0], 0)),
            pl.BlockSpec((rows_here, chans), lambda g, m: (m[0], 0)),
            pl.BlockSpec(out_cols.shape, lambda g, m: (0, 0)),
            pl.BlockSpec(down_cols.shape, lambda g, m: (0, 0)),
        ],
        out_specs=[
            pl.BlockSpec(mix_g.shape, lambda g, m: (0, 0)),
            pl.BlockSpec(att_g.shape, lambda g, m: (0, 0)),
            pl.BlockSpec((rows_here, padded), lambda g, m: (0, 0)),
            pl.BlockSpec((rows_here, padded), lambda g, m: (0, 0)),
            pl.BlockSpec((share, padded), lambda g, m: (0, 0)),
        ],
    )
    mix_s, att_s, down_s, up_s, tap_s = call(
        functools.partial(slice_kernel, heads_axis=nh),
        [
            sds(mix_g.shape, BF),
            sds(att_g.shape, BF),
            sds((rows_here, padded), F32),
            sds((rows_here, padded), F32),
            sds((share, padded), F32),
        ],
        grid_spec=grid_spec,
    )(me, mix_g, mix_o, att_g, att_o, gram, gram_o, tap_keep, tap_o, taps, w_qkv, w_up, out_cols, down_cols)

    r1 = rows_here // nh
    p1 = round_up(r1, 8)
    r3 = share // nh
    piece_rows = round_up(2 * p1 + r3, 32)

    def fit(x, count):
        x = x.astype(BF).reshape(nh, count, padded)
        return jnp.pad(x, ((0, 0), (0, round_up(count, 8) - count), (0, 0)))

    parts = jnp.concatenate([fit(down_s, r1), fit(up_s, r1), fit(tap_s, r3)], axis=1)
    parts = jnp.pad(parts, ((0, 0), (0, piece_rows - parts.shape[1]), (0, 0)))
    mine = lax.dynamic_index_in_dim(parts, h, 0, keepdims=False).astype(F32)
    for d in range(1, nh):
        mine = mine + swap(lax.dynamic_index_in_dim(parts, h ^ d, 0, keepdims=False), "heads", d).astype(F32)
    piece = mine.astype(BF).reshape(2, 1, piece_rows // 2, padded)
    piece = double(piece, "frames", chip_bits, 1)
    p_first = piece[0][None]
    p_second = piece[1][None]
    for a, b in zip(head_bits, reversed(head_bits)):
        a_in = swap(p_first, "heads", a)
        b_in = swap(p_second, "heads", b)
        p_first = jnp.concatenate([p_first, a_in], axis=0)
        p_second = jnp.concatenate([p_second, b_in], axis=0)
    q_first = swap(p_first, "frames", 1)
    q_second = swap(p_second, "frames", 1)

    own = local[0].astype(F32)
    for d in range(1, nh):
        own = own + swap(local[d], "heads", d).astype(F32)
    own = own.astype(BF).reshape(6, half, chans)
    core = f & 1

    def four(which):
        return jnp.concatenate(
            [
                lax.dynamic_slice_in_dim(own, which, 1, axis=0),
                lax.dynamic_slice_in_dim(own, 2 + which, 3, axis=0),
            ]
        )

    mine4 = four(core)
    other4 = swap(four(1 - core), "frames", 1)
    output, grad_clip = call(
        functools.partial(finish_kernel, coarse_frames=nf),
        [sds(clip2.shape, BF), sds(clip2.shape, F32)],
        in_specs=[smem()] + [vmem()] * 5,
        out_specs=[vmem()] * 2,
        scratch_shapes=[pltpu.VMEM((4, half_c, chans), F32)],
    )(me, hidden, base, mine4, other4, w_time)

    step = 256
    grad_qkv, grad_out = call(
        split_grad_kernel,
        [sds((width, pieces * HD), F32), sds((heads * HD, width), F32)],
        grid=(width // step,),
        in_specs=[
            pl.BlockSpec((padded, step), lambda g: (0, g)),
            whole(*mix_s.shape),
            whole(*att_s.shape),
            pl.BlockSpec((step, chans), lambda g: (g, 0)),
        ],
        out_specs=[
            pl.BlockSpec((step, pieces * HD), lambda g: (g, 0)),
            pl.BlockSpec((heads * HD, step), lambda g: (0, g)),
        ],
    )(down, mix_s, att_s, w_up)

    devices = nf * nh
    aligned = r1 % 8 == 0
    layout = (chips, nh, r1, p1, r3, piece_rows // 2)
    time_rows = 3 * chans // r3
    outs = [sds((time_rows, r3, chans), F32), sds((devices, r1, chans), F32)]
    scratch = []
    if aligned:
        outs += [sds((chans, width), F32), sds((w_embed.shape[0], width), F32)]
        scratch = [pltpu.VMEM((devices, r1, padded), F32)]
    else:
        outs += [sds((devices, r1, padded), F32)]
    embed_col = embed.astype(F32)[:, None]
    got = call(
        functools.partial(gather_kernel, layout=layout, aligned=aligned),
        outs,
        in_specs=[smem()] + [vmem()] * 5,
        out_specs=[vmem()] * len(outs),
        scratch_shapes=scratch,
    )(me, embed_col, p_first, p_second, q_first, q_second)
    grad_time = got[0].reshape(w_time.shape)
    grad_up = got[1].reshape(width, chans)
    if aligned:
        grad_down, grad_embed = got[2], got[3]
    else:
        table = got[2].reshape(width, padded)
        grad_down = table[:, :chans].T
        grad_embed = embed_col * table[:, chans][None, :]
    return (
        output.reshape(clip.shape),
        grad_clip.reshape(clip.shape),
        grad_time,
        grad_down,
        grad_embed,
        grad_qkv,
        grad_out,
        grad_up,
    )


def solution(mesh):
    return jax.shard_map(
        shards,
        mesh=mesh,
        in_specs=(
            P("frames", "heads", None, None),
            P(),
            P(),
            P(),
            P(None, "heads"),
            P("heads", None),
            P(),
            P(),
            P("frames", "heads", None, None),
        ),
        out_specs=(
            P("frames", "heads", None, None),
            P("frames", "heads", None, None),
            P(),
            P(),
            P(),
            P(None, "heads"),
            P("heads", None),
            P(),
        ),
        check_vma=False,
    )
```

```python
import functools
import math

import jax
import jax.numpy as jnp
from jax import lax
from jax.experimental import pallas as pl
from jax.experimental.pallas import tpu as pltpu
from jax.sharding import PartitionSpec as P

HD = 80
SLOT = 128
BF = jnp.bfloat16
F32 = jnp.float32


def nn(a, b):
    return lax.dot_general(a, b, (((1,), (0,)), ((), ())), preferred_element_type=F32)


def nt(a, b):
    return lax.dot_general(a, b, (((1,), (1,)), ((), ())), preferred_element_type=F32)


def tn(a, b):
    return lax.dot_general(a, b, (((0,), (0,)), ((), ())), preferred_element_type=F32)


def round_up(value, step):
    return -(-value // step) * step


def call(kernel, out_shape, **kw):
    return pl.pallas_call(
        kernel,
        out_shape=out_shape,
        compiler_params=pltpu.CompilerParams(vmem_limit_bytes=56 * 1024 * 1024),
        **kw,
    )


def smem():
    return pl.BlockSpec(memory_space=pltpu.SMEM)


def vmem():
    return pl.BlockSpec(memory_space=pltpu.VMEM)


def sds(shape, dtype):
    return jax.ShapeDtypeStruct(shape, dtype)


def bit_list(count):
    bits = []
    while (1 << len(bits)) < count:
        bits.append(1 << len(bits))
    return bits


def reversed_bits(value, count):
    n = len(bit_list(count))
    out = 0
    for i in range(n):
        out = out + (((value >> i) & 1) << (n - 1 - i))
    return out


def swap(x, axis, bit):
    n = lax.axis_size(axis)
    return lax.ppermute(x, axis, [(i, i ^ bit) for i in range(n)])


def time_embed(timestep, width):
    half = width // 2
    freqs = jnp.exp(-math.log(10000.0) * jnp.arange(half, dtype=F32) / half)
    angle = timestep.astype(F32)[0] * freqs
    return jax.nn.silu(jnp.concatenate([jnp.cos(angle), jnp.sin(angle)])).astype(BF)


def pool_matrix(half_c, columns):
    row = lax.broadcasted_iota(jnp.int32, (half_c, columns), 0)
    col = lax.broadcasted_iota(jnp.int32, (half_c, columns), 1)
    return jnp.where((col >> 1) == row, 1.0, 0.0).astype(BF)


def pool_kernel(me, clip, cot, keep, send, tmp):
    half_c = tmp.shape[1]
    half = half_c // 2
    quart = half // 2
    pool = pool_matrix(half_c, clip.shape[3])
    for t in range(2):
        tmp[t] = (nt(pool, clip[t, 0]) + nt(pool, clip[t, 1])) * 0.25
    tmp[2] = (nt(pool, cot[0, 0]) + nt(pool, cot[0, 1])) + (nt(pool, cot[1, 0]) + nt(pool, cot[1, 1]))
    core = me[0] & 1
    for color in range(2):
        for item in range(3):
            base = pl.multiple_of(core * half + color * quart, quart)
            keep[color, item] = tmp[item, pl.ds(base, quart), :].astype(BF)
            base = pl.multiple_of((1 - core) * half + color * quart, quart)
            send[color, item] = tmp[item, pl.ds(base, quart), :].astype(BF)


def edge_kernel(clip, cot, after, head, tail):
    del after
    for r in range(2):
        head[r] = clip[0, r]
        head[2 + r] = cot[0, r]
        tail[r] = clip[1, r]
        tail[2 + r] = cot[1, r]


def weight_kernel(w_down, w_embed, embed, w_qkv, w_out, w_up, down, mix, out_mix, direct):
    chans = w_down.shape[0]
    padded = down.shape[0]
    shift = nn(embed[...], w_embed[...])
    high = shift.astype(BF)
    low = (shift - high.astype(F32)).astype(BF)
    down[0:chans, :] = w_down[...]
    row = lax.broadcasted_iota(jnp.int32, (padded - chans, shift.shape[1]), 0)
    tail = jnp.where(row == 0, high.astype(F32), jnp.where(row == 1, low.astype(F32), 0.0))
    down[chans:padded, :] = tail.astype(BF)
    full = down[...]
    pieces = w_qkv.shape[0] // HD
    prod = nt(full, w_qkv[...])
    mix[...] = jnp.zeros(mix.shape, BF)
    for i in range(pieces):
        mix[:, i * SLOT : i * SLOT + HD] = prod[:, i * HD : (i + 1) * HD].astype(BF)
    up = w_up[...]
    small = nt(w_out[...], up)
    out_mix[...] = jnp.zeros(out_mix.shape, BF)
    for i in range(pieces // 3):
        out_mix[i * SLOT : i * SLOT + HD, :] = small[i * HD : (i + 1) * HD, :].astype(BF)
    direct[...] = nt(full, up).astype(BF)


def fine_kernel(clip, cot, lo, hi, w_time, hidden, base, taps, wide, grad):
    chans = w_time.shape[1]
    columns = clip.shape[3]
    for t in range(4):
        for r in range(2):
            at = slice((2 * t + r) * columns, (2 * t + r + 1) * columns)
            if t in (0, 3):
                halo = lo if t == 0 else hi
                wide[:, at] = halo[r]
                grad[:, at] = halo[2 + r]
            else:
                wide[:, at] = clip[t - 1, r]
                grad[:, at] = cot[t - 1, r]
    cells = 2 * columns
    taps[3 * chans :, :] = jnp.zeros((taps.shape[0] - 3 * chans, chans), BF)
    here = grad[:, cells : 3 * cells]
    for tap in range(3):
        taps[tap * chans : (tap + 1) * chans, :] = nt(wide[:, tap * cells : (tap + 2) * cells], here).astype(BF)
    acc = wide[:, cells : 3 * cells].astype(F32)
    back = here.astype(F32)
    for tap in range(3):
        acc = acc + tn(w_time[tap], wide[:, tap * cells : (tap + 2) * cells])
        back = back + nn(w_time[tap], grad[:, (2 - tap) * cells : (4 - tap) * cells])
    for t in range(2):
        for r in range(2):
            at = slice((2 * t + r) * columns, (2 * t + r + 1) * columns)
            hidden[t, r] = acc[:, at].astype(BF)
            base[t, r] = back[:, at]


def coarse_kernel(
    me, first, second, w_time, mix, out_mix, direct, q_rows, u_rows, o_rows, d_rows, taps,
    local, grad_mix, grad_att, keep, send,
    shifted, centre, pooled, upper, qkv, att_grad, att, qkv_grad, fields, spread_all, rows_down, rows_up, rows_tap,
    *, coarse_frames, heads_axis, rest,
):
    step = pl.program_id(0)
    frame = me[0]
    quart = first.shape[2]
    chans = first.shape[3]
    padded = pooled.shape[1]
    tokens = coarse_frames * quart
    total = 2 * tokens
    chips = coarse_frames // 2
    heads = att.shape[1] // SLOT
    scale = 1.0 / math.sqrt(HD)
    part = 1.0 / heads_axis
    here_rows = pl.ds(pl.multiple_of(step * total, total), total)

    @pl.when(step == 0)
    def _():
        lane = lax.broadcasted_iota(jnp.int32, (pooled.shape[0], padded - chans), 1)
        pooled[:, chans:padded] = jnp.where(lane < 2, 1.0, 0.0).astype(BF)
        shifted[:, 3 * chans :] = jnp.zeros((shifted.shape[0], shifted.shape[1] - 3 * chans), BF)

    def entry(index):
        gap = index ^ frame
        return (reversed_bits(gap >> 1, chips) * 2 + (gap & 1)) * 3

    for color, source in ((0, first), (1, second)):
        before = jnp.zeros((quart, chans), F32)
        here = source[0, entry(0)].astype(F32)
        for u in range(coarse_frames):
            at = entry(u)
            last = source[0, at + 1].astype(F32)
            after = source[0, entry(u + 1)].astype(F32) if u + 1 < coarse_frames else jnp.zeros((quart, chans), F32)
            offset = color * tokens + u * quart
            rows = pl.ds(pl.multiple_of(step * total + offset, quart), quart)
            mid = 0.5 * (here + last)
            shifted[rows, 0:chans] = (0.5 * (before + here)).astype(BF)
            shifted[rows, chans : 2 * chans] = mid.astype(BF)
            shifted[rows, 2 * chans : 3 * chans] = (0.5 * (last + after)).astype(BF)
            centre[offset : offset + quart, :] = mid
            upper[rows, :] = source[0, at + 2]
            before, here = last, after
    pool = (centre[...] + nn(shifted[here_rows, 0 : 3 * chans], w_time[...])).astype(BF)
    pooled[here_rows, 0:chans] = pool
    lines = pooled[here_rows, :]
    ups = upper[here_rows, :]
    qkv[...] = nn(lines, mix[...]).astype(BF)
    att_grad[...] = nt(ups, out_mix[...]).astype(BF)
    row = lax.broadcasted_iota(jnp.int32, (tokens, tokens), 0)
    col = lax.broadcasted_iota(jnp.int32, (tokens, tokens), 1)
    same = (row & (quart - 1)) == (col & (quart - 1))
    for color in range(2):
        rows = slice(color * tokens, (color + 1) * tokens)
        out = pl.ds(pl.multiple_of(step * total + color * tokens, tokens), tokens)
        for n in range(heads):
            q = qkv[rows, (3 * n) * SLOT : (3 * n + 1) * SLOT]
            k = qkv[rows, (3 * n + 1) * SLOT : (3 * n + 2) * SLOT]
            v = qkv[rows, (3 * n + 2) * SLOT : (3 * n + 3) * SLOT]
            da = att_grad[rows, n * SLOT : (n + 1) * SLOT]
            scores = jnp.where(same, nt(q, k) * scale, -jnp.inf)
            peak = jnp.max(scores, axis=1, keepdims=True)
            ex = jnp.exp(scores - peak)
            probs = ex * (1.0 / jnp.sum(ex, axis=1, keepdims=True))
            weights = probs.astype(BF)
            att[out, n * SLOT : (n + 1) * SLOT] = nn(weights, v).astype(BF)
            dw = nt(da, v)
            inner = jnp.sum(probs * dw, axis=1, keepdims=True)
            ds = (probs * (dw - inner) * scale).astype(BF)
            qkv_grad[out, (3 * n) * SLOT : (3 * n + 1) * SLOT] = nn(ds, k).astype(BF)
            qkv_grad[out, (3 * n + 1) * SLOT : (3 * n + 2) * SLOT] = tn(ds, q).astype(BF)
            qkv_grad[out, (3 * n + 2) * SLOT : (3 * n + 3) * SLOT] = tn(weights, da).astype(BF)
    lifted = nn(att[here_rows, :], out_mix[...]) + nn(lines, direct[...]) * part
    spread = nt(qkv_grad[here_rows, :], mix[...]) + nt(ups, direct[...]) * part
    spread = spread[:, 0:chans].astype(BF)
    spread_all[here_rows, :] = spread
    fields[0] = lifted.astype(BF).reshape(2 * coarse_frames, quart, chans)
    fields[1] = spread.reshape(2 * coarse_frames, quart, chans)
    mine = (frame >> 1) * 2
    for color in range(2):
        for i in range(2):
            local[0, i, color] = fields[0, color * coarse_frames + mine + i]
        for i in range(4):
            at = jnp.clip(mine + i - 1, 0, coarse_frames - 1)
            local[0, 2 + i, color] = fields[1, color * coarse_frames + at]

    @pl.when(step == heads_axis - 1)
    def _():
        g = tn(pooled[...], qkv_grad[...])
        for i in range(3 * heads):
            grad_mix[:, i * HD : (i + 1) * HD] = g[:, i * SLOT : i * SLOT + HD].astype(BF)
        a = tn(att[...], upper[...])
        for n in range(heads):
            grad_att[n * HD : (n + 1) * HD, :] = a[n * SLOT : n * SLOT + HD, :].astype(BF)
        s = tn(pooled[...], upper[...]).astype(BF)
        pair = rows_tap.shape[0]
        own = shifted[:, pl.ds(pl.multiple_of((frame >> 1) * pair, pair), pair)]
        rows_tap[:, 0:chans] = tn(own, spread_all[...])
        rows_tap[:, chans:] = jnp.zeros((pair, padded - chans), F32)
        rows_down[...] = nt(q_rows[...], grad_mix[...]) + nt(u_rows[...], s) * part
        rows_up[:, 0:chans] = nn(o_rows[...], grad_att[...]) + nn(d_rows[...], s) * part
        rows_up[:, chans:] = jnp.zeros((rows_up.shape[0], padded - chans), F32)
        core = frame & 1
        p1, r3, piece = rest
        extra = jnp.zeros((piece - 2 * p1 - r3, padded), F32)
        for dest, which in ((keep, core), (send, 1 - core)):
            for j in range(heads_axis):
                at = pl.ds(pl.multiple_of((which * heads_axis + j) * p1, p1), p1)
                tap = rows_tap[pl.ds(pl.multiple_of((which * heads_axis + j) * r3, r3), r3), :]
                if dest is keep:
                    more = jnp.concatenate([taps[j * r3 : (j + 1) * r3, :].astype(F32), jnp.zeros((r3, padded - chans), F32)], axis=1)
                    tap = tap + more
                parts = [rows_down[at, :], rows_up[at, :], tap]
                if piece > 2 * p1 + r3:
                    parts.append(extra)
                dest[j] = jnp.concatenate(parts, axis=0).astype(BF)


def order_kernel(me, keep, got, *outs):
    head = me[1]
    for d, out in enumerate(outs):
        at = head ^ d
        out[...] = (keep[at].astype(F32) + got[at].astype(F32)).astype(BF)


def sum_kernel(*refs):
    acc = refs[0][...].astype(F32)
    for ref in refs[1:-1]:
        acc = acc + ref[...].astype(F32)
    refs[-1][...] = acc.astype(BF)


def split_grad_kernel(down, mix_a, mix_b, att_a, att_b, w_up, qkv_out, att_out, flipped):
    @pl.when(pl.program_id(0) == 0)
    def _():
        flipped[...] = (mix_a[...].astype(F32) + mix_b[...].astype(F32)).T.astype(BF)

    qkv_out[...] = nn(flipped[...], down[...])
    att_out[...] = nn((att_a[...].astype(F32) + att_b[...].astype(F32)).astype(BF), w_up[...])


def finish_kernel(me, hidden, base, own, other, w_time, output, grad_clip, rows, *, coarse_frames):
    frame = me[0]
    core = frame & 1
    half = own.shape[1]
    columns = hidden.shape[3]
    for i in range(4):
        rows[i, pl.ds(pl.multiple_of(core * half, half), half), :] = own[i].astype(F32)
        rows[i, pl.ds(pl.multiple_of((1 - core) * half, half), half), :] = other[i].astype(F32)
    lift = pool_matrix(2 * half, columns)
    fine = tn(rows[0].astype(BF), lift)
    for t in range(2):
        for r in range(2):
            output[t, r] = (hidden[t, r].astype(F32) + fine).astype(BF)
    before = (rows[1] * jnp.where(frame == 0, 0.0, 1.0)).astype(BF)
    here = rows[2].astype(BF)
    after = (rows[3] * jnp.where(frame == coarse_frames - 1, 0.0, 1.0)).astype(BF)
    mid = rows[2] + nt(here, w_time[1])
    even = mid + nt(here, w_time[0]) + nt(before, w_time[2])
    odd = mid + nt(after, w_time[0]) + nt(here, w_time[2])
    for t, value in ((0, even), (1, odd)):
        high = value.astype(BF)
        low = (value - high.astype(F32)).astype(BF)
        add = (tn(high, lift) + tn(low, lift)) * 0.125
        for r in range(2):
            grad_clip[t, r] = base[t, r] + add


def gather_kernel(me, embed, *refs, layout, aligned):
    pieces = refs[:4]
    time_out, down_rows, up_rows = refs[4], refs[-2], refs[-1]
    frame, head = me[0], me[1]
    chips, heads_axis, r1, p1, r3 = layout
    chans = time_out.shape[2]
    devices = 2 * chips * heads_axis
    for core in range(2):
        for idx in range(chips * heads_axis):
            hi, zi = idx // chips, idx % chips
            colors = []
            for color in range(2):
                src = pieces[2 * core + color]
                off = hi if color == 0 else reversed_bits(hi, heads_axis)
                colors.append(src[off, zi].astype(F32))
            value = jnp.concatenate(colors, axis=0)
            owner = (frame ^ (reversed_bits(zi, chips) * 2 + core)) * heads_axis + (head ^ hi)
            down_rows[owner] = value[0:r1]
            up_rows[owner] = value[p1 : p1 + r1]

            @pl.when(owner < time_out.shape[0])
            def _():
                time_out[owner] = value[2 * p1 : 2 * p1 + r3, 0:chans]

    if aligned:
        down_out, embed_out, up_out = refs[5], refs[6], refs[7]
        lanes = down_rows.shape[2]
        eye = (lax.broadcasted_iota(jnp.int32, (lanes, lanes), 0) == lax.broadcasted_iota(jnp.int32, (lanes, lanes), 1))
        eye = eye.astype(F32).astype(BF)
        flipped = nt(eye, down_rows[...].reshape(devices * r1, lanes).astype(BF))
        down_out[...] = flipped[0:chans]
        embed_out[...] = embed[...] * flipped[chans : chans + 1]
        up_out[...] = nt(eye, up_rows[...].reshape(devices * r1, lanes).astype(BF))[0:chans]


def double(x, axis, bits, dim):
    for bit in bits:
        got = swap(x, axis, bit)
        x = jnp.concatenate([x, got], axis=dim)
    return x


def cross(first, second, bits):
    for a, b in zip(bits, reversed(bits)):
        first_in = swap(first, "heads", a)
        second_in = swap(second, "heads", b)
        first = jnp.concatenate([first, first_in], axis=0)
        second = jnp.concatenate([second, second_in], axis=0)
    return first, second


def body(clip, w_time, w_down, w_embed, w_qkv, w_out, w_up, timestep, cotangent):
    nf = lax.axis_size("frames")
    nh = lax.axis_size("heads")
    f = lax.axis_index("frames")
    h = lax.axis_index("heads")
    me = jnp.stack([f, h]).astype(jnp.int32)
    _, _, columns, chans = clip.shape
    width = w_down.shape[1]
    half_c = columns // 2
    half = half_c // 2
    quart = half // 2
    chips = nf // 2
    padded = round_up(chans + 2, 128)
    pieces = w_qkv.shape[1] // HD
    heads = pieces // 3
    chip_bits = [2 * b for b in reversed(bit_list(chips))]
    head_bits = bit_list(nh)
    devices = nf * nh

    clip_t = clip.transpose(0, 1, 3, 2)
    cot_t = cotangent.transpose(0, 1, 3, 2)
    w_qkv_t = w_qkv.T
    w_up_t = w_up.T

    keep, send = call(
        pool_kernel,
        [sds((2, 3, quart, chans), BF)] * 2,
        in_specs=[smem(), vmem(), vmem()],
        out_specs=[vmem()] * 2,
        scratch_shapes=[pltpu.VMEM((3, half_c, chans), F32)],
    )(me, clip_t, cot_t)
    keep_in = swap(send, "frames", 1)
    block = jnp.concatenate([keep, keep_in], axis=1)
    block = double(block, "frames", chip_bits, 1)
    first, second = cross(block[0][None], block[1][None], head_bits)

    embed = time_embed(timestep, w_embed.shape[0])
    down, mix, out_mix, direct = call(
        weight_kernel,
        [
            sds((padded, width), BF),
            sds((padded, pieces * SLOT), BF),
            sds((heads * SLOT, chans), BF),
            sds((padded, chans), BF),
        ],
    )(w_down, w_embed, embed[None, :], w_qkv_t, w_out, w_up_t)

    head, tail = call(
        edge_kernel,
        [sds((4, chans, columns), BF)] * 2,
        in_specs=[vmem(), vmem(), pl.BlockSpec(memory_space=pl.ANY)],
        out_specs=[vmem()] * 2,
    )(clip_t, cot_t, keep)
    lo = lax.ppermute(tail, "frames", [(i, i + 1) for i in range(nf - 1)])
    hi = lax.ppermute(head, "frames", [(i + 1, i) for i in range(nf - 1)])
    tap_rows = round_up(3 * chans, devices * 8)
    hidden, base, taps = call(
        fine_kernel,
        [
            sds(clip_t.shape, BF),
            sds(clip_t.shape, F32),
            sds((tap_rows, chans), BF),
        ],
        scratch_shapes=[pltpu.VMEM((chans, 8 * columns), BF)] * 2,
    )(clip_t, cot_t, lo, hi, w_time)
    share = tap_rows // nf
    bits = bit_list(nf)
    taps = taps.reshape([2] * len(bits) + [share, chans])
    for i in range(len(bits)):
        axis = len(bits) - 1 - i
        mine = (f >> i) & 1
        other = lax.dynamic_index_in_dim(taps, 1 - mine, axis, keepdims=False)
        same = lax.dynamic_index_in_dim(taps, mine, axis, keepdims=False)
        got = swap(other, "frames", 1 << i)
        taps = (same.astype(F32) + got.astype(F32)).astype(BF)

    chip_rows = 2 * width // nf
    r1 = width // devices
    p1 = round_up(r1, 8)
    r3 = share // nh
    piece_rows = round_up(2 * p1 + r3, 16)
    start = (f >> 1) * chip_rows

    def rows_of(x, axis):
        x = lax.dynamic_slice_in_dim(x, start, chip_rows, axis=axis)
        x = x.T if axis == 1 else x
        x = x.reshape(2 * nh, r1, x.shape[1])
        return jnp.pad(x, ((0, 0), (0, p1 - r1), (0, 0))).reshape(2 * nh * p1, x.shape[2])

    q_rows = rows_of(w_qkv, 0)
    u_rows = rows_of(w_up, 0)
    o_rows = rows_of(w_out, 1)
    d_rows = rows_of(down, 1)

    blk = pl.BlockSpec((1, nf * 3, quart, chans), lambda g: (g, 0, 0, 0))
    mirrored = pl.BlockSpec((1, nf * 3, quart, chans), lambda g: (reversed_bits(g, nh), 0, 0, 0))
    total = 2 * nf * quart
    every = nh * total

    def whole(*shape):
        return pl.BlockSpec(shape, lambda g: (0,) * len(shape))

    w_time2 = w_time.reshape(3 * chans, chans)
    statics = (w_time2, mix, out_mix, direct, q_rows, u_rows, o_rows, d_rows, taps)
    local, mix_g, att_g, d_keep, d_send = call(
        functools.partial(coarse_kernel, coarse_frames=nf, heads_axis=nh, rest=(p1, r3, piece_rows)),
        [
            sds((nh, 6, 2, quart, chans), BF),
            sds((padded, pieces * HD), BF),
            sds((heads * HD, chans), BF),
            sds((nh, piece_rows, padded), BF),
            sds((nh, piece_rows, padded), BF),
        ],
        grid=(nh,),
        in_specs=[smem(), blk, mirrored] + [whole(*x.shape) for x in statics],
        out_specs=[
            pl.BlockSpec((1, 6, 2, quart, chans), lambda g: (g, 0, 0, 0, 0)),
            whole(padded, pieces * HD),
            whole(heads * HD, chans),
            whole(nh, piece_rows, padded),
            whole(nh, piece_rows, padded),
        ],
        scratch_shapes=[
            pltpu.VMEM((every, tap_rows), BF),
            pltpu.VMEM((total, chans), F32),
            pltpu.VMEM((every, padded), BF),
            pltpu.VMEM((every, chans), BF),
            pltpu.VMEM((total, pieces * SLOT), BF),
            pltpu.VMEM((total, heads * SLOT), BF),
            pltpu.VMEM((every, heads * SLOT), BF),
            pltpu.VMEM((every, pieces * SLOT), BF),
            pltpu.VMEM((2, 2 * nf, quart, chans), BF),
            pltpu.VMEM((every, chans), BF),
            pltpu.VMEM((2 * nh * p1, padded), F32),
            pltpu.VMEM((2 * nh * p1, padded), F32),
            pltpu.VMEM((2 * share, padded), F32),
        ],
    )(me, first, second, *statics)

    d_got = swap(d_send, "frames", 1)
    ordered = call(
        order_kernel,
        [sds((piece_rows, padded), BF)] * nh,
        in_specs=[smem(), vmem(), vmem()],
        out_specs=[vmem()] * nh,
    )(me, d_keep, d_got)
    got = []
    for d in range(1, nh):
        got.append(swap(ordered[d], "heads", d))
    piece = call(sum_kernel, sds((piece_rows, padded), BF))(ordered[0], *got)
    piece = piece.reshape(2, 1, piece_rows // 2, padded)
    piece = double(piece, "frames", chip_bits, 1)
    p_first, p_second = cross(piece[0][None], piece[1][None], head_bits)
    q_first = swap(p_first, "frames", 1)
    q_second = swap(p_second, "frames", 1)

    got = []
    for d in range(1, nh):
        got.append(swap(local[d], "heads", d))
    own = call(sum_kernel, sds(local.shape[1:], BF))(local[0], *got)
    own = own.reshape(6, half, chans)
    core = f & 1

    def four(which):
        return jnp.concatenate(
            [
                lax.dynamic_slice_in_dim(own, which, 1, axis=0),
                lax.dynamic_slice_in_dim(own, 2 + which, 3, axis=0),
            ]
        )

    mine4 = four(core)
    other4 = swap(four(1 - core), "frames", 1)
    output, grad_clip = call(
        functools.partial(finish_kernel, coarse_frames=nf),
        [sds(clip_t.shape, BF), sds(clip_t.shape, F32)],
        in_specs=[smem()] + [vmem()] * 5,
        out_specs=[vmem()] * 2,
        scratch_shapes=[pltpu.VMEM((4, half_c, chans), F32)],
    )(me, hidden, base, mine4, other4, w_time)

    mix_o = swap(mix_g, "frames", 1)
    att_o = swap(att_g, "frames", 1)
    step = 256
    grad_qkv, grad_out = call(
        split_grad_kernel,
        [sds((pieces * HD, width), F32), sds((heads * HD, width), F32)],
        grid=(width // step,),
        in_specs=[
            pl.BlockSpec((padded, step), lambda g: (0, g)),
            whole(*mix_g.shape),
            whole(*mix_g.shape),
            whole(*att_g.shape),
            whole(*att_g.shape),
            pl.BlockSpec((chans, step), lambda g: (0, g)),
        ],
        out_specs=[
            pl.BlockSpec((pieces * HD, step), lambda g: (0, g)),
            pl.BlockSpec((heads * HD, step), lambda g: (0, g)),
        ],
        scratch_shapes=[pltpu.VMEM((pieces * HD, padded), BF)],
    )(down, mix_g, mix_o, att_g, att_o, w_up_t)

    output, grad_clip, grad_qkv, grad_out, q_second = lax.optimization_barrier(
        (output, grad_clip, grad_qkv, grad_out, q_second)
    )
    aligned = r1 % 8 == 0
    layout = (chips, nh, r1, p1, r3)
    outs = [sds((3 * chans // r3, r3, chans), F32)]
    table = (devices, r1, padded)
    scratch = []
    if aligned:
        outs += [sds((chans, width), F32), sds((w_embed.shape[0], width), F32), sds((chans, width), F32)]
        scratch = [pltpu.VMEM(table, F32)] * 2
    else:
        outs += [sds(table, F32)] * 2
    embed_col = embed.astype(F32)[:, None]
    got = call(
        functools.partial(gather_kernel, layout=layout, aligned=aligned),
        outs,
        in_specs=[smem()] + [vmem()] * 5,
        out_specs=[vmem()] * len(outs),
        scratch_shapes=scratch,
    )(me, embed_col, p_first, p_second, q_first, q_second)
    grad_time = got[0].reshape(w_time.shape)
    if aligned:
        grad_down, grad_embed, grad_up = got[1], got[2], got[3].T
    else:
        down_rows = got[1].reshape(width, padded)
        grad_down = down_rows[:, :chans].T
        grad_embed = embed_col * down_rows[:, chans][None, :]
        grad_up = got[2].reshape(width, padded)[:, :chans]
    return (
        output.transpose(0, 1, 3, 2),
        grad_clip.transpose(0, 1, 3, 2),
        grad_time,
        grad_down,
        grad_embed,
        grad_qkv.T,
        grad_out,
        grad_up,
    )


def solution(mesh):
    return jax.shard_map(
        body,
        mesh=mesh,
        in_specs=(
            P("frames", "heads", None, None),
            P(),
            P(),
            P(),
            P(None, "heads"),
            P("heads", None),
            P(),
            P(),
            P("frames", "heads", None, None),
        ),
        out_specs=(
            P("frames", "heads", None, None),
            P("frames", "heads", None, None),
            P(),
            P(),
            P(),
            P(None, "heads"),
            P("heads", None),
            P(),
        ),
        check_vma=False,
    )
```

```python
import functools
import math

import jax
import jax.numpy as jnp
from jax import lax
from jax.experimental import pallas as pl
from jax.experimental.pallas import tpu as pltpu
from jax.sharding import PartitionSpec as P


HD = 80
SLOT = 128
BF = jnp.bfloat16
F32 = jnp.float32


def nn(a, b):
    return lax.dot_general(a, b, (((1,), (0,)), ((), ())), preferred_element_type=F32)


def nt(a, b):
    return lax.dot_general(a, b, (((1,), (1,)), ((), ())), preferred_element_type=F32)


def tn(a, b):
    return lax.dot_general(a, b, (((0,), (0,)), ((), ())), preferred_element_type=F32)


def round_up(value, step):
    return -(-value // step) * step


def call(kernel, out_shape, **kw):
    return pl.pallas_call(
        kernel,
        out_shape=out_shape,
        compiler_params=pltpu.CompilerParams(vmem_limit_bytes=56 * 1024 * 1024),
        **kw,
    )


def smem():
    return pl.BlockSpec(memory_space=pltpu.SMEM)


def vmem():
    return pl.BlockSpec(memory_space=pltpu.VMEM)


def sds(shape, dtype):
    return jax.ShapeDtypeStruct(shape, dtype)


def bit_list(count):
    bits = []
    while (1 << len(bits)) < count:
        bits.append(1 << len(bits))
    return bits


def reversed_bits(value, count):
    n = len(bit_list(count))
    out = 0
    for i in range(n):
        out = out + (((value >> i) & 1) << (n - 1 - i))
    return out


def swap(x, axis, bit):
    n = lax.axis_size(axis)
    return lax.ppermute(x, axis, [(i, i ^ bit) for i in range(n)])


def time_embed(timestep, width):
    half = width // 2
    freqs = jnp.exp(-math.log(10000.0) * jnp.arange(half, dtype=F32) / half)
    angle = timestep.astype(F32)[0] * freqs
    return jax.nn.silu(jnp.concatenate([jnp.cos(angle), jnp.sin(angle)])).astype(BF)


def pool_matrix(half_c, columns):
    row = lax.broadcasted_iota(jnp.int32, (half_c, columns), 0)
    col = lax.broadcasted_iota(jnp.int32, (half_c, columns), 1)
    return jnp.where((col >> 1) == row, 1.0, 0.0).astype(BF)


def pool_kernel(me, clip, cot, keep, send, tmp):
    half_c = tmp.shape[1]
    half = half_c // 2
    quart = half // 2
    pool = pool_matrix(half_c, clip.shape[3])
    for t in range(2):
        tmp[t] = (nt(pool, clip[t, 0]) + nt(pool, clip[t, 1])) * 0.25
    tmp[2] = (nt(pool, cot[0, 0]) + nt(pool, cot[0, 1])) + (nt(pool, cot[1, 0]) + nt(pool, cot[1, 1]))
    core = me[0] & 1
    for color in range(2):
        for item in range(3):
            base = pl.multiple_of(core * half + color * quart, quart)
            keep[color, item] = tmp[item, pl.ds(base, quart), :].astype(BF)
            base = pl.multiple_of((1 - core) * half + color * quart, quart)
            send[color, item] = tmp[item, pl.ds(base, quart), :].astype(BF)


def edge_kernel(clip, cot, after, head, tail):
    del after
    for r in range(2):
        head[r] = clip[0, r]
        head[2 + r] = cot[0, r]
        tail[r] = clip[1, r]
        tail[2 + r] = cot[1, r]


def weight_kernel(w_down, w_embed, embed, w_qkv, w_out, w_up, down, mix, out_mix, direct):
    chans = w_down.shape[0]
    padded = down.shape[0]
    shift = nn(embed[...], w_embed[...])
    high = shift.astype(BF)
    low = (shift - high.astype(F32)).astype(BF)
    down[0:chans, :] = w_down[...]
    row = lax.broadcasted_iota(jnp.int32, (padded - chans, shift.shape[1]), 0)
    tail = jnp.where(row == 0, high.astype(F32), jnp.where(row == 1, low.astype(F32), 0.0))
    down[chans:padded, :] = tail.astype(BF)
    full = down[...]
    pieces = w_qkv.shape[0] // HD
    prod = nt(full, w_qkv[...])
    mix[...] = jnp.zeros(mix.shape, BF)
    for i in range(pieces):
        mix[:, i * SLOT : i * SLOT + HD] = prod[:, i * HD : (i + 1) * HD].astype(BF)
    up = w_up[...]
    small = nt(w_out[...], up)
    out_mix[...] = jnp.zeros(out_mix.shape, BF)
    for i in range(pieces // 3):
        out_mix[i * SLOT : i * SLOT + HD, :] = small[i * HD : (i + 1) * HD, :].astype(BF)
    direct[...] = nt(full, up).astype(BF)


def fine_kernel(clip, cot, lo, hi, w_time, hidden, base, taps, wide, grad):
    chans = w_time.shape[1]
    columns = clip.shape[3]
    for t in range(4):
        for r in range(2):
            at = slice((2 * t + r) * columns, (2 * t + r + 1) * columns)
            if t in (0, 3):
                halo = lo if t == 0 else hi
                wide[:, at] = halo[r]
                grad[:, at] = halo[2 + r]
            else:
                wide[:, at] = clip[t - 1, r]
                grad[:, at] = cot[t - 1, r]
    cells = 2 * columns
    taps[3 * chans :, :] = jnp.zeros((taps.shape[0] - 3 * chans, chans), BF)
    here = grad[:, cells : 3 * cells]
    for tap in range(3):
        taps[tap * chans : (tap + 1) * chans, :] = nt(wide[:, tap * cells : (tap + 2) * cells], here).astype(BF)
    acc = wide[:, cells : 3 * cells].astype(F32)
    back = here.astype(F32)
    for tap in range(3):
        acc = acc + tn(w_time[tap], wide[:, tap * cells : (tap + 2) * cells])
        back = back + nn(w_time[tap], grad[:, (2 - tap) * cells : (4 - tap) * cells])
    for t in range(2):
        for r in range(2):
            at = slice((2 * t + r) * columns, (2 * t + r + 1) * columns)
            hidden[t, r] = acc[:, at].astype(BF)
            base[t, r] = back[:, at]


def coarse_kernel(
    me, first_a, first_b, second_a, second_b, w_time, mix, out_mix, direct, q_rows, u_rows, o_rows, d_rows, taps,
    local, grad_mix, grad_att, keep, send,
    stage, shifted, centre, pooled, upper, qkv, att_grad, att, qkv_grad, score, slope, weight, delta, fields, spread_all,
    rows_down, rows_up, rows_tap,
    *, coarse_frames, heads_axis, rest,
):
    step = pl.program_id(0)
    frame = me[0]
    quart = stage.shape[2]
    chans = stage.shape[3]
    padded = pooled.shape[1]
    tokens = coarse_frames * quart
    total = 2 * tokens
    chips = coarse_frames // 2
    heads = att.shape[1] // SLOT
    scale = 1.0 / math.sqrt(HD)
    part = 1.0 / heads_axis
    here_rows = pl.ds(pl.multiple_of(step * total, total), total)

    @pl.when(step == 0)
    def _():
        lane = lax.broadcasted_iota(jnp.int32, (pooled.shape[0], padded - chans), 1)
        pooled[:, chans:padded] = jnp.where(lane < 2, 1.0, 0.0).astype(BF)
        shifted[:, 3 * chans :] = jnp.zeros((shifted.shape[0], shifted.shape[1] - 3 * chans), BF)

    def entry(index):
        gap = index ^ frame
        return (reversed_bits(gap >> 1, chips) * 2 + (gap & 1)) * 3

    for color, sources in ((0, (first_a, first_b)), (1, (second_a, second_b))):
        place = step if color == 0 else reversed_bits(step, heads_axis)
        for late in range(2):

            @pl.when((place >= heads_axis // 2) == bool(late))
            def _():
                stage[color] = sources[late][0]

    for color in range(2):
        before = jnp.zeros((quart, chans), F32)
        here = stage[color, entry(0)].astype(F32)
        for u in range(coarse_frames):
            at = entry(u)
            last = stage[color, at + 1].astype(F32)
            after = stage[color, entry(u + 1)].astype(F32) if u + 1 < coarse_frames else jnp.zeros((quart, chans), F32)
            offset = color * tokens + u * quart
            rows = pl.ds(pl.multiple_of(step * total + offset, quart), quart)
            mid = 0.5 * (here + last)
            shifted[rows, 0:chans] = (0.5 * (before + here)).astype(BF)
            shifted[rows, chans : 2 * chans] = mid.astype(BF)
            shifted[rows, 2 * chans : 3 * chans] = (0.5 * (last + after)).astype(BF)
            centre[offset : offset + quart, :] = mid
            upper[rows, :] = stage[color, at + 2]
            before, here = last, after
    pool = (centre[...] + nn(shifted[here_rows, 0 : 3 * chans], w_time[...])).astype(BF)
    pooled[here_rows, 0:chans] = pool
    lines = pooled[here_rows, :]
    ups = upper[here_rows, :]
    qkv[...] = nn(lines, mix[...]).astype(BF)
    att_grad[...] = nt(ups, out_mix[...]).astype(BF)
    row = lax.broadcasted_iota(jnp.int32, (tokens, tokens), 0)
    col = lax.broadcasted_iota(jnp.int32, (tokens, tokens), 1)
    same = (row & (quart - 1)) == (col & (quart - 1))
    cases = [(color, n) for color in range(2) for n in range(heads)]

    def part_of(color, n, which):
        return qkv[color * tokens : (color + 1) * tokens, (3 * n + which) * SLOT : (3 * n + which + 1) * SLOT]

    def grad_of(color, n):
        return att_grad[color * tokens : (color + 1) * tokens, n * SLOT : (n + 1) * SLOT]

    for i, (color, n) in enumerate(cases):
        score[i] = nt(part_of(color, n, 0), part_of(color, n, 1))
        slope[i] = nt(grad_of(color, n), part_of(color, n, 2))
    for i, (color, n) in enumerate(cases):
        scores = jnp.where(same, score[i] * scale, -jnp.inf)
        ex = jnp.exp(scores - jnp.max(scores, axis=1, keepdims=True))
        probs = ex * (1.0 / jnp.sum(ex, axis=1, keepdims=True))
        dw = slope[i]
        inner = jnp.sum(probs * dw, axis=1, keepdims=True)
        weight[i] = probs.astype(BF)
        delta[i] = (probs * (dw - inner) * scale).astype(BF)
    for i, (color, n) in enumerate(cases):
        out = pl.ds(pl.multiple_of(step * total + color * tokens, tokens), tokens)
        att[out, n * SLOT : (n + 1) * SLOT] = nn(weight[i], part_of(color, n, 2)).astype(BF)
        qkv_grad[out, (3 * n) * SLOT : (3 * n + 1) * SLOT] = nn(delta[i], part_of(color, n, 1)).astype(BF)
        qkv_grad[out, (3 * n + 1) * SLOT : (3 * n + 2) * SLOT] = tn(delta[i], part_of(color, n, 0)).astype(BF)
        qkv_grad[out, (3 * n + 2) * SLOT : (3 * n + 3) * SLOT] = tn(weight[i], grad_of(color, n)).astype(BF)
    spread = nt(qkv_grad[here_rows, :], mix[...]) + nt(ups, direct[...]) * part
    spread = spread[:, 0:chans].astype(BF)
    spread_all[here_rows, :] = spread
    fields[...] = spread.reshape(2 * coarse_frames, quart, chans)
    mine = (frame >> 1) * 2
    att_rows, line_rows = [], []
    for color in range(2):
        rows = pl.ds(pl.multiple_of(step * total + color * tokens + mine * quart, 2 * quart), 2 * quart)
        att_rows.append(att[rows, :])
        line_rows.append(pooled[rows, :])
    lifted = nn(jnp.concatenate(att_rows, axis=0), out_mix[...])
    lifted = lifted + nn(jnp.concatenate(line_rows, axis=0), direct[...]) * part
    lifted = lifted.astype(BF).reshape(4, quart, chans)
    for color in range(2):
        for i in range(2):
            local[0, i, color] = lifted[2 * color + i]
        for i in range(4):
            at = jnp.clip(mine + i - 1, 0, coarse_frames - 1)
            local[0, 2 + i, color] = fields[color * coarse_frames + at]

    @pl.when(step == heads_axis - 1)
    def _():
        g = tn(pooled[...], qkv_grad[...])
        for i in range(3 * heads):
            grad_mix[:, i * HD : (i + 1) * HD] = g[:, i * SLOT : i * SLOT + HD].astype(BF)
        a = tn(att[...], upper[...])
        for n in range(heads):
            grad_att[n * HD : (n + 1) * HD, :] = a[n * SLOT : n * SLOT + HD, :].astype(BF)
        s = tn(pooled[...], upper[...]).astype(BF)
        pair = rows_tap.shape[0]
        own = shifted[:, pl.ds(pl.multiple_of((frame >> 1) * pair, pair), pair)]
        rows_tap[:, 0:chans] = tn(own, spread_all[...])
        rows_tap[:, chans:] = jnp.zeros((pair, padded - chans), F32)
        rows_down[...] = nt(q_rows[...], grad_mix[...]) + nt(u_rows[...], s) * part
        rows_up[:, 0:chans] = nn(o_rows[...], grad_att[...]) + nn(d_rows[...], s) * part
        rows_up[:, chans:] = jnp.zeros((rows_up.shape[0], padded - chans), F32)
        core = frame & 1
        p1, r3, piece = rest
        extra = jnp.zeros((piece - 2 * p1 - r3, padded), F32)
        for dest, which in ((keep, core), (send, 1 - core)):
            for j in range(heads_axis):
                at = pl.ds(pl.multiple_of((which * heads_axis + j) * p1, p1), p1)
                tap = rows_tap[pl.ds(pl.multiple_of((which * heads_axis + j) * r3, r3), r3), :]
                if dest is keep:
                    more = jnp.concatenate([taps[j * r3 : (j + 1) * r3, :].astype(F32), jnp.zeros((r3, padded - chans), F32)], axis=1)
                    tap = tap + more
                parts = [rows_down[at, :], rows_up[at, :], tap]
                if piece > 2 * p1 + r3:
                    parts.append(extra)
                dest[j] = jnp.concatenate(parts, axis=0).astype(BF)


def order_kernel(me, keep, got, *outs):
    head = me[1]
    for d, out in enumerate(outs):
        at = head ^ d
        out[...] = (keep[at].astype(F32) + got[at].astype(F32)).astype(BF)


def sum_kernel(*refs):
    acc = refs[0][...].astype(F32)
    for ref in refs[1:-1]:
        acc = acc + ref[...].astype(F32)
    refs[-1][...] = acc.astype(BF)


def local_kernel(me, *refs):
    parts, (mine, send, acc) = refs[:-3], refs[-3:]
    core = me[0] & 1
    for i in range(acc.shape[0]):
        value = parts[0][i].astype(F32)
        for ref in parts[1:]:
            value = value + ref[i].astype(F32)
        acc[i] = value
    for dest, which in ((mine, core), (send, 1 - core)):
        dest[0] = acc[which].astype(BF)
        for i in range(3):
            dest[1 + i] = acc[2 + which + i].astype(BF)


def split_grad_kernel(down, mix_a, mix_b, att_a, att_b, w_up, qkv_out, att_out, flipped):
    @pl.when(pl.program_id(0) == 0)
    def _():
        flipped[...] = (mix_a[...].astype(F32) + mix_b[...].astype(F32)).T.astype(BF)

    qkv_out[...] = nn(flipped[...], down[...])
    att_out[...] = nn((att_a[...].astype(F32) + att_b[...].astype(F32)).astype(BF), w_up[...])


def finish_kernel(me, hidden, base, own, other, w_time, output, grad_clip, rows, *, coarse_frames):
    frame = me[0]
    core = frame & 1
    half = own.shape[1]
    columns = hidden.shape[3]
    for i in range(4):
        rows[i, pl.ds(pl.multiple_of(core * half, half), half), :] = own[i].astype(F32)
        rows[i, pl.ds(pl.multiple_of((1 - core) * half, half), half), :] = other[i].astype(F32)
    lift = pool_matrix(2 * half, columns)
    fine = tn(rows[0].astype(BF), lift)
    for t in range(2):
        for r in range(2):
            output[t, r] = (hidden[t, r].astype(F32) + fine).astype(BF)
    before = (rows[1] * jnp.where(frame == 0, 0.0, 1.0)).astype(BF)
    here = rows[2].astype(BF)
    after = (rows[3] * jnp.where(frame == coarse_frames - 1, 0.0, 1.0)).astype(BF)
    mid = rows[2] + nt(here, w_time[1])
    even = mid + nt(here, w_time[0]) + nt(before, w_time[2])
    odd = mid + nt(after, w_time[0]) + nt(here, w_time[2])
    for t, value in ((0, even), (1, odd)):
        high = value.astype(BF)
        low = (value - high.astype(F32)).astype(BF)
        add = (tn(high, lift) + tn(low, lift)) * 0.125
        for r in range(2):
            grad_clip[t, r] = base[t, r] + add


def gather_kernel(me, embed, *refs, layout, aligned):
    pieces = refs[:8]
    time_out, down_rows, up_rows = refs[8], refs[-2], refs[-1]
    frame, head = me[0], me[1]
    chips, heads_axis, r1, p1, r3 = layout
    chans = time_out.shape[2]
    devices = 2 * chips * heads_axis
    for core in range(2):
        for idx in range(chips * heads_axis):
            hi, zi = idx // chips, idx % chips
            colors = []
            for color in range(2):
                off = hi if color == 0 else reversed_bits(hi, heads_axis)
                edge = heads_axis // 2
                src = pieces[4 * core + 2 * color + off // edge]
                colors.append(src[off % edge, zi].astype(F32))
            value = jnp.concatenate(colors, axis=0)
            owner = (frame ^ (reversed_bits(zi, chips) * 2 + core)) * heads_axis + (head ^ hi)
            down_rows[owner] = value[0:r1]
            up_rows[owner] = value[p1 : p1 + r1]

            @pl.when(owner < time_out.shape[0])
            def _():
                time_out[owner] = value[2 * p1 : 2 * p1 + r3, 0:chans]

    if aligned:
        down_out, embed_out, up_out = refs[9], refs[10], refs[11]
        lanes = down_rows.shape[2]
        eye = (lax.broadcasted_iota(jnp.int32, (lanes, lanes), 0) == lax.broadcasted_iota(jnp.int32, (lanes, lanes), 1))
        eye = eye.astype(F32).astype(BF)
        flipped = nt(eye, down_rows[...].reshape(devices * r1, lanes).astype(BF))
        down_out[...] = flipped[0:chans]
        embed_out[...] = embed[...] * flipped[chans : chans + 1]
        up_out[...] = nt(eye, up_rows[...].reshape(devices * r1, lanes).astype(BF))[0:chans]


def double(x, axis, bits, dim):
    for bit in bits:
        got = swap(x, axis, bit)
        x = jnp.concatenate([x, got], axis=dim)
    return x


def cross(first, second, bits):
    for i, (a, b) in enumerate(zip(bits, reversed(bits))):
        first_in = swap(first, "heads", a)
        second_in = swap(second, "heads", b)
        if i + 1 < len(bits):
            first = jnp.concatenate([first, first_in], axis=0)
            second = jnp.concatenate([second, second_in], axis=0)
    return first, first_in, second, second_in


def body(clip, w_time, w_down, w_embed, w_qkv, w_out, w_up, timestep, cotangent):
    nf = lax.axis_size("frames")
    nh = lax.axis_size("heads")
    f = lax.axis_index("frames")
    h = lax.axis_index("heads")
    me = jnp.stack([f, h]).astype(jnp.int32)
    _, _, columns, chans = clip.shape
    width = w_down.shape[1]
    half_c = columns // 2
    half = half_c // 2
    quart = half // 2
    chips = nf // 2
    padded = round_up(chans + 2, 128)
    pieces = w_qkv.shape[1] // HD
    heads = pieces // 3
    chip_bits = [2 * b for b in reversed(bit_list(chips))]
    head_bits = bit_list(nh)
    devices = nf * nh

    clip_t = clip.transpose(0, 1, 3, 2)
    cot_t = cotangent.transpose(0, 1, 3, 2)
    w_qkv_t = w_qkv.T
    w_up_t = w_up.T

    keep, send = call(
        pool_kernel,
        [sds((2, 3, quart, chans), BF)] * 2,
        in_specs=[smem(), vmem(), vmem()],
        out_specs=[vmem()] * 2,
        scratch_shapes=[pltpu.VMEM((3, half_c, chans), F32)],
    )(me, clip_t, cot_t)
    keep_in = swap(send, "frames", 1)
    block = jnp.concatenate([keep, keep_in], axis=1)
    block = double(block, "frames", chip_bits, 1)
    first, second = block[0][None], block[1][None]

    embed = time_embed(timestep, w_embed.shape[0])
    down, mix, out_mix, direct = call(
        weight_kernel,
        [
            sds((padded, width), BF),
            sds((padded, pieces * SLOT), BF),
            sds((heads * SLOT, chans), BF),
            sds((padded, chans), BF),
        ],
    )(w_down, w_embed, embed[None, :], w_qkv_t, w_out, w_up_t)

    head, tail = call(
        edge_kernel,
        [sds((4, chans, columns), BF)] * 2,
        in_specs=[vmem(), vmem(), pl.BlockSpec(memory_space=pl.ANY)],
        out_specs=[vmem()] * 2,
    )(clip_t, cot_t, keep)
    lo = lax.ppermute(tail, "frames", [(i, i + 1) for i in range(nf - 1)])
    hi = lax.ppermute(head, "frames", [(i + 1, i) for i in range(nf - 1)])
    tap_rows = round_up(3 * chans, devices * 8)
    hidden, base, taps = call(
        fine_kernel,
        [
            sds(clip_t.shape, BF),
            sds(clip_t.shape, F32),
            sds((tap_rows, chans), BF),
        ],
        scratch_shapes=[pltpu.VMEM((chans, 8 * columns), BF)] * 2,
    )(clip_t, cot_t, lo, hi, w_time)
    share = tap_rows // nf
    bits = bit_list(nf)
    taps = taps.reshape([2] * len(bits) + [share, chans])
    for i in range(len(bits)):
        axis = len(bits) - 1 - i
        mine = (f >> i) & 1
        other = lax.dynamic_index_in_dim(taps, 1 - mine, axis, keepdims=False)
        same = lax.dynamic_index_in_dim(taps, mine, axis, keepdims=False)
        got = swap(other, "frames", 1 << i)
        taps = (same.astype(F32) + got.astype(F32)).astype(BF)

    chip_rows = 2 * width // nf
    r1 = width // devices
    p1 = round_up(r1, 8)
    r3 = share // nh
    piece_rows = round_up(2 * p1 + r3, 16)
    start, first, second = lax.optimization_barrier(((f >> 1) * chip_rows, first, second))
    sides = cross(first, second, head_bits)

    def rows_of(x, axis):
        x = lax.dynamic_slice_in_dim(x, start, chip_rows, axis=axis)
        x = x.T if axis == 1 else x
        x = x.reshape(2 * nh, r1, x.shape[1])
        return jnp.pad(x, ((0, 0), (0, p1 - r1), (0, 0))).reshape(2 * nh * p1, x.shape[2])

    q_rows = rows_of(w_qkv, 0)
    u_rows = rows_of(w_up, 0)
    o_rows = rows_of(w_out, 1)
    d_rows = rows_of(down, 1)

    edge = nh // 2

    def side(mirrored, late):
        def index(g):
            at = reversed_bits(g, nh) if mirrored else g
            at = jnp.maximum(at - edge, 0) if late else jnp.minimum(at, edge - 1)
            return (at, 0, 0, 0)

        return pl.BlockSpec((1, nf * 3, quart, chans), index)

    side_specs = [side(False, False), side(False, True), side(True, False), side(True, True)]
    total = 2 * nf * quart
    every = nh * total

    def whole(*shape):
        return pl.BlockSpec(shape, lambda g: (0,) * len(shape))

    w_time2 = w_time.reshape(3 * chans, chans)
    statics = (w_time2, mix, out_mix, direct, q_rows, u_rows, o_rows, d_rows, taps)
    local, mix_g, att_g, d_keep, d_send = call(
        functools.partial(coarse_kernel, coarse_frames=nf, heads_axis=nh, rest=(p1, r3, piece_rows)),
        [
            sds((nh, 6, 2, quart, chans), BF),
            sds((padded, pieces * HD), BF),
            sds((heads * HD, chans), BF),
            sds((nh, piece_rows, padded), BF),
            sds((nh, piece_rows, padded), BF),
        ],
        grid=(nh,),
        in_specs=[smem()] + side_specs + [whole(*x.shape) for x in statics],
        out_specs=[
            pl.BlockSpec((1, 6, 2, quart, chans), lambda g: (g, 0, 0, 0, 0)),
            whole(padded, pieces * HD),
            whole(heads * HD, chans),
            whole(nh, piece_rows, padded),
            whole(nh, piece_rows, padded),
        ],
        scratch_shapes=[
            pltpu.VMEM((2, nf * 3, quart, chans), BF),
            pltpu.VMEM((every, tap_rows), BF),
            pltpu.VMEM((total, chans), F32),
            pltpu.VMEM((every, padded), BF),
            pltpu.VMEM((every, chans), BF),
            pltpu.VMEM((total, pieces * SLOT), BF),
            pltpu.VMEM((total, heads * SLOT), BF),
            pltpu.VMEM((every, heads * SLOT), BF),
            pltpu.VMEM((every, pieces * SLOT), BF),
            pltpu.VMEM((2 * heads, total // 2, total // 2), F32),
            pltpu.VMEM((2 * heads, total // 2, total // 2), F32),
            pltpu.VMEM((2 * heads, total // 2, total // 2), BF),
            pltpu.VMEM((2 * heads, total // 2, total // 2), BF),
            pltpu.VMEM((2 * nf, quart, chans), BF),
            pltpu.VMEM((every, chans), BF),
            pltpu.VMEM((2 * nh * p1, padded), F32),
            pltpu.VMEM((2 * nh * p1, padded), F32),
            pltpu.VMEM((2 * share, padded), F32),
        ],
    )(me, *sides, *statics)

    d_got = swap(d_send, "frames", 1)
    ordered = call(
        order_kernel,
        [sds((piece_rows, padded), BF)] * nh,
        in_specs=[smem(), vmem(), vmem()],
        out_specs=[vmem()] * nh,
    )(me, d_keep, d_got)
    got = []
    for d in range(1, nh):
        got.append(swap(ordered[d], "heads", d))
    piece = call(sum_kernel, sds((piece_rows, padded), BF))(ordered[0], *got)
    piece = piece.reshape(2, 1, piece_rows // 2, padded)
    piece = double(piece, "frames", chip_bits, 1)
    shares = cross(piece[0][None], piece[1][None], head_bits)
    mates = []
    for x in shares:
        mates.append(swap(x, "frames", 1))

    got = []
    for d in range(1, nh):
        got.append(swap(local[d], "heads", d))
    four = sds((4, 2, quart, chans), BF)
    mine4, send4 = call(
        local_kernel,
        [four, four],
        in_specs=[smem()] + [vmem()] * nh,
        out_specs=[vmem()] * 2,
        scratch_shapes=[pltpu.VMEM(local.shape[1:], F32)],
    )(me, local[0], *got)
    other4 = swap(send4, "frames", 1)
    mine4 = mine4.reshape(4, half, chans)
    other4 = other4.reshape(4, half, chans)
    output, grad_clip = call(
        functools.partial(finish_kernel, coarse_frames=nf),
        [sds(clip_t.shape, BF), sds(clip_t.shape, F32)],
        in_specs=[smem()] + [vmem()] * 5,
        out_specs=[vmem()] * 2,
        scratch_shapes=[pltpu.VMEM((4, half_c, chans), F32)],
    )(me, hidden, base, mine4, other4, w_time)

    mix_o = swap(mix_g, "frames", 1)
    att_o = swap(att_g, "frames", 1)
    step = 256
    grad_qkv, grad_out = call(
        split_grad_kernel,
        [sds((pieces * HD, width), F32), sds((heads * HD, width), F32)],
        grid=(width // step,),
        in_specs=[
            pl.BlockSpec((padded, step), lambda g: (0, g)),
            whole(*mix_g.shape),
            whole(*mix_g.shape),
            whole(*att_g.shape),
            whole(*att_g.shape),
            pl.BlockSpec((chans, step), lambda g: (0, g)),
        ],
        out_specs=[
            pl.BlockSpec((pieces * HD, step), lambda g: (0, g)),
            pl.BlockSpec((heads * HD, step), lambda g: (0, g)),
        ],
        scratch_shapes=[pltpu.VMEM((pieces * HD, padded), BF)],
    )(down, mix_g, mix_o, att_g, att_o, w_up_t)

    output, grad_clip, grad_qkv, grad_out, mates[3] = lax.optimization_barrier(
        (output, grad_clip, grad_qkv, grad_out, mates[3])
    )
    aligned = r1 % 8 == 0
    layout = (chips, nh, r1, p1, r3)
    outs = [sds((3 * chans // r3, r3, chans), F32)]
    table = (devices, r1, padded)
    scratch = []
    if aligned:
        outs += [sds((chans, width), F32), sds((w_embed.shape[0], width), F32), sds((chans, width), F32)]
        scratch = [pltpu.VMEM(table, F32)] * 2
    else:
        outs += [sds(table, F32)] * 2
    embed_col = embed.astype(F32)[:, None]
    got = call(
        functools.partial(gather_kernel, layout=layout, aligned=aligned),
        outs,
        in_specs=[smem()] + [vmem()] * 9,
        out_specs=[vmem()] * len(outs),
        scratch_shapes=scratch,
    )(me, embed_col, *shares, *mates)
    grad_time = got[0].reshape(w_time.shape)
    if aligned:
        grad_down, grad_embed, grad_up = got[1], got[2], got[3].T
    else:
        down_rows = got[1].reshape(width, padded)
        grad_down = down_rows[:, :chans].T
        grad_embed = embed_col * down_rows[:, chans][None, :]
        grad_up = got[2].reshape(width, padded)[:, :chans]
    return (
        output.transpose(0, 1, 3, 2),
        grad_clip.transpose(0, 1, 3, 2),
        grad_time,
        grad_down,
        grad_embed,
        grad_qkv.T,
        grad_out,
        grad_up,
    )


def solution(mesh):
    return jax.shard_map(
        body,
        mesh=mesh,
        in_specs=(
            P("frames", "heads", None, None),
            P(),
            P(),
            P(),
            P(None, "heads"),
            P("heads", None),
            P(),
            P(),
            P("frames", "heads", None, None),
        ),
        out_specs=(
            P("frames", "heads", None, None),
            P("frames", "heads", None, None),
            P(),
            P(),
            P(),
            P(None, "heads"),
            P("heads", None),
            P(),
        ),
        check_vma=False,
    )
```

```python
import functools
import math

import jax
import jax.numpy as jnp
from jax import lax
from jax.experimental import pallas as pl
from jax.experimental.pallas import tpu as pltpu
from jax.sharding import PartitionSpec as P


HD = 80
SLOT = 128
BF = jnp.bfloat16
F32 = jnp.float32


def nn(a, b):
    return lax.dot_general(a, b, (((1,), (0,)), ((), ())), preferred_element_type=F32)


def nt(a, b):
    return lax.dot_general(a, b, (((1,), (1,)), ((), ())), preferred_element_type=F32)


def tn(a, b):
    return lax.dot_general(a, b, (((0,), (0,)), ((), ())), preferred_element_type=F32)


def round_up(value, step):
    return -(-value // step) * step


def call(kernel, out_shape, **kw):
    return pl.pallas_call(
        kernel,
        out_shape=out_shape,
        compiler_params=pltpu.CompilerParams(vmem_limit_bytes=56 * 1024 * 1024),
        **kw,
    )


def smem():
    return pl.BlockSpec(memory_space=pltpu.SMEM)


def vmem():
    return pl.BlockSpec(memory_space=pltpu.VMEM)


def sds(shape, dtype):
    return jax.ShapeDtypeStruct(shape, dtype)


def bit_list(count):
    bits = []
    while (1 << len(bits)) < count:
        bits.append(1 << len(bits))
    return bits


def reversed_bits(value, count):
    n = len(bit_list(count))
    out = 0
    for i in range(n):
        out = out + (((value >> i) & 1) << (n - 1 - i))
    return out


def swap(x, axis, bit):
    n = lax.axis_size(axis)
    return lax.ppermute(x, axis, [(i, i ^ bit) for i in range(n)])


def time_embed(timestep, width):
    half = width // 2
    freqs = jnp.exp(-math.log(10000.0) * jnp.arange(half, dtype=F32) / half)
    angle = timestep.astype(F32)[0] * freqs
    return jax.nn.silu(jnp.concatenate([jnp.cos(angle), jnp.sin(angle)])).astype(BF)


def pool_matrix(half_c, columns):
    row = lax.broadcasted_iota(jnp.int32, (half_c, columns), 0)
    col = lax.broadcasted_iota(jnp.int32, (half_c, columns), 1)
    return jnp.where((col >> 1) == row, 1.0, 0.0).astype(BF)


def fold(x):
    half = x.shape[0] // 2
    return jnp.concatenate([x[:half], x[half:]], axis=1).astype(BF)


def unfold(x):
    half = x.shape[1] // 2
    x = x.astype(F32)
    return jnp.concatenate([x[:, :half], x[:, half:]], axis=0)


def pool_kernel(me, clip, cot, keep, send, tmp):
    half_c = tmp.shape[1]
    half = half_c // 2
    quart = half // 2
    pool = pool_matrix(half_c, clip.shape[3])
    for t in range(2):
        tmp[t] = (nt(pool, clip[t, 0]) + nt(pool, clip[t, 1])) * 0.25
    tmp[2] = (nt(pool, cot[0, 0]) + nt(pool, cot[0, 1])) + (nt(pool, cot[1, 0]) + nt(pool, cot[1, 1]))
    core = me[0] & 1
    for color in range(2):
        for item in range(3):
            base = pl.multiple_of(core * half + color * quart, quart)
            keep[color, item] = fold(tmp[item, pl.ds(base, quart), :])
            base = pl.multiple_of((1 - core) * half + color * quart, quart)
            send[color, item] = fold(tmp[item, pl.ds(base, quart), :])


def edge_kernel(clip, cot, after, head, tail):
    del after
    for r in range(2):
        head[r] = clip[0, r]
        head[2 + r] = cot[0, r]
        tail[r] = clip[1, r]
        tail[2 + r] = cot[1, r]


def weight_kernel(w_down, w_embed, embed, w_qkv, w_out, w_up, down, mix, out_mix, direct):
    chans = w_down.shape[0]
    padded = down.shape[0]
    shift = nn(embed[...], w_embed[...])
    high = shift.astype(BF)
    low = (shift - high.astype(F32)).astype(BF)
    down[0:chans, :] = w_down[...]
    row = lax.broadcasted_iota(jnp.int32, (padded - chans, shift.shape[1]), 0)
    tail = jnp.where(row == 0, high.astype(F32), jnp.where(row == 1, low.astype(F32), 0.0))
    down[chans:padded, :] = tail.astype(BF)
    full = down[...]
    pieces = w_qkv.shape[0] // HD
    prod = nt(full, w_qkv[...])
    mix[...] = jnp.zeros(mix.shape, BF)
    for i in range(pieces):
        mix[:, i * SLOT : i * SLOT + HD] = prod[:, i * HD : (i + 1) * HD].astype(BF)
    up = w_up[...]
    small = nt(w_out[...], up)
    out_mix[...] = jnp.zeros(out_mix.shape, BF)
    for i in range(pieces // 3):
        out_mix[i * SLOT : i * SLOT + HD, :] = small[i * HD : (i + 1) * HD, :].astype(BF)
    direct[...] = nt(full, up).astype(BF)


def fine_kernel(clip, cot, lo, hi, w_time, hidden, base, taps, wide, grad):
    chans = w_time.shape[1]
    columns = clip.shape[3]
    for t in range(4):
        for r in range(2):
            at = slice((2 * t + r) * columns, (2 * t + r + 1) * columns)
            if t in (0, 3):
                halo = lo if t == 0 else hi
                wide[:, at] = halo[r]
                grad[:, at] = halo[2 + r]
            else:
                wide[:, at] = clip[t - 1, r]
                grad[:, at] = cot[t - 1, r]
    cells = 2 * columns
    taps[3 * chans :, :] = jnp.zeros((taps.shape[0] - 3 * chans, chans), BF)
    here = grad[:, cells : 3 * cells]
    for tap in range(3):
        taps[tap * chans : (tap + 1) * chans, :] = nt(wide[:, tap * cells : (tap + 2) * cells], here).astype(BF)
    acc = wide[:, cells : 3 * cells].astype(F32)
    back = here.astype(F32)
    for tap in range(3):
        acc = acc + tn(w_time[tap], wide[:, tap * cells : (tap + 2) * cells])
        back = back + nn(w_time[tap], grad[:, (2 - tap) * cells : (4 - tap) * cells])
    for t in range(2):
        for r in range(2):
            at = slice((2 * t + r) * columns, (2 * t + r + 1) * columns)
            hidden[t, r] = acc[:, at].astype(BF)
            base[t, r] = back[:, at]


def coarse_kernel(
    me, first_a, first_b, second_a, second_b, w_time, mix, out_mix, direct, taps, *refs,
    coarse_frames, heads_axis, rest,
):
    p1, r3, piece, panes, shift = rest
    windows = [refs[i * panes : (i + 1) * panes] for i in range(4)]
    local = refs[4 * panes : 4 * panes + heads_axis]
    grad_mix, grad_att, keep, send = refs[4 * panes + heads_axis : 4 * panes + heads_axis + 4]
    (
    stage, shifted, centre, pooled, upper, qkv, att_grad, att, qkv_grad, score, slope, weight, delta, fields, spread_all,
    rows_down, rows_up, rows_tap,
    ) = refs[4 * panes + heads_axis + 4 :]
    step = pl.program_id(0)
    frame = me[0]
    quart = 2 * stage.shape[2]
    chans = stage.shape[3] // 2
    padded = pooled.shape[1]
    tokens = coarse_frames * quart
    total = 2 * tokens
    chips = coarse_frames // 2
    heads = att.shape[1] // SLOT
    scale = 1.0 / math.sqrt(HD)
    part = 1.0 / heads_axis
    here_rows = pl.ds(pl.multiple_of(step * total, total), total)

    @pl.when(step == 0)
    def _():
        lane = lax.broadcasted_iota(jnp.int32, (pooled.shape[0], padded - chans), 1)
        pooled[:, chans:padded] = jnp.where(lane < 2, 1.0, 0.0).astype(BF)
        shifted[:, 3 * chans :] = jnp.zeros((shifted.shape[0], shifted.shape[1] - 3 * chans), BF)

    def entry(index):
        gap = index ^ frame
        return (reversed_bits(gap >> 1, chips) * 2 + (gap & 1)) * 3

    for color, sources in ((0, (first_a, first_b)), (1, (second_a, second_b))):
        place = step if color == 0 else reversed_bits(step, heads_axis)
        for late in range(2):

            @pl.when((place >= heads_axis // 2) == bool(late))
            def _():
                stage[color] = sources[late][0]

    for color in range(2):
        before = jnp.zeros((quart, chans), F32)
        here = unfold(stage[color, entry(0)])
        for u in range(coarse_frames):
            at = entry(u)
            last = unfold(stage[color, at + 1])
            after = unfold(stage[color, entry(u + 1)]) if u + 1 < coarse_frames else jnp.zeros((quart, chans), F32)
            offset = color * tokens + u * quart
            rows = pl.ds(pl.multiple_of(step * total + offset, quart), quart)
            mid = 0.5 * (here + last)
            shifted[rows, 0:chans] = (0.5 * (before + here)).astype(BF)
            shifted[rows, chans : 2 * chans] = mid.astype(BF)
            shifted[rows, 2 * chans : 3 * chans] = (0.5 * (last + after)).astype(BF)
            centre[offset : offset + quart, :] = mid
            upper[rows, :] = unfold(stage[color, at + 2]).astype(BF)
            before, here = last, after
    pool = (centre[...] + nn(shifted[here_rows, 0 : 3 * chans], w_time[...])).astype(BF)
    pooled[here_rows, 0:chans] = pool
    lines = pooled[here_rows, :]
    ups = upper[here_rows, :]
    qkv[...] = nn(lines, mix[...]).astype(BF)
    att_grad[...] = nt(ups, out_mix[...]).astype(BF)
    row = lax.broadcasted_iota(jnp.int32, (tokens, tokens), 0)
    col = lax.broadcasted_iota(jnp.int32, (tokens, tokens), 1)
    same = (row & (quart - 1)) == (col & (quart - 1))
    cases = [(color, n) for color in range(2) for n in range(heads)]

    def part_of(color, n, which):
        return qkv[color * tokens : (color + 1) * tokens, (3 * n + which) * SLOT : (3 * n + which + 1) * SLOT]

    def grad_of(color, n):
        return att_grad[color * tokens : (color + 1) * tokens, n * SLOT : (n + 1) * SLOT]

    for i, (color, n) in enumerate(cases):
        score[i] = nt(part_of(color, n, 0), part_of(color, n, 1))
        slope[i] = nt(grad_of(color, n), part_of(color, n, 2))
    for i, (color, n) in enumerate(cases):
        scores = jnp.where(same, score[i] * scale, -jnp.inf)
        ex = jnp.exp(scores - jnp.max(scores, axis=1, keepdims=True))
        probs = ex * (1.0 / jnp.sum(ex, axis=1, keepdims=True))
        dw = slope[i]
        inner = jnp.sum(probs * dw, axis=1, keepdims=True)
        weight[i] = probs.astype(BF)
        delta[i] = (probs * (dw - inner) * scale).astype(BF)
    for i, (color, n) in enumerate(cases):
        out = pl.ds(pl.multiple_of(step * total + color * tokens, tokens), tokens)
        att[out, n * SLOT : (n + 1) * SLOT] = nn(weight[i], part_of(color, n, 2)).astype(BF)
        qkv_grad[out, (3 * n) * SLOT : (3 * n + 1) * SLOT] = nn(delta[i], part_of(color, n, 1)).astype(BF)
        qkv_grad[out, (3 * n + 1) * SLOT : (3 * n + 2) * SLOT] = tn(delta[i], part_of(color, n, 0)).astype(BF)
        qkv_grad[out, (3 * n + 2) * SLOT : (3 * n + 3) * SLOT] = tn(weight[i], grad_of(color, n)).astype(BF)
    spread = nt(qkv_grad[here_rows, :], mix[...]) + nt(ups, direct[...]) * part
    spread = spread[:, 0:chans].astype(BF)
    spread_all[here_rows, :] = spread
    fields[...] = spread.reshape(2 * coarse_frames, quart, chans)
    mine = (frame >> 1) * 2
    att_rows, line_rows = [], []
    for color in range(2):
        rows = pl.ds(pl.multiple_of(step * total + color * tokens + mine * quart, 2 * quart), 2 * quart)
        att_rows.append(att[rows, :])
        line_rows.append(pooled[rows, :])
    lifted = nn(jnp.concatenate(att_rows, axis=0), out_mix[...])
    lifted = lifted + nn(jnp.concatenate(line_rows, axis=0), direct[...]) * part
    lifted = lifted.astype(BF).reshape(4, quart, chans)
    for d in range(heads_axis):

        @pl.when(step == d)
        def _():
            for color in range(2):
                for i in range(2):
                    local[d][i, color] = lifted[2 * color + i]
                for i in range(4):
                    at = jnp.clip(mine + i - 1, 0, coarse_frames - 1)
                    local[d][2 + i, color] = fields[color * coarse_frames + at]

    @pl.when(step == heads_axis - 1)
    def _():
        g = tn(pooled[...], qkv_grad[...])
        for i in range(3 * heads):
            grad_mix[:, i * HD : (i + 1) * HD] = g[:, i * SLOT : i * SLOT + HD].astype(BF)
        a = tn(att[...], upper[...])
        for n in range(heads):
            grad_att[n * HD : (n + 1) * HD, :] = a[n * SLOT : n * SLOT + HD, :].astype(BF)
        s = tn(pooled[...], upper[...]).astype(BF)
        pair = rows_tap.shape[0]
        own = shifted[:, pl.ds(pl.multiple_of((frame >> 1) * pair, pair), pair)]
        rows_tap[:, 0:chans] = tn(own, spread_all[...])
        rows_tap[:, chans:] = jnp.zeros((pair, padded - chans), F32)
        q_win, u_win, o_win, d_win = [jnp.concatenate([ref[...] for ref in group], axis=1) for group in windows]
        down_t = nn(grad_mix[...], q_win) + nn(s, u_win) * part
        rows_down[...] = down_t.astype(BF).T.astype(F32)
        up_t = tn(grad_att[...], o_win) + tn(s, d_win) * part
        rows_up[:, 0:chans] = up_t.astype(BF).T.astype(F32)
        rows_up[:, chans:] = jnp.zeros((rows_up.shape[0], padded - chans), F32)
        core = frame & 1
        base = ((frame >> 1) * shift) & (SLOT - 1)
        extra = jnp.zeros((piece - 2 * p1 - r3, padded), F32)
        for dest, which in ((keep, core), (send, 1 - core)):
            for j in range(heads_axis):
                at = pl.ds(pl.multiple_of(base + (which * heads_axis + j) * p1, 8), p1)
                tap = rows_tap[pl.ds(pl.multiple_of((which * heads_axis + j) * r3, r3), r3), :]
                if dest is keep:
                    more = jnp.concatenate([taps[j * r3 : (j + 1) * r3, :].astype(F32), jnp.zeros((r3, padded - chans), F32)], axis=1)
                    tap = tap + more
                parts = [rows_down[at, :], rows_up[at, :], tap]
                if piece > 2 * p1 + r3:
                    parts.append(extra)
                dest[j] = jnp.concatenate(parts, axis=0).astype(BF)


def order_kernel(me, keep, got, *outs):
    head = me[1]
    for d, out in enumerate(outs):
        at = head ^ d
        out[...] = (keep[at].astype(F32) + got[at].astype(F32)).astype(BF)


def sum_kernel(*refs):
    acc = refs[0][...].astype(F32)
    for ref in refs[1:-1]:
        acc = acc + ref[...].astype(F32)
    refs[-1][...] = acc.astype(BF)


def local_kernel(me, *refs):
    parts, (mine, send, acc) = refs[:-3], refs[-3:]
    core = me[0] & 1
    for i in range(acc.shape[0]):
        value = parts[0][i].astype(F32)
        for ref in parts[1:]:
            value = value + ref[i].astype(F32)
        acc[i] = value
    for dest, which in ((mine, core), (send, 1 - core)):
        dest[0] = acc[which].astype(BF)
        for i in range(3):
            dest[1 + i] = acc[2 + which + i].astype(BF)


def split_grad_kernel(down, mix_a, mix_b, *refs, late):
    if late:
        _, qkv_out, flipped = refs
    else:
        att_a, att_b, w_up, qkv_out, att_out, flipped = refs

    @pl.when(pl.program_id(0) == 0)
    def _():
        flipped[...] = (mix_a[...].astype(F32) + mix_b[...].astype(F32)).T.astype(BF)
        if not late:
            att_out[...] = nn((att_a[...].astype(F32) + att_b[...].astype(F32)).astype(BF), w_up[...])

    qkv_out[...] = nn(flipped[...], down[...])


def finish_kernel(me, hidden, base, own, other, w_time, output, grad_clip, rows, *, coarse_frames):
    frame = me[0]
    core = frame & 1
    half = own.shape[1]
    columns = hidden.shape[3]
    for i in range(4):
        rows[i, pl.ds(pl.multiple_of(core * half, half), half), :] = own[i].astype(F32)
        rows[i, pl.ds(pl.multiple_of((1 - core) * half, half), half), :] = other[i].astype(F32)
    lift = pool_matrix(2 * half, columns)
    fine = tn(rows[0].astype(BF), lift)
    for t in range(2):
        for r in range(2):
            output[t, r] = (hidden[t, r].astype(F32) + fine).astype(BF)
    before = (rows[1] * jnp.where(frame == 0, 0.0, 1.0)).astype(BF)
    here = rows[2].astype(BF)
    after = (rows[3] * jnp.where(frame == coarse_frames - 1, 0.0, 1.0)).astype(BF)
    mid = rows[2] + nt(here, w_time[1])
    even = mid + nt(here, w_time[0]) + nt(before, w_time[2])
    odd = mid + nt(after, w_time[0]) + nt(here, w_time[2])
    for t, value in ((0, even), (1, odd)):
        high = value.astype(BF)
        low = (value - high.astype(F32)).astype(BF)
        add = (tn(high, lift) + tn(low, lift)) * 0.125
        for r in range(2):
            grad_clip[t, r] = base[t, r] + add


def gather_kernel(me, embed, *refs, layout, aligned):
    pieces = refs[:8]
    time_out, down_rows, up_rows = refs[8], refs[-2], refs[-1]
    frame, head = me[0], me[1]
    chips, heads_axis, r1, p1, r3 = layout
    chans = time_out.shape[2]
    devices = 2 * chips * heads_axis
    for core in range(2):
        for idx in range(chips * heads_axis):
            hi, zi = idx // chips, idx % chips
            colors = []
            for color in range(2):
                off = hi if color == 0 else reversed_bits(hi, heads_axis)
                edge = heads_axis // 2
                src = pieces[4 * core + 2 * color + off // edge]
                colors.append(src[off % edge, zi].astype(F32))
            value = jnp.concatenate(colors, axis=0)
            owner = (frame ^ (reversed_bits(zi, chips) * 2 + core)) * heads_axis + (head ^ hi)
            down_rows[owner] = value[0:r1]
            up_rows[owner] = value[p1 : p1 + r1]

            @pl.when(owner < time_out.shape[0])
            def _():
                time_out[owner] = value[2 * p1 : 2 * p1 + r3, 0:chans]

    if aligned:
        down_out, embed_out, up_out = refs[9], refs[10], refs[11]
        lanes = down_rows.shape[2]
        eye = (lax.broadcasted_iota(jnp.int32, (lanes, lanes), 0) == lax.broadcasted_iota(jnp.int32, (lanes, lanes), 1))
        eye = eye.astype(F32).astype(BF)
        flipped = nt(eye, down_rows[...].reshape(devices * r1, lanes).astype(BF))
        down_out[...] = flipped[0:chans]
        embed_out[...] = embed[...] * flipped[chans : chans + 1]
        up_out[...] = nt(eye, up_rows[...].reshape(devices * r1, lanes).astype(BF))[0:chans]


def double(x, axis, bits, dim):
    for bit in bits:
        got = swap(x, axis, bit)
        x = jnp.concatenate([x, got], axis=dim)
    return x


def cross(first, second, bits):
    for i, (a, b) in enumerate(zip(bits, reversed(bits))):
        first_in = swap(first, "heads", a)
        second_in = swap(second, "heads", b)
        if i + 1 < len(bits):
            first = jnp.concatenate([first, first_in], axis=0)
            second = jnp.concatenate([second, second_in], axis=0)
    return first, first_in, second, second_in


def body(clip, w_time, w_down, w_embed, w_qkv, w_out, w_up, timestep, cotangent):
    nf = lax.axis_size("frames")
    nh = lax.axis_size("heads")
    f = lax.axis_index("frames")
    h = lax.axis_index("heads")
    me = jnp.stack([f, h]).astype(jnp.int32)
    _, _, columns, chans = clip.shape
    width = w_down.shape[1]
    half_c = columns // 2
    half = half_c // 2
    quart = half // 2
    chips = nf // 2
    padded = round_up(chans + 2, 128)
    pieces = w_qkv.shape[1] // HD
    heads = pieces // 3
    chip_bits = [2 * b for b in reversed(bit_list(chips))]
    head_bits = bit_list(nh)
    devices = nf * nh

    clip_t = clip.transpose(0, 1, 3, 2)
    cot_t = cotangent.transpose(0, 1, 3, 2)
    w_qkv_t = w_qkv.T
    w_up_t = w_up.T

    keep, send = call(
        pool_kernel,
        [sds((2, 3, quart // 2, 2 * chans), BF)] * 2,
        in_specs=[smem(), vmem(), vmem()],
        out_specs=[vmem()] * 2,
        scratch_shapes=[pltpu.VMEM((3, half_c, chans), F32)],
    )(me, clip_t, cot_t)
    keep_in = swap(send, "frames", 1)
    block = jnp.concatenate([keep, keep_in], axis=1)
    block = double(block, "frames", chip_bits, 1)
    first, second = block[0][None], block[1][None]

    embed = time_embed(timestep, w_embed.shape[0])
    down, mix, out_mix, direct = call(
        weight_kernel,
        [
            sds((padded, width), BF),
            sds((padded, pieces * SLOT), BF),
            sds((heads * SLOT, chans), BF),
            sds((padded, chans), BF),
        ],
    )(w_down, w_embed, embed[None, :], w_qkv_t, w_out, w_up_t)

    head, tail = call(
        edge_kernel,
        [sds((4, chans, columns), BF)] * 2,
        in_specs=[vmem(), vmem(), pl.BlockSpec(memory_space=pl.ANY)],
        out_specs=[vmem()] * 2,
    )(clip_t, cot_t, keep)
    lo = lax.ppermute(tail, "frames", [(i, i + 1) for i in range(nf - 1)])
    hi = lax.ppermute(head, "frames", [(i + 1, i) for i in range(nf - 1)])
    tap_rows = round_up(3 * chans, devices * 8)
    hidden, base, taps = call(
        fine_kernel,
        [
            sds(clip_t.shape, BF),
            sds(clip_t.shape, F32),
            sds((tap_rows, chans), BF),
        ],
        scratch_shapes=[pltpu.VMEM((chans, 8 * columns), BF)] * 2,
    )(clip_t, cot_t, lo, hi, w_time)
    share = tap_rows // nf
    bits = bit_list(nf)
    taps = taps.reshape([2] * len(bits) + [share, chans])
    for i in range(len(bits)):
        axis = len(bits) - 1 - i
        mine = (f >> i) & 1
        other = lax.dynamic_index_in_dim(taps, 1 - mine, axis, keepdims=False)
        same = lax.dynamic_index_in_dim(taps, mine, axis, keepdims=False)
        got = swap(other, "frames", 1 << i)
        taps = (same.astype(F32) + got.astype(F32)).astype(BF)

    chip_rows = 2 * width // nf
    r1 = width // devices
    p1 = round_up(r1, 8)
    r3 = share // nh
    piece_rows = round_up(2 * p1 + r3, 16)
    sides = cross(first, second, head_bits)
    simple = r1 == p1
    if simple:
        panes = -(-(chip_rows + SLOT - math.gcd(chip_rows, SLOT)) // SLOT)
        shift = chip_rows
        cells = (w_qkv_t, w_up_t, w_out, down)
    else:
        panes = -(-(2 * nh * p1) // SLOT)
        shift = 0
        start = (f >> 1) * chip_rows

        def columns_of(x):
            x = lax.dynamic_slice_in_dim(x, start, chip_rows, axis=1).reshape(x.shape[0], 2 * nh, r1)
            x = jnp.pad(x, ((0, 0), (0, 0), (0, p1 - r1))).reshape(x.shape[0], 2 * nh * p1)
            return jnp.pad(x, ((0, 0), (0, panes * SLOT - x.shape[1])))

        cells = tuple(columns_of(x) for x in (w_qkv_t, w_up_t, w_out, down))

    def pane(x, i):
        return pl.BlockSpec((x.shape[0], SLOT), lambda g, m: (0, ((m[0] >> 1) * shift) // SLOT + i))

    edge = nh // 2

    def side(mirrored, late):
        def index(g, m):
            at = reversed_bits(g, nh) if mirrored else g
            at = jnp.maximum(at - edge, 0) if late else jnp.minimum(at, edge - 1)
            return (at, 0, 0, 0)

        return pl.BlockSpec((1, nf * 3, quart // 2, 2 * chans), index)

    side_specs = [side(False, False), side(False, True), side(True, False), side(True, True)]
    total = 2 * nf * quart
    every = nh * total

    def whole(*shape):
        return pl.BlockSpec(shape, lambda *g: (0,) * len(shape))

    w_time2 = w_time.reshape(3 * chans, chans)
    statics = (w_time2, mix, out_mix, direct, taps)
    window = panes * SLOT
    outs = [sds((6, 2, quart, chans), BF)] * nh + [
        sds((padded, pieces * HD), BF),
        sds((heads * HD, chans), BF),
        sds((nh, piece_rows, padded), BF),
        sds((nh, piece_rows, padded), BF),
    ]
    grid_spec = pltpu.PrefetchScalarGridSpec(
        num_scalar_prefetch=1,
        grid=(nh,),
        in_specs=side_specs + [whole(*x.shape) for x in statics] + [pane(x, i) for x in cells for i in range(panes)],
        out_specs=[whole(*x.shape) for x in outs],
        scratch_shapes=[
            pltpu.VMEM((2, nf * 3, quart // 2, 2 * chans), BF),
            pltpu.VMEM((every, tap_rows), BF),
            pltpu.VMEM((total, chans), F32),
            pltpu.VMEM((every, padded), BF),
            pltpu.VMEM((every, chans), BF),
            pltpu.VMEM((total, pieces * SLOT), BF),
            pltpu.VMEM((total, heads * SLOT), BF),
            pltpu.VMEM((every, heads * SLOT), BF),
            pltpu.VMEM((every, pieces * SLOT), BF),
            pltpu.VMEM((2 * heads, total // 2, total // 2), F32),
            pltpu.VMEM((2 * heads, total // 2, total // 2), F32),
            pltpu.VMEM((2 * heads, total // 2, total // 2), BF),
            pltpu.VMEM((2 * heads, total // 2, total // 2), BF),
            pltpu.VMEM((2 * nf, quart, chans), BF),
            pltpu.VMEM((every, chans), BF),
            pltpu.VMEM((window, padded), F32),
            pltpu.VMEM((window, padded), F32),
            pltpu.VMEM((2 * share, padded), F32),
        ],
    )
    rest = (p1, r3, piece_rows, panes, shift)
    results = call(
        functools.partial(coarse_kernel, coarse_frames=nf, heads_axis=nh, rest=rest),
        outs,
        grid_spec=grid_spec,
    )(me, *sides, *statics, *[x for x in cells for _ in range(panes)])
    local = results[:nh]
    mix_g, att_g, d_keep, d_send = results[nh:]

    d_got = swap(d_send, "frames", 1)
    ordered = call(
        order_kernel,
        [sds((piece_rows, padded), BF)] * nh,
        in_specs=[smem(), vmem(), vmem()],
        out_specs=[vmem()] * nh,
    )(me, d_keep, d_got)
    got = []
    for d in range(1, nh):
        got.append(swap(ordered[d], "heads", d))
    piece = call(sum_kernel, sds((piece_rows, padded), BF))(ordered[0], *got)
    piece = piece.reshape(2, 1, piece_rows // 2, padded)
    piece = double(piece, "frames", chip_bits, 1)
    shares = cross(piece[0][None], piece[1][None], head_bits)
    mates = []
    for x in shares:
        mates.append(swap(x, "frames", 1))

    got = []
    for d in range(1, nh):
        got.append(swap(local[d], "heads", d))
    four = sds((4, 2, quart, chans), BF)
    mine4, send4 = call(
        local_kernel,
        [four, four],
        in_specs=[smem()] + [vmem()] * nh,
        out_specs=[vmem()] * 2,
        scratch_shapes=[pltpu.VMEM(local[0].shape, F32)],
    )(me, local[0], *got)
    other4 = swap(send4, "frames", 1)
    mine4 = mine4.reshape(4, half, chans)
    other4 = other4.reshape(4, half, chans)
    output, grad_clip = call(
        functools.partial(finish_kernel, coarse_frames=nf),
        [sds(clip_t.shape, BF), sds(clip_t.shape, F32)],
        in_specs=[smem()] + [vmem()] * 5,
        out_specs=[vmem()] * 2,
        scratch_shapes=[pltpu.VMEM((4, half_c, chans), F32)],
    )(me, hidden, base, mine4, other4, w_time)

    mix_o = swap(mix_g, "frames", 1)
    att_o = swap(att_g, "frames", 1)
    step = 256
    early = 2
    wide = sds((pieces * HD, width), F32)
    scratch = [pltpu.VMEM((pieces * HD, padded), BF)]
    grad_qkv, grad_out = call(
        functools.partial(split_grad_kernel, late=False),
        [wide, sds((heads * HD, width), F32)],
        grid=(early,),
        in_specs=[
            pl.BlockSpec((padded, step), lambda g: (0, g)),
            whole(*mix_g.shape),
            whole(*mix_g.shape),
            whole(*att_g.shape),
            whole(*att_g.shape),
            whole(*w_up_t.shape),
        ],
        out_specs=[
            pl.BlockSpec((pieces * HD, step), lambda g: (0, g)),
            whole(heads * HD, width),
        ],
        scratch_shapes=scratch,
    )(down, mix_g, mix_o, att_g, att_o, w_up_t)
    grad_qkv = call(
        functools.partial(split_grad_kernel, late=True),
        wide,
        grid=(width // step - early,),
        in_specs=[
            pl.BlockSpec((padded, step), lambda g: (0, g + early)),
            whole(*mix_g.shape),
            whole(*mix_g.shape),
            pl.BlockSpec(memory_space=pl.ANY),
        ],
        out_specs=pl.BlockSpec((pieces * HD, step), lambda g: (0, g + early)),
        scratch_shapes=scratch,
        input_output_aliases={3: 0},
    )(down, mix_g, mix_o, grad_qkv)

    output, grad_clip, grad_qkv, grad_out, mates[3] = lax.optimization_barrier(
        (output, grad_clip, grad_qkv, grad_out, mates[3])
    )
    aligned = r1 % 8 == 0
    layout = (chips, nh, r1, p1, r3)
    outs = [sds((3 * chans // r3, r3, chans), F32)]
    table = (devices, r1, padded)
    scratch = []
    if aligned:
        outs += [sds((chans, width), F32), sds((w_embed.shape[0], width), F32), sds((chans, width), F32)]
        scratch = [pltpu.VMEM(table, F32)] * 2
    else:
        outs += [sds(table, F32)] * 2
    embed_col = embed.astype(F32)[:, None]
    got = call(
        functools.partial(gather_kernel, layout=layout, aligned=aligned),
        outs,
        in_specs=[smem()] + [vmem()] * 9,
        out_specs=[vmem()] * len(outs),
        scratch_shapes=scratch,
    )(me, embed_col, *shares, *mates)
    grad_time = got[0].reshape(w_time.shape)
    if aligned:
        grad_down, grad_embed, grad_up = got[1], got[2], got[3].T
    else:
        down_rows = got[1].reshape(width, padded)
        grad_down = down_rows[:, :chans].T
        grad_embed = embed_col * down_rows[:, chans][None, :]
        grad_up = got[2].reshape(width, padded)[:, :chans]
    return (
        output.transpose(0, 1, 3, 2),
        grad_clip.transpose(0, 1, 3, 2),
        grad_time,
        grad_down,
        grad_embed,
        grad_qkv.T,
        grad_out,
        grad_up,
    )


def solution(mesh):
    return jax.shard_map(
        body,
        mesh=mesh,
        in_specs=(
            P("frames", "heads", None, None),
            P(),
            P(),
            P(),
            P(None, "heads"),
            P("heads", None),
            P(),
            P(),
            P("frames", "heads", None, None),
        ),
        out_specs=(
            P("frames", "heads", None, None),
            P("frames", "heads", None, None),
            P(),
            P(),
            P(),
            P(None, "heads"),
            P("heads", None),
            P(),
        ),
        check_vma=False,
    )
```

```python
import functools
import math

import jax
import jax.numpy as jnp
from jax import lax
from jax.experimental import pallas as pl
from jax.experimental.pallas import tpu as pltpu
from jax.sharding import PartitionSpec as P


HD = 80
SLOT = 128
BF = jnp.bfloat16
F32 = jnp.float32


def nn(a, b):
    return lax.dot_general(a, b, (((1,), (0,)), ((), ())), preferred_element_type=F32)


def nt(a, b):
    return lax.dot_general(a, b, (((1,), (1,)), ((), ())), preferred_element_type=F32)


def tn(a, b):
    return lax.dot_general(a, b, (((0,), (0,)), ((), ())), preferred_element_type=F32)


def round_up(value, step):
    return -(-value // step) * step


def call(kernel, out_shape, **kw):
    return pl.pallas_call(
        kernel,
        out_shape=out_shape,
        compiler_params=pltpu.CompilerParams(vmem_limit_bytes=56 * 1024 * 1024),
        **kw,
    )


def smem():
    return pl.BlockSpec(memory_space=pltpu.SMEM)


def vmem():
    return pl.BlockSpec(memory_space=pltpu.VMEM)


def sds(shape, dtype):
    return jax.ShapeDtypeStruct(shape, dtype)


def bit_list(count):
    bits = []
    while (1 << len(bits)) < count:
        bits.append(1 << len(bits))
    return bits


def reversed_bits(value, count):
    n = len(bit_list(count))
    out = 0
    for i in range(n):
        out = out + (((value >> i) & 1) << (n - 1 - i))
    return out


def swap(x, axis, bit):
    n = lax.axis_size(axis)
    return lax.ppermute(x, axis, [(i, i ^ bit) for i in range(n)])


def time_embed(timestep, width):
    half = width // 2
    freqs = jnp.exp(-math.log(10000.0) * jnp.arange(half, dtype=F32) / half)
    angle = timestep.astype(F32)[0] * freqs
    return jax.nn.silu(jnp.concatenate([jnp.cos(angle), jnp.sin(angle)])).astype(BF)


def pool_matrix(half_c, columns):
    row = lax.broadcasted_iota(jnp.int32, (half_c, columns), 0)
    col = lax.broadcasted_iota(jnp.int32, (half_c, columns), 1)
    return jnp.where((col >> 1) == row, 1.0, 0.0).astype(BF)


def fold(x):
    half = x.shape[0] // 2
    return jnp.concatenate([x[:half], x[half:]], axis=1).astype(BF)


def unfold(x):
    half = x.shape[1] // 2
    x = x.astype(F32)
    return jnp.concatenate([x[:, :half], x[:, half:]], axis=0)


def pool_kernel(me, clip, cot, keep, send, tmp):
    half_c = tmp.shape[1]
    half = half_c // 2
    quart = half // 2
    pool = pool_matrix(half_c, clip.shape[3])
    for t in range(2):
        tmp[t] = (nt(pool, clip[t, 0]) + nt(pool, clip[t, 1])) * 0.25
    tmp[2] = (nt(pool, cot[0, 0]) + nt(pool, cot[0, 1])) + (nt(pool, cot[1, 0]) + nt(pool, cot[1, 1]))
    core = me[0] & 1
    for color in range(2):
        for item in range(3):
            base = pl.multiple_of(core * half + color * quart, quart)
            keep[color, item] = fold(tmp[item, pl.ds(base, quart), :])
            base = pl.multiple_of((1 - core) * half + color * quart, quart)
            send[color, item] = fold(tmp[item, pl.ds(base, quart), :])


def edge_kernel(clip, cot, after, head, tail):
    del after
    for r in range(2):
        head[r] = clip[0, r]
        head[2 + r] = cot[0, r]
        tail[r] = clip[1, r]
        tail[2 + r] = cot[1, r]


def weight_kernel(w_down, w_embed, embed, w_qkv, w_out, w_up, down, mix, out_mix, direct, column):
    wide = embed.shape[1]
    eye = lax.broadcasted_iota(jnp.int32, (wide, wide), 0) == lax.broadcasted_iota(jnp.int32, (wide, wide), 1)
    line = jnp.broadcast_to(embed[...].astype(F32), (SLOT, wide)).astype(BF)
    column[...] = nt(eye.astype(F32).astype(BF), line)
    chans = w_down.shape[0]
    padded = down.shape[0]
    shift = nn(embed[...], w_embed[...])
    high = shift.astype(BF)
    low = (shift - high.astype(F32)).astype(BF)
    down[0:chans, :] = w_down[...]
    row = lax.broadcasted_iota(jnp.int32, (padded - chans, shift.shape[1]), 0)
    tail = jnp.where(row == 0, high.astype(F32), jnp.where(row == 1, low.astype(F32), 0.0))
    down[chans:padded, :] = tail.astype(BF)
    full = down[...]
    pieces = w_qkv.shape[0] // HD
    prod = nt(full, w_qkv[...])
    mix[...] = jnp.zeros(mix.shape, BF)
    for i in range(pieces):
        mix[:, i * SLOT : i * SLOT + HD] = prod[:, i * HD : (i + 1) * HD].astype(BF)
    up = w_up[...]
    small = nt(w_out[...], up)
    out_mix[...] = jnp.zeros(out_mix.shape, BF)
    for i in range(pieces // 3):
        out_mix[i * SLOT : i * SLOT + HD, :] = small[i * HD : (i + 1) * HD, :].astype(BF)
    direct[...] = nt(full, up).astype(BF)


def fine_kernel(me, clip, cot, lo, hi, w_time, hidden, base, keep, send, wide, grad, taps):
    chans = w_time.shape[1]
    columns = clip.shape[3]
    for t in range(4):
        for r in range(2):
            at = slice((2 * t + r) * columns, (2 * t + r + 1) * columns)
            if t in (0, 3):
                halo = lo if t == 0 else hi
                wide[:, at] = halo[r]
                grad[:, at] = halo[2 + r]
            else:
                wide[:, at] = clip[t - 1, r]
                grad[:, at] = cot[t - 1, r]
    cells = 2 * columns
    taps[3 * chans :, :] = jnp.zeros((taps.shape[0] - 3 * chans, chans), F32)
    here = grad[:, cells : 3 * cells]
    for tap in range(3):
        taps[tap * chans : (tap + 1) * chans, :] = nt(wide[:, tap * cells : (tap + 2) * cells], here)
    core = me[0] & 1
    share = keep.shape[1]
    for z in range(keep.shape[0]):
        keep[z] = taps[pl.ds(pl.multiple_of((2 * z + core) * share, share), share), :].astype(BF)
        send[z] = taps[pl.ds(pl.multiple_of((2 * z + 1 - core) * share, share), share), :].astype(BF)
    acc = wide[:, cells : 3 * cells].astype(F32)
    back = here.astype(F32)
    for tap in range(3):
        acc = acc + tn(w_time[tap], wide[:, tap * cells : (tap + 2) * cells])
        back = back + nn(w_time[tap], grad[:, (2 - tap) * cells : (4 - tap) * cells])
    for t in range(2):
        for r in range(2):
            at = slice((2 * t + r) * columns, (2 * t + r + 1) * columns)
            hidden[t, r] = acc[:, at].astype(BF)
            base[t, r] = back[:, at]


def tap_kernel(me, keep, got, *outs):
    for d, out in enumerate(outs):
        at = (me[0] >> 1) ^ d
        out[...] = (keep[at].astype(F32) + got[at].astype(F32)).astype(BF)


def coarse_kernel(
    me, first_a, first_b, second_a, second_b, w_time, mix, out_mix, direct, *refs,
    coarse_frames, heads_axis, rest,
):
    p1, r3, piece, panes, shift = rest
    windows = [refs[i * panes : (i + 1) * panes] for i in range(4)]
    local = refs[4 * panes : 4 * panes + heads_axis]
    grad_mix, grad_att, keep, send = refs[4 * panes + heads_axis : 4 * panes + heads_axis + 4]
    (
    stage, shifted, centre, pooled, upper, qkv, att_grad, att, qkv_grad, score, slope, weight, delta, fields, spread_all,
    rows_down, rows_up, rows_tap,
    ) = refs[4 * panes + heads_axis + 4 :]
    step = pl.program_id(0)
    frame = me[0]
    quart = 2 * stage.shape[2]
    chans = stage.shape[3] // 2
    padded = pooled.shape[1]
    tokens = coarse_frames * quart
    total = 2 * tokens
    chips = coarse_frames // 2
    heads = att.shape[1] // SLOT
    scale = 1.0 / math.sqrt(HD)
    part = 1.0 / heads_axis
    here_rows = pl.ds(pl.multiple_of(step * total, total), total)

    @pl.when(step == 0)
    def _():
        lane = lax.broadcasted_iota(jnp.int32, (pooled.shape[0], padded - chans), 1)
        pooled[:, chans:padded] = jnp.where(lane < 2, 1.0, 0.0).astype(BF)
        shifted[:, 3 * chans :] = jnp.zeros((shifted.shape[0], shifted.shape[1] - 3 * chans), BF)

    def entry(index):
        gap = index ^ frame
        return (reversed_bits(gap >> 1, chips) * 2 + (gap & 1)) * 3

    for color, sources in ((0, (first_a, first_b)), (1, (second_a, second_b))):
        place = step if color == 0 else reversed_bits(step, heads_axis)
        for late in range(2):

            @pl.when((place >= heads_axis // 2) == bool(late))
            def _():
                stage[color] = sources[late][0]

    for color in range(2):
        before = jnp.zeros((quart, chans), F32)
        here = unfold(stage[color, entry(0)])
        for u in range(coarse_frames):
            at = entry(u)
            last = unfold(stage[color, at + 1])
            after = unfold(stage[color, entry(u + 1)]) if u + 1 < coarse_frames else jnp.zeros((quart, chans), F32)
            offset = color * tokens + u * quart
            rows = pl.ds(pl.multiple_of(step * total + offset, quart), quart)
            mid = 0.5 * (here + last)
            shifted[rows, 0:chans] = (0.5 * (before + here)).astype(BF)
            shifted[rows, chans : 2 * chans] = mid.astype(BF)
            shifted[rows, 2 * chans : 3 * chans] = (0.5 * (last + after)).astype(BF)
            centre[offset : offset + quart, :] = mid
            upper[rows, :] = unfold(stage[color, at + 2]).astype(BF)
            before, here = last, after
    pool = (centre[...] + nn(shifted[here_rows, 0 : 3 * chans], w_time[...])).astype(BF)
    pooled[here_rows, 0:chans] = pool
    lines = pooled[here_rows, :]
    ups = upper[here_rows, :]
    qkv[...] = nn(lines, mix[...]).astype(BF)
    att_grad[...] = nt(ups, out_mix[...]).astype(BF)
    row = lax.broadcasted_iota(jnp.int32, (tokens, tokens), 0)
    col = lax.broadcasted_iota(jnp.int32, (tokens, tokens), 1)
    same = (row & (quart - 1)) == (col & (quart - 1))
    cases = [(color, n) for color in range(2) for n in range(heads)]

    def part_of(color, n, which):
        return qkv[color * tokens : (color + 1) * tokens, (3 * n + which) * SLOT : (3 * n + which + 1) * SLOT]

    def grad_of(color, n):
        return att_grad[color * tokens : (color + 1) * tokens, n * SLOT : (n + 1) * SLOT]

    for i, (color, n) in enumerate(cases):
        score[i] = nt(part_of(color, n, 0), part_of(color, n, 1))
        slope[i] = nt(grad_of(color, n), part_of(color, n, 2))
    for i, (color, n) in enumerate(cases):
        scores = jnp.where(same, score[i] * scale, -jnp.inf)
        ex = jnp.exp(scores - jnp.max(scores, axis=1, keepdims=True))
        probs = ex * (1.0 / jnp.sum(ex, axis=1, keepdims=True))
        dw = slope[i]
        inner = jnp.sum(probs * dw, axis=1, keepdims=True)
        weight[i] = probs.astype(BF)
        delta[i] = (probs * (dw - inner) * scale).astype(BF)
    for i, (color, n) in enumerate(cases):
        out = pl.ds(pl.multiple_of(step * total + color * tokens, tokens), tokens)
        att[out, n * SLOT : (n + 1) * SLOT] = nn(weight[i], part_of(color, n, 2)).astype(BF)
        qkv_grad[out, (3 * n) * SLOT : (3 * n + 1) * SLOT] = nn(delta[i], part_of(color, n, 1)).astype(BF)
        qkv_grad[out, (3 * n + 1) * SLOT : (3 * n + 2) * SLOT] = tn(delta[i], part_of(color, n, 0)).astype(BF)
        qkv_grad[out, (3 * n + 2) * SLOT : (3 * n + 3) * SLOT] = tn(weight[i], grad_of(color, n)).astype(BF)
    spread = nt(qkv_grad[here_rows, :], mix[...]) + nt(ups, direct[...]) * part
    spread = spread[:, 0:chans].astype(BF)
    spread_all[here_rows, :] = spread
    fields[...] = spread.reshape(2 * coarse_frames, quart, chans)
    mine = (frame >> 1) * 2
    att_rows, line_rows = [], []
    for color in range(2):
        rows = pl.ds(pl.multiple_of(step * total + color * tokens + mine * quart, 2 * quart), 2 * quart)
        att_rows.append(att[rows, :])
        line_rows.append(pooled[rows, :])
    lifted = nn(jnp.concatenate(att_rows, axis=0), out_mix[...])
    lifted = lifted + nn(jnp.concatenate(line_rows, axis=0), direct[...]) * part
    lifted = lifted.astype(BF).reshape(4, quart, chans)
    for d in range(heads_axis):

        @pl.when(step == d)
        def _():
            for color in range(2):
                for i in range(2):
                    local[d][i, color] = lifted[2 * color + i]
                for i in range(4):
                    at = jnp.clip(mine + i - 1, 0, coarse_frames - 1)
                    local[d][2 + i, color] = fields[color * coarse_frames + at]

    @pl.when(step == heads_axis - 1)
    def _():
        g = tn(pooled[...], qkv_grad[...])
        for i in range(3 * heads):
            grad_mix[:, i * HD : (i + 1) * HD] = g[:, i * SLOT : i * SLOT + HD].astype(BF)
        used = 3 * heads * HD
        grad_mix[:, used:] = jnp.zeros((padded, grad_mix.shape[1] - used), BF)
        a = tn(att[...], upper[...])
        for n in range(heads):
            grad_att[n * HD : (n + 1) * HD, :] = a[n * SLOT : n * SLOT + HD, :].astype(BF)
        s = tn(pooled[...], upper[...]).astype(BF)
        pair = rows_tap.shape[0]
        own = shifted[:, pl.ds(pl.multiple_of((frame >> 1) * pair, pair), pair)]
        rows_tap[:, 0:chans] = tn(own, spread_all[...])
        rows_tap[:, chans:] = jnp.zeros((pair, padded - chans), F32)
        q_win, u_win, o_win, d_win = [jnp.concatenate([ref[...] for ref in group], axis=1) for group in windows]
        down_t = nn(grad_mix[:, 0:used], q_win) + nn(s, u_win) * part
        rows_down[...] = down_t.astype(BF).T.astype(F32)
        up_t = tn(grad_att[...], o_win) + tn(s, d_win) * part
        rows_up[:, 0:chans] = up_t.astype(BF).T.astype(F32)
        rows_up[:, chans:] = jnp.zeros((rows_up.shape[0], padded - chans), F32)
        core = frame & 1
        base = ((frame >> 1) * shift) & (SLOT - 1)
        extra = jnp.zeros((piece - 2 * p1 - r3, padded), F32)
        for dest, which in ((keep, core), (send, 1 - core)):
            for j in range(heads_axis):
                at = pl.ds(pl.multiple_of(base + (which * heads_axis + j) * p1, 8), p1)
                tap = rows_tap[pl.ds(pl.multiple_of((which * heads_axis + j) * r3, r3), r3), :]
                parts = [rows_down[at, :], rows_up[at, :], tap]
                if piece > 2 * p1 + r3:
                    parts.append(extra)
                dest[j] = jnp.concatenate(parts, axis=0).astype(BF)


def order_kernel(me, keep, got, *refs, at, taps):
    parts, outs = refs[:taps], refs[taps:]
    head = me[1]
    rows = parts[0].shape[0] // len(outs)
    chans = parts[0].shape[1]
    for d, out in enumerate(outs):
        value = keep[head ^ d].astype(F32) + got[head ^ d].astype(F32)
        here = pl.ds(pl.multiple_of((head ^ d) * rows, rows), rows)
        tap = value[at : at + rows, 0:chans]
        for ref in parts:
            tap = tap + ref[here, :].astype(F32)
        out[...] = value.astype(BF)
        out[at : at + rows, 0:chans] = tap.astype(BF)


def sum_kernel(*refs):
    acc = refs[0][...].astype(F32)
    for ref in refs[1:-1]:
        acc = acc + ref[...].astype(F32)
    refs[-1][...] = acc.astype(BF)


def local_kernel(me, *refs):
    parts, (mine, send, acc) = refs[:-3], refs[-3:]
    core = me[0] & 1
    for i in range(acc.shape[0]):
        value = parts[0][i].astype(F32)
        for ref in parts[1:]:
            value = value + ref[i].astype(F32)
        acc[i] = value
    for dest, which in ((mine, core), (send, 1 - core)):
        dest[0] = acc[which].astype(BF)
        for i in range(3):
            dest[1 + i] = acc[2 + which + i].astype(BF)


def split_grad_kernel(down, mix_a, mix_b, *refs, late):
    if late:
        _, qkv_out, flipped = refs
    else:
        att_a, att_b, w_up, qkv_out, att_out, flipped = refs

    @pl.when(pl.program_id(0) == 0)
    def _():
        flipped[...] = (mix_a[...].astype(F32) + mix_b[...].astype(F32)).astype(BF).T[0 : flipped.shape[0]]
        if not late:
            att_out[...] = nn((att_a[...].astype(F32) + att_b[...].astype(F32)).astype(BF), w_up[...])

    qkv_out[...] = nn(flipped[...], down[...])


def finish_kernel(me, hidden, base, own, other, w_time, output, grad_clip, rows, *, coarse_frames):
    frame = me[0]
    core = frame & 1
    half = own.shape[1]
    columns = hidden.shape[3]
    for i in range(4):
        rows[i, pl.ds(pl.multiple_of(core * half, half), half), :] = own[i].astype(F32)
        rows[i, pl.ds(pl.multiple_of((1 - core) * half, half), half), :] = other[i].astype(F32)
    lift = pool_matrix(2 * half, columns)
    fine = tn(rows[0].astype(BF), lift)
    for t in range(2):
        for r in range(2):
            output[t, r] = (hidden[t, r].astype(F32) + fine).astype(BF)
    before = (rows[1] * jnp.where(frame == 0, 0.0, 1.0)).astype(BF)
    here = rows[2].astype(BF)
    after = (rows[3] * jnp.where(frame == coarse_frames - 1, 0.0, 1.0)).astype(BF)
    mid = rows[2] + nt(here, w_time[1])
    even = mid + nt(here, w_time[0]) + nt(before, w_time[2])
    odd = mid + nt(after, w_time[0]) + nt(here, w_time[2])
    for t, value in ((0, even), (1, odd)):
        high = value.astype(BF)
        low = (value - high.astype(F32)).astype(BF)
        add = (tn(high, lift) + tn(low, lift)) * 0.125
        for r in range(2):
            grad_clip[t, r] = base[t, r] + add


def gather_kernel(me, embed, *refs, layout, aligned):
    pieces = refs[:8]
    time_out, down_rows, up_rows = refs[8], refs[-2], refs[-1]
    frame, head = me[0], me[1]
    chips, heads_axis, r1, p1, r3 = layout
    chans = time_out.shape[2]
    devices = 2 * chips * heads_axis
    for core in range(2):
        for idx in range(chips * heads_axis):
            hi, zi = idx // chips, idx % chips
            colors = []
            for color in range(2):
                off = hi if color == 0 else reversed_bits(hi, heads_axis)
                edge = heads_axis // 2
                src = pieces[4 * core + 2 * color + off // edge]
                colors.append(src[off % edge, zi].astype(F32))
            value = jnp.concatenate(colors, axis=0)
            owner = (frame ^ (reversed_bits(zi, chips) * 2 + core)) * heads_axis + (head ^ hi)
            down_rows[owner] = value[0:r1]
            up_rows[owner] = value[p1 : p1 + r1]

            @pl.when(owner < time_out.shape[0])
            def _():
                time_out[owner] = value[2 * p1 : 2 * p1 + r3, 0:chans]

    if aligned:
        down_out, embed_out, up_out = refs[9], refs[10], refs[11]
        lanes = down_rows.shape[2]
        eye = (lax.broadcasted_iota(jnp.int32, (lanes, lanes), 0) == lax.broadcasted_iota(jnp.int32, (lanes, lanes), 1))
        eye = eye.astype(F32).astype(BF)
        flipped = nt(eye, down_rows[...].reshape(devices * r1, lanes).astype(BF))
        down_out[...] = flipped[0:chans]
        embed_out[...] = embed[:, 0:1] * flipped[chans : chans + 1]
        up_out[...] = nt(eye, up_rows[...].reshape(devices * r1, lanes).astype(BF))[0:chans]


def double(x, axis, bits, dim):
    for bit in bits:
        got = swap(x, axis, bit)
        x = jnp.concatenate([x, got], axis=dim)
    return x


def cross(first, second, bits):
    for i, (a, b) in enumerate(zip(bits, reversed(bits))):
        first_in = swap(first, "heads", a)
        second_in = swap(second, "heads", b)
        if i + 1 < len(bits):
            first = jnp.concatenate([first, first_in], axis=0)
            second = jnp.concatenate([second, second_in], axis=0)
    return first, first_in, second, second_in


def body(clip, w_time, w_down, w_embed, w_qkv, w_out, w_up, timestep, cotangent):
    nf = lax.axis_size("frames")
    nh = lax.axis_size("heads")
    f = lax.axis_index("frames")
    h = lax.axis_index("heads")
    me = jnp.stack([f, h]).astype(jnp.int32)
    _, _, columns, chans = clip.shape
    width = w_down.shape[1]
    half_c = columns // 2
    half = half_c // 2
    quart = half // 2
    chips = nf // 2
    padded = round_up(chans + 2, 128)
    pieces = w_qkv.shape[1] // HD
    heads = pieces // 3
    chip_bits = [2 * b for b in reversed(bit_list(chips))]
    head_bits = bit_list(nh)
    devices = nf * nh

    clip_t = clip.transpose(0, 1, 3, 2)
    cot_t = cotangent.transpose(0, 1, 3, 2)
    w_qkv_t = w_qkv.T
    w_up_t = w_up.T

    keep, send = call(
        pool_kernel,
        [sds((2, 3, quart // 2, 2 * chans), BF)] * 2,
        in_specs=[smem(), vmem(), vmem()],
        out_specs=[vmem()] * 2,
        scratch_shapes=[pltpu.VMEM((3, half_c, chans), F32)],
    )(f.astype(jnp.int32).reshape(1), clip_t, cot_t)
    keep_in = swap(send, "frames", 1)
    block = jnp.concatenate([keep, keep_in], axis=1)
    block = double(block, "frames", chip_bits, 1)
    first, second = block[0][None], block[1][None]

    embed = time_embed(timestep, w_embed.shape[0])
    down, mix, out_mix, direct, embed_col = call(
        weight_kernel,
        [
            sds((padded, width), BF),
            sds((padded, pieces * SLOT), BF),
            sds((heads * SLOT, chans), BF),
            sds((padded, chans), BF),
            sds((embed.shape[0], SLOT), F32),
        ],
    )(w_down, w_embed, embed[None, :], w_qkv_t, w_out, w_up_t)

    head, tail = call(
        edge_kernel,
        [sds((4, chans, columns), BF)] * 2,
        in_specs=[vmem(), vmem(), pl.BlockSpec(memory_space=pl.ANY)],
        out_specs=[vmem()] * 2,
    )(clip_t, cot_t, keep)
    lo = lax.ppermute(tail, "frames", [(i, i + 1) for i in range(nf - 1)])
    hi = lax.ppermute(head, "frames", [(i + 1, i) for i in range(nf - 1)])
    tap_rows = round_up(3 * chans, devices * 8)
    hidden, base, tap_keep, tap_send = call(
        fine_kernel,
        [
            sds(clip_t.shape, BF),
            sds(clip_t.shape, F32),
            sds((chips, tap_rows // nf, chans), BF),
            sds((chips, tap_rows // nf, chans), BF),
        ],
        in_specs=[smem()] + [vmem()] * 5,
        out_specs=[vmem()] * 4,
        scratch_shapes=[pltpu.VMEM((chans, 8 * columns), BF)] * 2 + [pltpu.VMEM((tap_rows, chans), F32)],
    )(me, clip_t, cot_t, lo, hi, w_time)
    share = tap_rows // nf
    tap_got = swap(tap_send, "frames", 1)
    tap_parts = call(
        tap_kernel,
        [sds((share, chans), BF)] * chips,
        in_specs=[smem(), vmem(), vmem()],
        out_specs=[vmem()] * chips,
    )(me, tap_keep, tap_got)
    taps = [tap_parts[0]]
    for d in range(1, chips):
        taps.append(swap(tap_parts[d], "frames", 2 * d))

    chip_rows = 2 * width // nf
    r1 = width // devices
    p1 = round_up(r1, 8)
    r3 = share // nh
    piece_rows = round_up(2 * p1 + r3, 16)
    sides = cross(first, second, head_bits)
    simple = r1 == p1
    if simple:
        panes = -(-(chip_rows + SLOT - math.gcd(chip_rows, SLOT)) // SLOT)
        shift = chip_rows
        cells = (w_qkv_t, w_up_t, w_out, down)
    else:
        panes = -(-(2 * nh * p1) // SLOT)
        shift = 0
        start = (f >> 1) * chip_rows

        def columns_of(x):
            x = lax.dynamic_slice_in_dim(x, start, chip_rows, axis=1).reshape(x.shape[0], 2 * nh, r1)
            x = jnp.pad(x, ((0, 0), (0, 0), (0, p1 - r1))).reshape(x.shape[0], 2 * nh * p1)
            return jnp.pad(x, ((0, 0), (0, panes * SLOT - x.shape[1])))

        cells = tuple(columns_of(x) for x in (w_qkv_t, w_up_t, w_out, down))

    def pane(x, i):
        return pl.BlockSpec((x.shape[0], SLOT), lambda g, m: (0, ((m[0] >> 1) * shift) // SLOT + i))

    edge = nh // 2

    def side(mirrored, late):
        def index(g, m):
            at = reversed_bits(g, nh) if mirrored else g
            at = jnp.maximum(at - edge, 0) if late else jnp.minimum(at, edge - 1)
            return (at, 0, 0, 0)

        return pl.BlockSpec((1, nf * 3, quart // 2, 2 * chans), index)

    side_specs = [side(False, False), side(False, True), side(True, False), side(True, True)]
    total = 2 * nf * quart
    every = nh * total

    def whole(*shape):
        return pl.BlockSpec(shape, lambda *g: (0,) * len(shape))

    w_time2 = w_time.reshape(3 * chans, chans)
    statics = (w_time2, mix, out_mix, direct)
    window = panes * SLOT
    outs = [sds((6, 2, quart, chans), BF)] * nh + [
        sds((padded, round_up(pieces * HD, SLOT)), BF),
        sds((heads * HD, chans), BF),
        sds((nh, piece_rows, padded), BF),
        sds((nh, piece_rows, padded), BF),
    ]
    grid_spec = pltpu.PrefetchScalarGridSpec(
        num_scalar_prefetch=1,
        grid=(nh,),
        in_specs=side_specs + [whole(*x.shape) for x in statics] + [pane(x, i) for x in cells for i in range(panes)],
        out_specs=[whole(*x.shape) for x in outs],
        scratch_shapes=[
            pltpu.VMEM((2, nf * 3, quart // 2, 2 * chans), BF),
            pltpu.VMEM((every, tap_rows), BF),
            pltpu.VMEM((total, chans), F32),
            pltpu.VMEM((every, padded), BF),
            pltpu.VMEM((every, chans), BF),
            pltpu.VMEM((total, pieces * SLOT), BF),
            pltpu.VMEM((total, heads * SLOT), BF),
            pltpu.VMEM((every, heads * SLOT), BF),
            pltpu.VMEM((every, pieces * SLOT), BF),
            pltpu.VMEM((2 * heads, total // 2, total // 2), F32),
            pltpu.VMEM((2 * heads, total // 2, total // 2), F32),
            pltpu.VMEM((2 * heads, total // 2, total // 2), BF),
            pltpu.VMEM((2 * heads, total // 2, total // 2), BF),
            pltpu.VMEM((2 * nf, quart, chans), BF),
            pltpu.VMEM((every, chans), BF),
            pltpu.VMEM((window, padded), F32),
            pltpu.VMEM((window, padded), F32),
            pltpu.VMEM((2 * share, padded), F32),
        ],
    )
    rest = (p1, r3, piece_rows, panes, shift)
    results = call(
        functools.partial(coarse_kernel, coarse_frames=nf, heads_axis=nh, rest=rest),
        outs,
        grid_spec=grid_spec,
    )(me, *sides, *statics, *[x for x in cells for _ in range(panes)])
    local = results[:nh]
    mix_g, att_g, d_keep, d_send = results[nh:]

    d_got = swap(d_send, "frames", 1)
    ordered = call(
        functools.partial(order_kernel, at=2 * p1, taps=chips),
        [sds((piece_rows, padded), BF)] * nh,
        in_specs=[smem()] + [vmem()] * (2 + chips),
        out_specs=[vmem()] * nh,
    )(me, d_keep, d_got, *taps)
    got = []
    for d in range(1, nh):
        got.append(swap(ordered[d], "heads", d))
    piece = call(sum_kernel, sds((piece_rows, padded), BF))(ordered[0], *got)
    piece = piece.reshape(2, 1, piece_rows // 2, padded)
    piece = double(piece, "frames", chip_bits, 1)
    shares = cross(piece[0][None], piece[1][None], head_bits)
    mates = []
    for x in shares:
        mates.append(swap(x, "frames", 1))

    got = []
    for d in range(1, nh):
        got.append(swap(local[d], "heads", d))
    four = sds((4, 2, quart, chans), BF)
    mine4, send4 = call(
        local_kernel,
        [four, four],
        in_specs=[smem()] + [vmem()] * nh,
        out_specs=[vmem()] * 2,
        scratch_shapes=[pltpu.VMEM(local[0].shape, F32)],
    )(me, local[0], *got)
    other4 = swap(send4, "frames", 1)
    mine4 = mine4.reshape(4, half, chans)
    other4 = other4.reshape(4, half, chans)
    output, grad_clip = call(
        functools.partial(finish_kernel, coarse_frames=nf),
        [sds(clip_t.shape, BF), sds(clip_t.shape, F32)],
        in_specs=[smem()] + [vmem()] * 5,
        out_specs=[vmem()] * 2,
        scratch_shapes=[pltpu.VMEM((4, half_c, chans), F32)],
    )(me, hidden, base, mine4, other4, w_time)

    mix_o = swap(mix_g, "frames", 1)
    att_o = swap(att_g, "frames", 1)
    step = 256
    early = 2
    wide = sds((pieces * HD, width), F32)
    scratch = [pltpu.VMEM((pieces * HD, padded), BF)]
    grad_qkv, grad_out = call(
        functools.partial(split_grad_kernel, late=False),
        [wide, sds((heads * HD, width), F32)],
        grid=(early,),
        in_specs=[
            pl.BlockSpec((padded, step), lambda g: (0, g)),
            whole(*mix_g.shape),
            whole(*mix_g.shape),
            whole(*att_g.shape),
            whole(*att_g.shape),
            whole(*w_up_t.shape),
        ],
        out_specs=[
            pl.BlockSpec((pieces * HD, step), lambda g: (0, g)),
            whole(heads * HD, width),
        ],
        scratch_shapes=scratch,
    )(down, mix_g, mix_o, att_g, att_o, w_up_t)
    grad_qkv = call(
        functools.partial(split_grad_kernel, late=True),
        wide,
        grid=(width // step - early,),
        in_specs=[
            pl.BlockSpec((padded, step), lambda g: (0, g + early)),
            whole(*mix_g.shape),
            whole(*mix_g.shape),
            pl.BlockSpec(memory_space=pl.ANY),
        ],
        out_specs=pl.BlockSpec((pieces * HD, step), lambda g: (0, g + early)),
        scratch_shapes=scratch,
        input_output_aliases={3: 0},
    )(down, mix_g, mix_o, grad_qkv)

    output, grad_clip, grad_qkv, grad_out, mates[3] = lax.optimization_barrier(
        (output, grad_clip, grad_qkv, grad_out, mates[3])
    )
    aligned = r1 % 8 == 0
    layout = (chips, nh, r1, p1, r3)
    outs = [sds((3 * chans // r3, r3, chans), F32)]
    table = (devices, r1, padded)
    scratch = []
    if aligned:
        outs += [sds((chans, width), F32), sds((w_embed.shape[0], width), F32), sds((chans, width), F32)]
        scratch = [pltpu.VMEM(table, F32)] * 2
    else:
        outs += [sds(table, F32)] * 2
    got = call(
        functools.partial(gather_kernel, layout=layout, aligned=aligned),
        outs,
        in_specs=[smem()] + [vmem()] * 9,
        out_specs=[vmem()] * len(outs),
        scratch_shapes=scratch,
    )(me, embed_col, *shares, *mates)
    grad_time = got[0].reshape(w_time.shape)
    if aligned:
        grad_down, grad_embed, grad_up = got[1], got[2], got[3].T
    else:
        down_rows = got[1].reshape(width, padded)
        grad_down = down_rows[:, :chans].T
        grad_embed = embed_col[:, 0:1] * down_rows[:, chans][None, :]
        grad_up = got[2].reshape(width, padded)[:, :chans]
    return (
        output.transpose(0, 1, 3, 2),
        grad_clip.transpose(0, 1, 3, 2),
        grad_time,
        grad_down,
        grad_embed,
        grad_qkv.T,
        grad_out,
        grad_up,
    )


def solution(mesh):
    return jax.shard_map(
        body,
        mesh=mesh,
        in_specs=(
            P("frames", "heads", None, None),
            P(),
            P(),
            P(),
            P(None, "heads"),
            P("heads", None),
            P(),
            P(),
            P("frames", "heads", None, None),
        ),
        out_specs=(
            P("frames", "heads", None, None),
            P("frames", "heads", None, None),
            P(),
            P(),
            P(),
            P(None, "heads"),
            P("heads", None),
            P(),
        ),
        check_vma=False,
    )
```

```python
import functools
import math

import jax
import jax.numpy as jnp
from jax import lax
from jax.experimental import pallas as pl
from jax.experimental.pallas import tpu as pltpu
from jax.sharding import PartitionSpec as P


HD = 80
SLOT = 128
BF = jnp.bfloat16
F32 = jnp.float32


def nn(a, b):
    return lax.dot_general(a, b, (((1,), (0,)), ((), ())), preferred_element_type=F32)


def nt(a, b):
    return lax.dot_general(a, b, (((1,), (1,)), ((), ())), preferred_element_type=F32)


def tn(a, b):
    return lax.dot_general(a, b, (((0,), (0,)), ((), ())), preferred_element_type=F32)


def round_up(value, step):
    return -(-value // step) * step


def call(kernel, out_shape, **kw):
    return pl.pallas_call(
        kernel,
        out_shape=out_shape,
        compiler_params=pltpu.CompilerParams(vmem_limit_bytes=56 * 1024 * 1024),
        **kw,
    )


def smem():
    return pl.BlockSpec(memory_space=pltpu.SMEM)


def vmem():
    return pl.BlockSpec(memory_space=pltpu.VMEM)


def sds(shape, dtype):
    return jax.ShapeDtypeStruct(shape, dtype)


def bit_list(count):
    bits = []
    while (1 << len(bits)) < count:
        bits.append(1 << len(bits))
    return bits


def reversed_bits(value, count):
    n = len(bit_list(count))
    out = 0
    for i in range(n):
        out = out + (((value >> i) & 1) << (n - 1 - i))
    return out


def swap(x, axis, bit):
    n = lax.axis_size(axis)
    return lax.ppermute(x, axis, [(i, i ^ bit) for i in range(n)])


def time_embed(timestep, width):
    half = width // 2
    freqs = jnp.exp(-math.log(10000.0) * jnp.arange(half, dtype=F32) / half)
    angle = timestep.astype(F32)[0] * freqs
    return jax.nn.silu(jnp.concatenate([jnp.cos(angle), jnp.sin(angle)])).astype(BF)


def pool_matrix(half_c, columns):
    row = lax.broadcasted_iota(jnp.int32, (half_c, columns), 0)
    col = lax.broadcasted_iota(jnp.int32, (half_c, columns), 1)
    return jnp.where((col >> 1) == row, 1.0, 0.0).astype(BF)


def fold(x):
    half = x.shape[0] // 2
    return jnp.concatenate([x[:half], x[half:]], axis=1).astype(BF)


def unfold(x):
    half = x.shape[1] // 2
    x = x.astype(F32)
    return jnp.concatenate([x[:, :half], x[:, half:]], axis=0)


def pool_kernel(me, clip, cot, keep, send, tmp):
    half_c = tmp.shape[1]
    half = half_c // 2
    quart = half // 2
    pool = pool_matrix(half_c, clip.shape[3])
    for t in range(2):
        tmp[t] = (nt(pool, clip[t, 0]) + nt(pool, clip[t, 1])) * 0.25
    tmp[2] = (nt(pool, cot[0, 0]) + nt(pool, cot[0, 1])) + (nt(pool, cot[1, 0]) + nt(pool, cot[1, 1]))
    core = me[0] & 1
    for color in range(2):
        for item in range(3):
            base = pl.multiple_of(core * half + color * quart, quart)
            keep[color, item] = fold(tmp[item, pl.ds(base, quart), :])
            base = pl.multiple_of((1 - core) * half + color * quart, quart)
            send[color, item] = fold(tmp[item, pl.ds(base, quart), :])


def edge_kernel(clip, cot, after, head, tail):
    del after
    for r in range(2):
        head[r] = clip[0, r]
        head[2 + r] = cot[0, r]
        tail[r] = clip[1, r]
        tail[2 + r] = cot[1, r]


def weight_kernel(w_down, w_embed, embed, w_qkv, w_out, w_up, down, mix, out_mix, direct, column):
    wide = embed.shape[1]
    eye = lax.broadcasted_iota(jnp.int32, (wide, wide), 0) == lax.broadcasted_iota(jnp.int32, (wide, wide), 1)
    line = jnp.broadcast_to(embed[...].astype(F32), (SLOT, wide)).astype(BF)
    column[...] = nt(eye.astype(F32).astype(BF), line)
    chans = w_down.shape[0]
    padded = down.shape[0]
    shift = nn(embed[...], w_embed[...])
    high = shift.astype(BF)
    low = (shift - high.astype(F32)).astype(BF)
    down[0:chans, :] = w_down[...]
    row = lax.broadcasted_iota(jnp.int32, (padded - chans, shift.shape[1]), 0)
    tail = jnp.where(row == 0, high.astype(F32), jnp.where(row == 1, low.astype(F32), 0.0))
    down[chans:padded, :] = tail.astype(BF)
    full = down[...]
    pieces = w_qkv.shape[0] // HD
    prod = nt(full, w_qkv[...])
    mix[...] = jnp.zeros(mix.shape, BF)
    for i in range(pieces):
        mix[:, i * SLOT : i * SLOT + HD] = prod[:, i * HD : (i + 1) * HD].astype(BF)
    up = w_up[...]
    small = nt(w_out[...], up)
    out_mix[...] = jnp.zeros(out_mix.shape, BF)
    for i in range(pieces // 3):
        out_mix[i * SLOT : i * SLOT + HD, :] = small[i * HD : (i + 1) * HD, :].astype(BF)
    direct[...] = nt(full, up).astype(BF)


def fine_kernel(me, clip, cot, lo, hi, w_time, hidden, base, keep, send, wide, grad, taps):
    chans = w_time.shape[1]
    columns = clip.shape[3]
    for t in range(4):
        for r in range(2):
            at = slice((2 * t + r) * columns, (2 * t + r + 1) * columns)
            if t in (0, 3):
                halo = lo if t == 0 else hi
                wide[:, at] = halo[r]
                grad[:, at] = halo[2 + r]
            else:
                wide[:, at] = clip[t - 1, r]
                grad[:, at] = cot[t - 1, r]
    cells = 2 * columns
    taps[3 * chans :, :] = jnp.zeros((taps.shape[0] - 3 * chans, chans), F32)
    here = grad[:, cells : 3 * cells]
    for tap in range(3):
        taps[tap * chans : (tap + 1) * chans, :] = nt(wide[:, tap * cells : (tap + 2) * cells], here)
    core = me[0] & 1
    share = keep.shape[1]
    for z in range(keep.shape[0]):
        keep[z] = taps[pl.ds(pl.multiple_of((2 * z + core) * share, share), share), :].astype(BF)
        send[z] = taps[pl.ds(pl.multiple_of((2 * z + 1 - core) * share, share), share), :].astype(BF)
    acc = wide[:, cells : 3 * cells].astype(F32)
    back = here.astype(F32)
    for tap in range(3):
        acc = acc + tn(w_time[tap], wide[:, tap * cells : (tap + 2) * cells])
        back = back + nn(w_time[tap], grad[:, (2 - tap) * cells : (4 - tap) * cells])
    for t in range(2):
        for r in range(2):
            at = slice((2 * t + r) * columns, (2 * t + r + 1) * columns)
            hidden[t, r] = acc[:, at].astype(BF)
            base[t, r] = back[:, at]


def tap_kernel(me, keep, got, *outs):
    for d, out in enumerate(outs):
        at = (me[0] >> 1) ^ d
        out[...] = (keep[at].astype(F32) + got[at].astype(F32)).astype(BF)


def coarse_kernel(
    me, first_a, first_b, second_a, second_b, w_time, mix, out_mix, direct, *refs,
    coarse_frames, heads_axis, rest,
):
    p1, r3, piece, panes, shift = rest
    windows = [refs[i * panes : (i + 1) * panes] for i in range(4)]
    local = refs[4 * panes : 4 * panes + heads_axis]
    grad_mix, grad_att, keep, send = refs[4 * panes + heads_axis : 4 * panes + heads_axis + 4]
    (
    stage, shifted, centre, pooled, upper, qkv, att_grad, att, qkv_grad, score, slope, weight, delta, fields, spread_all,
    rows_down, rows_up, rows_tap,
    ) = refs[4 * panes + heads_axis + 4 :]
    step = pl.program_id(0)
    frame = me[0]
    quart = 2 * stage.shape[2]
    chans = stage.shape[3] // 2
    padded = pooled.shape[1]
    tokens = coarse_frames * quart
    total = 2 * tokens
    chips = coarse_frames // 2
    heads = att.shape[1] // SLOT
    scale = 1.0 / math.sqrt(HD)
    part = 1.0 / heads_axis
    here_rows = pl.ds(pl.multiple_of(step * total, total), total)

    @pl.when(step == 0)
    def _():
        lane = lax.broadcasted_iota(jnp.int32, (pooled.shape[0], padded - chans), 1)
        pooled[:, chans:padded] = jnp.where(lane < 2, 1.0, 0.0).astype(BF)
        shifted[:, 3 * chans :] = jnp.zeros((shifted.shape[0], shifted.shape[1] - 3 * chans), BF)

    def entry(index):
        gap = index ^ frame
        return (reversed_bits(gap >> 1, chips) * 2 + (gap & 1)) * 3

    for color, sources in ((0, (first_a, first_b)), (1, (second_a, second_b))):
        place = step if color == 0 else reversed_bits(step, heads_axis)
        for late in range(2):

            @pl.when((place >= heads_axis // 2) == bool(late))
            def _():
                stage[color] = sources[late][0]

    for color in range(2):
        before = jnp.zeros((quart, chans), F32)
        here = unfold(stage[color, entry(0)])
        for u in range(coarse_frames):
            at = entry(u)
            last = unfold(stage[color, at + 1])
            after = unfold(stage[color, entry(u + 1)]) if u + 1 < coarse_frames else jnp.zeros((quart, chans), F32)
            offset = color * tokens + u * quart
            rows = pl.ds(pl.multiple_of(step * total + offset, quart), quart)
            mid = 0.5 * (here + last)
            shifted[rows, 0:chans] = (0.5 * (before + here)).astype(BF)
            shifted[rows, chans : 2 * chans] = mid.astype(BF)
            shifted[rows, 2 * chans : 3 * chans] = (0.5 * (last + after)).astype(BF)
            centre[offset : offset + quart, :] = mid
            upper[rows, :] = unfold(stage[color, at + 2]).astype(BF)
            before, here = last, after
    pool = (centre[...] + nn(shifted[here_rows, 0 : 3 * chans], w_time[...])).astype(BF)
    pooled[here_rows, 0:chans] = pool
    lines = pooled[here_rows, :]
    ups = upper[here_rows, :]
    qkv[...] = nn(lines, mix[...]).astype(BF)
    att_grad[...] = nt(ups, out_mix[...]).astype(BF)
    row = lax.broadcasted_iota(jnp.int32, (tokens, tokens), 0)
    col = lax.broadcasted_iota(jnp.int32, (tokens, tokens), 1)
    same = (row & (quart - 1)) == (col & (quart - 1))
    cases = [(color, n) for color in range(2) for n in range(heads)]

    def part_of(color, n, which):
        return qkv[color * tokens : (color + 1) * tokens, (3 * n + which) * SLOT : (3 * n + which + 1) * SLOT]

    def grad_of(color, n):
        return att_grad[color * tokens : (color + 1) * tokens, n * SLOT : (n + 1) * SLOT]

    for i, (color, n) in enumerate(cases):
        score[i] = nt(part_of(color, n, 0), part_of(color, n, 1))
        slope[i] = nt(grad_of(color, n), part_of(color, n, 2))
    for i, (color, n) in enumerate(cases):
        scores = jnp.where(same, score[i] * scale, -jnp.inf)
        ex = jnp.exp(scores - jnp.max(scores, axis=1, keepdims=True))
        probs = ex * (1.0 / jnp.sum(ex, axis=1, keepdims=True))
        dw = slope[i]
        inner = jnp.sum(probs * dw, axis=1, keepdims=True)
        weight[i] = probs.astype(BF)
        delta[i] = (probs * (dw - inner) * scale).astype(BF)
    for i, (color, n) in enumerate(cases):
        out = pl.ds(pl.multiple_of(step * total + color * tokens, tokens), tokens)
        att[out, n * SLOT : (n + 1) * SLOT] = nn(weight[i], part_of(color, n, 2)).astype(BF)
        qkv_grad[out, (3 * n) * SLOT : (3 * n + 1) * SLOT] = nn(delta[i], part_of(color, n, 1)).astype(BF)
        qkv_grad[out, (3 * n + 1) * SLOT : (3 * n + 2) * SLOT] = tn(delta[i], part_of(color, n, 0)).astype(BF)
        qkv_grad[out, (3 * n + 2) * SLOT : (3 * n + 3) * SLOT] = tn(weight[i], grad_of(color, n)).astype(BF)
    spread = nt(qkv_grad[here_rows, :], mix[...]) + nt(ups, direct[...]) * part
    spread = spread[:, 0:chans].astype(BF)
    spread_all[here_rows, :] = spread
    fields[...] = spread.reshape(2 * coarse_frames, quart, chans)
    mine = (frame >> 1) * 2
    att_rows, line_rows = [], []
    for color in range(2):
        rows = pl.ds(pl.multiple_of(step * total + color * tokens + mine * quart, 2 * quart), 2 * quart)
        att_rows.append(att[rows, :])
        line_rows.append(pooled[rows, :])
    lifted = nn(jnp.concatenate(att_rows, axis=0), out_mix[...])
    lifted = lifted + nn(jnp.concatenate(line_rows, axis=0), direct[...]) * part
    lifted = lifted.astype(BF).reshape(4, quart, chans)
    for d in range(heads_axis):

        @pl.when(step == d)
        def _():
            for color in range(2):
                for i in range(2):
                    local[d][i, color] = lifted[2 * color + i]
                for i in range(4):
                    at = jnp.clip(mine + i - 1, 0, coarse_frames - 1)
                    local[d][2 + i, color] = fields[color * coarse_frames + at]

    @pl.when(step == heads_axis - 1)
    def _():
        g = tn(pooled[...], qkv_grad[...])
        for i in range(3 * heads):
            grad_mix[:, i * HD : (i + 1) * HD] = g[:, i * SLOT : i * SLOT + HD].astype(BF)
        used = 3 * heads * HD
        grad_mix[:, used:] = jnp.zeros((padded, grad_mix.shape[1] - used), BF)
        a = tn(att[...], upper[...])
        for n in range(heads):
            grad_att[n * HD : (n + 1) * HD, :] = a[n * SLOT : n * SLOT + HD, :].astype(BF)
        s = tn(pooled[...], upper[...]).astype(BF)
        pair = rows_tap.shape[0]
        own = shifted[:, pl.ds(pl.multiple_of((frame >> 1) * pair, pair), pair)]
        rows_tap[:, 0:chans] = tn(own, spread_all[...])
        rows_tap[:, chans:] = jnp.zeros((pair, padded - chans), F32)
        q_win, u_win, o_win, d_win = [jnp.concatenate([ref[...] for ref in group], axis=1) for group in windows]
        down_t = nn(grad_mix[:, 0:used], q_win) + nn(s, u_win) * part
        rows_down[...] = down_t.astype(BF).T.astype(F32)
        up_t = tn(grad_att[...], o_win) + tn(s, d_win) * part
        rows_up[:, 0:chans] = up_t.astype(BF).T.astype(F32)
        rows_up[:, chans:] = jnp.zeros((rows_up.shape[0], padded - chans), F32)
        core = frame & 1
        base = ((frame >> 1) * shift) & (SLOT - 1)
        extra = jnp.zeros((piece - 2 * p1 - r3, padded), F32)
        for dest, which in ((keep, core), (send, 1 - core)):
            for j in range(heads_axis):
                at = pl.ds(pl.multiple_of(base + (which * heads_axis + j) * p1, 8), p1)
                tap = rows_tap[pl.ds(pl.multiple_of((which * heads_axis + j) * r3, r3), r3), :]
                parts = [rows_down[at, :], rows_up[at, :], tap]
                if piece > 2 * p1 + r3:
                    parts.append(extra)
                dest[j] = jnp.concatenate(parts, axis=0).astype(BF)


def order_kernel(me, keep, got, *refs, at, taps):
    parts, outs = refs[:taps], refs[taps:]
    head = me[1]
    rows = parts[0].shape[0] // len(outs)
    chans = parts[0].shape[1]
    for d, out in enumerate(outs):
        value = keep[head ^ d].astype(F32) + got[head ^ d].astype(F32)
        here = pl.ds(pl.multiple_of((head ^ d) * rows, rows), rows)
        tap = value[at : at + rows, 0:chans]
        for ref in parts:
            tap = tap + ref[here, :].astype(F32)
        out[...] = value.astype(BF)
        out[at : at + rows, 0:chans] = tap.astype(BF)


def sum_kernel(*refs):
    acc = refs[0][...].astype(F32)
    for ref in refs[1:-1]:
        acc = acc + ref[...].astype(F32)
    refs[-1][...] = acc.astype(BF)


def local_kernel(me, *refs):
    parts, (mine, send, acc) = refs[:-3], refs[-3:]
    core = me[0] & 1
    for i in range(acc.shape[0]):
        value = parts[0][i].astype(F32)
        for ref in parts[1:]:
            value = value + ref[i].astype(F32)
        acc[i] = value
    for dest, which in ((mine, core), (send, 1 - core)):
        dest[0] = acc[which].astype(BF)
        for i in range(3):
            dest[1 + i] = acc[2 + which + i].astype(BF)


def split_grad_kernel(down, mix_a, mix_b, *refs, late):
    if late:
        _, qkv_out, flipped = refs
    else:
        att_a, att_b, w_up, qkv_out, att_out, flipped = refs

    @pl.when(pl.program_id(0) == 0)
    def _():
        flipped[...] = (mix_a[...].astype(F32) + mix_b[...].astype(F32)).astype(BF).T[0 : flipped.shape[0]]
        if not late:
            att_out[...] = nn((att_a[...].astype(F32) + att_b[...].astype(F32)).astype(BF), w_up[...])

    qkv_out[...] = nn(flipped[...], down[...])


def finish_kernel(me, hidden, base, own, other, w_time, output, grad_clip, rows, *, coarse_frames):
    frame = me[0]
    core = frame & 1
    half = own.shape[1]
    columns = hidden.shape[3]
    for i in range(4):
        rows[i, pl.ds(pl.multiple_of(core * half, half), half), :] = own[i].astype(F32)
        rows[i, pl.ds(pl.multiple_of((1 - core) * half, half), half), :] = other[i].astype(F32)
    lift = pool_matrix(2 * half, columns)
    fine = tn(rows[0].astype(BF), lift)
    for t in range(2):
        for r in range(2):
            output[t, r] = (hidden[t, r].astype(F32) + fine).astype(BF)
    before = (rows[1] * jnp.where(frame == 0, 0.0, 1.0)).astype(BF)
    here = rows[2].astype(BF)
    after = (rows[3] * jnp.where(frame == coarse_frames - 1, 0.0, 1.0)).astype(BF)
    mid = rows[2] + nt(here, w_time[1])
    even = mid + nt(here, w_time[0]) + nt(before, w_time[2])
    odd = mid + nt(after, w_time[0]) + nt(here, w_time[2])
    for t, value in ((0, even), (1, odd)):
        high = value.astype(BF)
        low = (value - high.astype(F32)).astype(BF)
        add = (tn(high, lift) + tn(low, lift)) * 0.125
        for r in range(2):
            grad_clip[t, r] = base[t, r] + add


def gather_kernel(me, embed, *refs, layout, aligned):
    pieces = refs[:8]
    if aligned:
        results, (down_rows, up_rows, time_out, down_out, embed_out, up_out, sems) = refs[8:12], refs[12:]
    else:
        time_out, down_rows, up_rows = refs[8:]
    frame, head = me[0], me[1]
    chips, heads_axis, r1, p1, r3 = layout
    chans = time_out.shape[2]
    devices = 2 * chips * heads_axis
    for core in range(2):
        for idx in range(chips * heads_axis):
            hi, zi = idx // chips, idx % chips
            colors = []
            for color in range(2):
                off = hi if color == 0 else reversed_bits(hi, heads_axis)
                edge = heads_axis // 2
                src = pieces[4 * core + 2 * color + off // edge]
                colors.append(src[off % edge, zi].astype(F32))
            value = jnp.concatenate(colors, axis=0)
            owner = (frame ^ (reversed_bits(zi, chips) * 2 + core)) * heads_axis + (head ^ hi)
            down_rows[owner] = value[0:r1]
            up_rows[owner] = value[p1 : p1 + r1]

            @pl.when(owner < time_out.shape[0])
            def _():
                time_out[owner] = value[2 * p1 : 2 * p1 + r3, 0:chans]

    if aligned:
        buffers = (time_out, down_out, embed_out, up_out)
        copies = [pltpu.make_async_copy(buffers[i], results[i], sems.at[i]) for i in range(4)]
        copies[0].start()
        lanes = down_rows.shape[2]
        eye = (lax.broadcasted_iota(jnp.int32, (lanes, lanes), 0) == lax.broadcasted_iota(jnp.int32, (lanes, lanes), 1))
        eye = eye.astype(F32).astype(BF)
        flipped = nt(eye, down_rows[...].reshape(devices * r1, lanes).astype(BF))
        down_out[...] = flipped[0:chans]
        copies[1].start()
        embed_out[...] = embed[:, 0:1] * flipped[chans : chans + 1]
        copies[2].start()
        up_out[...] = nt(eye[0:chans], up_rows[...].reshape(devices * r1, lanes).astype(BF))
        copies[3].start()
        for copy in copies:
            copy.wait()


def double(x, axis, bits, dim):
    for bit in bits:
        got = swap(x, axis, bit)
        x = jnp.concatenate([x, got], axis=dim)
    return x


def cross(first, second, bits):
    for i, (a, b) in enumerate(zip(bits, reversed(bits))):
        first_in = swap(first, "heads", a)
        second_in = swap(second, "heads", b)
        if i + 1 < len(bits):
            first = jnp.concatenate([first, first_in], axis=0)
            second = jnp.concatenate([second, second_in], axis=0)
    return first, first_in, second, second_in


def body(clip, w_time, w_down, w_embed, w_qkv, w_out, w_up, timestep, cotangent):
    nf = lax.axis_size("frames")
    nh = lax.axis_size("heads")
    f = lax.axis_index("frames")
    h = lax.axis_index("heads")
    me = jnp.stack([f, h]).astype(jnp.int32)
    _, _, columns, chans = clip.shape
    width = w_down.shape[1]
    half_c = columns // 2
    half = half_c // 2
    quart = half // 2
    chips = nf // 2
    padded = round_up(chans + 2, 128)
    pieces = w_qkv.shape[1] // HD
    heads = pieces // 3
    chip_bits = [2 * b for b in reversed(bit_list(chips))]
    head_bits = bit_list(nh)
    devices = nf * nh

    clip_t = clip.transpose(0, 1, 3, 2)
    cot_t = cotangent.transpose(0, 1, 3, 2)
    w_qkv_t = w_qkv.T
    w_up_t = w_up.T

    keep, send = call(
        pool_kernel,
        [sds((2, 3, quart // 2, 2 * chans), BF)] * 2,
        in_specs=[smem(), vmem(), vmem()],
        out_specs=[vmem()] * 2,
        scratch_shapes=[pltpu.VMEM((3, half_c, chans), F32)],
    )(f.astype(jnp.int32).reshape(1), clip_t, cot_t)
    keep_in = swap(send, "frames", 1)
    block = jnp.concatenate([keep, keep_in], axis=1)
    block = double(block, "frames", chip_bits, 1)
    first, second = block[0][None], block[1][None]

    embed = time_embed(timestep, w_embed.shape[0])
    down, mix, out_mix, direct, embed_col = call(
        weight_kernel,
        [
            sds((padded, width), BF),
            sds((padded, pieces * SLOT), BF),
            sds((heads * SLOT, chans), BF),
            sds((padded, chans), BF),
            sds((embed.shape[0], SLOT), F32),
        ],
    )(w_down, w_embed, embed[None, :], w_qkv_t, w_out, w_up_t)

    head, tail = call(
        edge_kernel,
        [sds((4, chans, columns), BF)] * 2,
        in_specs=[vmem(), vmem(), pl.BlockSpec(memory_space=pl.ANY)],
        out_specs=[vmem()] * 2,
    )(clip_t, cot_t, keep)
    lo = lax.ppermute(tail, "frames", [(i, i + 1) for i in range(nf - 1)])
    hi = lax.ppermute(head, "frames", [(i + 1, i) for i in range(nf - 1)])
    tap_rows = round_up(3 * chans, devices * 8)
    hidden, base, tap_keep, tap_send = call(
        fine_kernel,
        [
            sds(clip_t.shape, BF),
            sds(clip_t.shape, F32),
            sds((chips, tap_rows // nf, chans), BF),
            sds((chips, tap_rows // nf, chans), BF),
        ],
        in_specs=[smem()] + [vmem()] * 5,
        out_specs=[vmem()] * 4,
        scratch_shapes=[pltpu.VMEM((chans, 8 * columns), BF)] * 2 + [pltpu.VMEM((tap_rows, chans), F32)],
    )(me, clip_t, cot_t, lo, hi, w_time)
    share = tap_rows // nf
    tap_got = swap(tap_send, "frames", 1)
    tap_parts = call(
        tap_kernel,
        [sds((share, chans), BF)] * chips,
        in_specs=[smem(), vmem(), vmem()],
        out_specs=[vmem()] * chips,
    )(me, tap_keep, tap_got)
    taps = [tap_parts[0]]
    for d in range(1, chips):
        taps.append(swap(tap_parts[d], "frames", 2 * d))

    chip_rows = 2 * width // nf
    r1 = width // devices
    p1 = round_up(r1, 8)
    r3 = share // nh
    piece_rows = round_up(2 * p1 + r3, 16)
    sides = cross(first, second, head_bits)
    simple = r1 == p1
    if simple:
        panes = -(-(chip_rows + SLOT - math.gcd(chip_rows, SLOT)) // SLOT)
        shift = chip_rows
        cells = (w_qkv_t, w_up_t, w_out, down)
    else:
        panes = -(-(2 * nh * p1) // SLOT)
        shift = 0
        start = (f >> 1) * chip_rows

        def columns_of(x):
            x = lax.dynamic_slice_in_dim(x, start, chip_rows, axis=1).reshape(x.shape[0], 2 * nh, r1)
            x = jnp.pad(x, ((0, 0), (0, 0), (0, p1 - r1))).reshape(x.shape[0], 2 * nh * p1)
            return jnp.pad(x, ((0, 0), (0, panes * SLOT - x.shape[1])))

        cells = tuple(columns_of(x) for x in (w_qkv_t, w_up_t, w_out, down))

    def pane(x, i):
        return pl.BlockSpec((x.shape[0], SLOT), lambda g, m: (0, ((m[0] >> 1) * shift) // SLOT + i))

    edge = nh // 2

    def side(mirrored, late):
        def index(g, m):
            at = reversed_bits(g, nh) if mirrored else g
            at = jnp.maximum(at - edge, 0) if late else jnp.minimum(at, edge - 1)
            return (at, 0, 0, 0)

        return pl.BlockSpec((1, nf * 3, quart // 2, 2 * chans), index)

    side_specs = [side(False, False), side(False, True), side(True, False), side(True, True)]
    total = 2 * nf * quart
    every = nh * total

    def whole(*shape):
        return pl.BlockSpec(shape, lambda *g: (0,) * len(shape))

    w_time2 = w_time.reshape(3 * chans, chans)
    statics = (w_time2, mix, out_mix, direct)
    window = panes * SLOT
    outs = [sds((6, 2, quart, chans), BF)] * nh + [
        sds((padded, round_up(pieces * HD, SLOT)), BF),
        sds((heads * HD, chans), BF),
        sds((nh, piece_rows, padded), BF),
        sds((nh, piece_rows, padded), BF),
    ]
    grid_spec = pltpu.PrefetchScalarGridSpec(
        num_scalar_prefetch=1,
        grid=(nh,),
        in_specs=side_specs + [whole(*x.shape) for x in statics] + [pane(x, i) for x in cells for i in range(panes)],
        out_specs=[whole(*x.shape) for x in outs],
        scratch_shapes=[
            pltpu.VMEM((2, nf * 3, quart // 2, 2 * chans), BF),
            pltpu.VMEM((every, tap_rows), BF),
            pltpu.VMEM((total, chans), F32),
            pltpu.VMEM((every, padded), BF),
            pltpu.VMEM((every, chans), BF),
            pltpu.VMEM((total, pieces * SLOT), BF),
            pltpu.VMEM((total, heads * SLOT), BF),
            pltpu.VMEM((every, heads * SLOT), BF),
            pltpu.VMEM((every, pieces * SLOT), BF),
            pltpu.VMEM((2 * heads, total // 2, total // 2), F32),
            pltpu.VMEM((2 * heads, total // 2, total // 2), F32),
            pltpu.VMEM((2 * heads, total // 2, total // 2), BF),
            pltpu.VMEM((2 * heads, total // 2, total // 2), BF),
            pltpu.VMEM((2 * nf, quart, chans), BF),
            pltpu.VMEM((every, chans), BF),
            pltpu.VMEM((window, padded), F32),
            pltpu.VMEM((window, padded), F32),
            pltpu.VMEM((2 * share, padded), F32),
        ],
    )
    rest = (p1, r3, piece_rows, panes, shift)
    results = call(
        functools.partial(coarse_kernel, coarse_frames=nf, heads_axis=nh, rest=rest),
        outs,
        grid_spec=grid_spec,
    )(me, *sides, *statics, *[x for x in cells for _ in range(panes)])
    local = results[:nh]
    mix_g, att_g, d_keep, d_send = results[nh:]

    d_got = swap(d_send, "frames", 1)
    ordered = call(
        functools.partial(order_kernel, at=2 * p1, taps=chips),
        [sds((piece_rows, padded), BF)] * nh,
        in_specs=[smem()] + [vmem()] * (2 + chips),
        out_specs=[vmem()] * nh,
    )(me, d_keep, d_got, *taps)
    got = []
    for d in range(1, nh):
        got.append(swap(ordered[d], "heads", d))
    piece = call(sum_kernel, sds((piece_rows, padded), BF))(ordered[0], *got)
    piece = piece.reshape(2, 1, piece_rows // 2, padded)
    piece = double(piece, "frames", chip_bits, 1)
    shares = cross(piece[0][None], piece[1][None], head_bits)
    mates = []
    for x in shares:
        mates.append(swap(x, "frames", 1))

    got = []
    for d in range(1, nh):
        got.append(swap(local[d], "heads", d))
    four = sds((4, 2, quart, chans), BF)
    mine4, send4 = call(
        local_kernel,
        [four, four],
        in_specs=[smem()] + [vmem()] * nh,
        out_specs=[vmem()] * 2,
        scratch_shapes=[pltpu.VMEM(local[0].shape, F32)],
    )(me, local[0], *got)
    other4 = swap(send4, "frames", 1)
    mine4 = mine4.reshape(4, half, chans)
    other4 = other4.reshape(4, half, chans)
    output, grad_clip = call(
        functools.partial(finish_kernel, coarse_frames=nf),
        [sds(clip_t.shape, BF), sds(clip_t.shape, F32)],
        in_specs=[smem()] + [vmem()] * 5,
        out_specs=[vmem()] * 2,
        scratch_shapes=[pltpu.VMEM((4, half_c, chans), F32)],
    )(me, hidden, base, mine4, other4, w_time)

    mix_o = swap(mix_g, "frames", 1)
    att_o = swap(att_g, "frames", 1)
    step = 256
    early = 2
    wide = sds((pieces * HD, width), F32)
    scratch = [pltpu.VMEM((pieces * HD, padded), BF)]
    grad_qkv, grad_out = call(
        functools.partial(split_grad_kernel, late=False),
        [wide, sds((heads * HD, width), F32)],
        grid=(early,),
        in_specs=[
            pl.BlockSpec((padded, step), lambda g: (0, g)),
            whole(*mix_g.shape),
            whole(*mix_g.shape),
            whole(*att_g.shape),
            whole(*att_g.shape),
            whole(*w_up_t.shape),
        ],
        out_specs=[
            pl.BlockSpec((pieces * HD, step), lambda g: (0, g)),
            whole(heads * HD, width),
        ],
        scratch_shapes=scratch,
    )(down, mix_g, mix_o, att_g, att_o, w_up_t)
    grad_qkv = call(
        functools.partial(split_grad_kernel, late=True),
        wide,
        grid=(width // step - early,),
        in_specs=[
            pl.BlockSpec((padded, step), lambda g: (0, g + early)),
            whole(*mix_g.shape),
            whole(*mix_g.shape),
            pl.BlockSpec(memory_space=pl.ANY),
        ],
        out_specs=pl.BlockSpec((pieces * HD, step), lambda g: (0, g + early)),
        scratch_shapes=scratch,
        input_output_aliases={3: 0},
    )(down, mix_g, mix_o, grad_qkv)

    output, grad_clip, grad_qkv, grad_out, mates[3] = lax.optimization_barrier(
        (output, grad_clip, grad_qkv, grad_out, mates[3])
    )
    aligned = r1 % 8 == 0
    layout = (chips, nh, r1, p1, r3)
    outs = [sds((3 * chans // r3, r3, chans), F32)]
    table = (devices, r1, padded)
    scratch = []
    if aligned:
        outs += [sds((chans, width), F32), sds((w_embed.shape[0], width), F32), sds((chans, width), F32)]
        scratch = [pltpu.VMEM(table, F32)] * 2 + [pltpu.VMEM(x.shape, F32) for x in outs]
        scratch.append(pltpu.SemaphoreType.DMA((4,)))
    else:
        outs += [sds(table, F32)] * 2
    got = call(
        functools.partial(gather_kernel, layout=layout, aligned=aligned),
        outs,
        in_specs=[smem()] + [vmem()] * 9,
        out_specs=[pl.BlockSpec(memory_space=pl.ANY) if aligned else vmem()] * len(outs),
        scratch_shapes=scratch,
    )(me, embed_col, *shares, *mates)
    grad_time = got[0].reshape(w_time.shape)
    if aligned:
        grad_down, grad_embed, grad_up = got[1], got[2], got[3].T
    else:
        down_rows = got[1].reshape(width, padded)
        grad_down = down_rows[:, :chans].T
        grad_embed = embed_col[:, 0:1] * down_rows[:, chans][None, :]
        grad_up = got[2].reshape(width, padded)[:, :chans]
    return (
        output.transpose(0, 1, 3, 2),
        grad_clip.transpose(0, 1, 3, 2),
        grad_time,
        grad_down,
        grad_embed,
        grad_qkv.T,
        grad_out,
        grad_up,
    )


def solution(mesh):
    return jax.shard_map(
        body,
        mesh=mesh,
        in_specs=(
            P("frames", "heads", None, None),
            P(),
            P(),
            P(),
            P(None, "heads"),
            P("heads", None),
            P(),
            P(),
            P("frames", "heads", None, None),
        ),
        out_specs=(
            P("frames", "heads", None, None),
            P("frames", "heads", None, None),
            P(),
            P(),
            P(),
            P(None, "heads"),
            P("heads", None),
            P(),
        ),
        check_vma=False,
    )
```

```python
import functools
import math

import jax
import jax.numpy as jnp
from jax import lax
from jax.experimental import pallas as pl
from jax.experimental.pallas import tpu as pltpu
from jax.sharding import PartitionSpec as P


HD = 80
SLOT = 128
BF = jnp.bfloat16
F32 = jnp.float32


def nn(a, b):
    return lax.dot_general(a, b, (((1,), (0,)), ((), ())), preferred_element_type=F32)


def nt(a, b):
    return lax.dot_general(a, b, (((1,), (1,)), ((), ())), preferred_element_type=F32)


def tn(a, b):
    return lax.dot_general(a, b, (((0,), (0,)), ((), ())), preferred_element_type=F32)


def round_up(value, step):
    return -(-value // step) * step


def call(kernel, out_shape, **kw):
    return pl.pallas_call(
        kernel,
        out_shape=out_shape,
        compiler_params=pltpu.CompilerParams(vmem_limit_bytes=56 * 1024 * 1024),
        **kw,
    )


def smem():
    return pl.BlockSpec(memory_space=pltpu.SMEM)


def vmem():
    return pl.BlockSpec(memory_space=pltpu.VMEM)


def sds(shape, dtype):
    return jax.ShapeDtypeStruct(shape, dtype)


def bit_list(count):
    bits = []
    while (1 << len(bits)) < count:
        bits.append(1 << len(bits))
    return bits


def reversed_bits(value, count):
    n = len(bit_list(count))
    out = 0
    for i in range(n):
        out = out + (((value >> i) & 1) << (n - 1 - i))
    return out


def swap(x, axis, bit):
    n = lax.axis_size(axis)
    return lax.ppermute(x, axis, [(i, i ^ bit) for i in range(n)])


def time_embed(timestep, width):
    half = width // 2
    freqs = jnp.exp(-math.log(10000.0) * jnp.arange(half, dtype=F32) / half)
    angle = timestep.astype(F32)[0] * freqs
    return jax.nn.silu(jnp.concatenate([jnp.cos(angle), jnp.sin(angle)])).astype(BF)


def pool_matrix(half_c, columns):
    row = lax.broadcasted_iota(jnp.int32, (half_c, columns), 0)
    col = lax.broadcasted_iota(jnp.int32, (half_c, columns), 1)
    return jnp.where((col >> 1) == row, 1.0, 0.0).astype(BF)


def fold(x):
    half = x.shape[0] // 2
    return jnp.concatenate([x[:half], x[half:]], axis=1).astype(BF)


def unfold(x):
    half = x.shape[1] // 2
    x = x.astype(F32)
    return jnp.concatenate([x[:, :half], x[:, half:]], axis=0)


def pool_kernel(me, clip, cot, keep, send, tmp):
    half_c = tmp.shape[1]
    half = half_c // 2
    quart = half // 2
    pool = pool_matrix(half_c, clip.shape[3])
    for t in range(2):
        tmp[t] = (nt(pool, clip[t, 0]) + nt(pool, clip[t, 1])) * 0.25
    tmp[2] = (nt(pool, cot[0, 0]) + nt(pool, cot[0, 1])) + (nt(pool, cot[1, 0]) + nt(pool, cot[1, 1]))
    core = me[0] & 1
    for color in range(2):
        for item in range(3):
            base = pl.multiple_of(core * half + color * quart, quart)
            keep[color, item] = fold(tmp[item, pl.ds(base, quart), :])
            base = pl.multiple_of((1 - core) * half + color * quart, quart)
            send[color, item] = fold(tmp[item, pl.ds(base, quart), :])


def edge_kernel(cells, after, head, tail):
    del after
    for r in range(2):
        head[r] = cells[0, r]
        tail[r] = cells[1, r]


def weight_kernel(w_down, w_embed, embed, w_qkv, w_out, w_up, down, mix, out_mix, direct, column):
    wide = embed.shape[1]
    eye = lax.broadcasted_iota(jnp.int32, (wide, wide), 0) == lax.broadcasted_iota(jnp.int32, (wide, wide), 1)
    line = jnp.broadcast_to(embed[...].astype(F32), (SLOT, wide)).astype(BF)
    column[...] = nt(eye.astype(F32).astype(BF), line)
    chans = w_down.shape[0]
    padded = down.shape[0]
    shift = nn(embed[...], w_embed[...])
    high = shift.astype(BF)
    low = (shift - high.astype(F32)).astype(BF)
    down[0:chans, :] = w_down[...]
    row = lax.broadcasted_iota(jnp.int32, (padded - chans, shift.shape[1]), 0)
    tail = jnp.where(row == 0, high.astype(F32), jnp.where(row == 1, low.astype(F32), 0.0))
    down[chans:padded, :] = tail.astype(BF)
    full = down[...]
    pieces = w_qkv.shape[0] // HD
    prod = nt(full, w_qkv[...])
    mix[...] = jnp.zeros(mix.shape, BF)
    for i in range(pieces):
        mix[:, i * SLOT : i * SLOT + HD] = prod[:, i * HD : (i + 1) * HD].astype(BF)
    up = w_up[...]
    small = nt(w_out[...], up)
    out_mix[...] = jnp.zeros(out_mix.shape, BF)
    for i in range(pieces // 3):
        out_mix[i * SLOT : i * SLOT + HD, :] = small[i * HD : (i + 1) * HD, :].astype(BF)
    direct[...] = nt(full, up).astype(BF)


def fine_kernel(me, clip, cot, lo, hi, keep, send, wide, here, taps):
    chans, columns = clip.shape[2], clip.shape[3]
    cells = 2 * columns
    for t in range(4):
        for r in range(2):
            at = slice((2 * t + r) * columns, (2 * t + r + 1) * columns)
            wide[:, at] = lo[r] if t == 0 else (hi[r] if t == 3 else cot[t - 1, r])
            if t in (1, 2):
                here[:, (2 * t - 2 + r) * columns : (2 * t - 1 + r) * columns] = clip[t - 1, r]
    taps[3 * chans :, :] = jnp.zeros((taps.shape[0] - 3 * chans, chans), F32)
    for tap in range(3):
        taps[tap * chans : (tap + 1) * chans, :] = nt(here[...], wide[:, (2 - tap) * cells : (4 - tap) * cells])
    core = me[0] & 1
    share = keep.shape[1]
    for z in range(keep.shape[0]):
        keep[z] = taps[pl.ds(pl.multiple_of((2 * z + core) * share, share), share), :].astype(BF)
        send[z] = taps[pl.ds(pl.multiple_of((2 * z + 1 - core) * share, share), share), :].astype(BF)


def tap_kernel(me, keep, got, *outs):
    for d, out in enumerate(outs):
        at = (me[0] >> 1) ^ d
        out[...] = (keep[at].astype(F32) + got[at].astype(F32)).astype(BF)


def coarse_kernel(
    me, first_a, first_b, second_a, second_b, w_time, mix, out_mix, direct, *refs,
    coarse_frames, heads_axis, rest,
):
    p1, r3, piece, panes, shift = rest
    windows = [refs[i * panes : (i + 1) * panes] for i in range(4)]
    local = refs[4 * panes : 4 * panes + heads_axis]
    grad_mix, grad_att, keep, send = refs[4 * panes + heads_axis : 4 * panes + heads_axis + 4]
    (
    stage, shifted, centre, pooled, upper, qkv, att_grad, att, qkv_grad, score, slope, weight, delta, fields, spread_all,
    rows_down, rows_up, rows_tap,
    ) = refs[4 * panes + heads_axis + 4 :]
    step = pl.program_id(0)
    frame = me[0]
    quart = 2 * stage.shape[2]
    chans = stage.shape[3] // 2
    padded = pooled.shape[1]
    tokens = coarse_frames * quart
    total = 2 * tokens
    chips = coarse_frames // 2
    heads = att.shape[1] // SLOT
    scale = 1.0 / math.sqrt(HD)
    part = 1.0 / heads_axis
    here_rows = pl.ds(pl.multiple_of(step * total, total), total)

    @pl.when(step == 0)
    def _():
        lane = lax.broadcasted_iota(jnp.int32, (pooled.shape[0], padded - chans), 1)
        pooled[:, chans:padded] = jnp.where(lane < 2, 1.0, 0.0).astype(BF)
        shifted[:, 3 * chans :] = jnp.zeros((shifted.shape[0], shifted.shape[1] - 3 * chans), BF)

    def entry(index):
        gap = index ^ frame
        return (reversed_bits(gap >> 1, chips) * 2 + (gap & 1)) * 3

    for color, sources in ((0, (first_a, first_b)), (1, (second_a, second_b))):
        place = step if color == 0 else reversed_bits(step, heads_axis)
        for late in range(2):

            @pl.when((place >= heads_axis // 2) == bool(late))
            def _():
                stage[color] = sources[late][0]

    for color in range(2):
        before = jnp.zeros((quart, chans), F32)
        here = unfold(stage[color, entry(0)])
        for u in range(coarse_frames):
            at = entry(u)
            last = unfold(stage[color, at + 1])
            after = unfold(stage[color, entry(u + 1)]) if u + 1 < coarse_frames else jnp.zeros((quart, chans), F32)
            offset = color * tokens + u * quart
            rows = pl.ds(pl.multiple_of(step * total + offset, quart), quart)
            mid = 0.5 * (here + last)
            shifted[rows, 0:chans] = (0.5 * (before + here)).astype(BF)
            shifted[rows, chans : 2 * chans] = mid.astype(BF)
            shifted[rows, 2 * chans : 3 * chans] = (0.5 * (last + after)).astype(BF)
            centre[offset : offset + quart, :] = mid
            upper[rows, :] = unfold(stage[color, at + 2]).astype(BF)
            before, here = last, after
    pool = (centre[...] + nn(shifted[here_rows, 0 : 3 * chans], w_time[...])).astype(BF)
    pooled[here_rows, 0:chans] = pool
    lines = pooled[here_rows, :]
    ups = upper[here_rows, :]
    qkv[...] = nn(lines, mix[...]).astype(BF)
    att_grad[...] = nt(ups, out_mix[...]).astype(BF)
    row = lax.broadcasted_iota(jnp.int32, (tokens, tokens), 0)
    col = lax.broadcasted_iota(jnp.int32, (tokens, tokens), 1)
    same = (row & (quart - 1)) == (col & (quart - 1))
    ones = jnp.ones((tokens, tokens), BF)
    cases = [(color, n) for color in range(2) for n in range(heads)]

    def part_of(color, n, which):
        return qkv[color * tokens : (color + 1) * tokens, (3 * n + which) * SLOT : (3 * n + which + 1) * SLOT]

    def grad_of(color, n):
        return att_grad[color * tokens : (color + 1) * tokens, n * SLOT : (n + 1) * SLOT]

    for i, (color, n) in enumerate(cases):
        score[i] = nt(part_of(color, n, 0), part_of(color, n, 1))
        slope[i] = nt(grad_of(color, n), part_of(color, n, 2))
    for i, (color, n) in enumerate(cases):
        scores = jnp.where(same, score[i] * scale, -jnp.inf)
        ex = jnp.exp(scores - jnp.max(scores, axis=1, keepdims=True))
        probs = ex * (1.0 / nn(ex.astype(BF), ones))
        dw = slope[i]
        inner = nn((probs * dw).astype(BF), ones)
        weight[i] = probs.astype(BF)
        delta[i] = (probs * (dw - inner) * scale).astype(BF)
    for i, (color, n) in enumerate(cases):
        out = pl.ds(pl.multiple_of(step * total + color * tokens, tokens), tokens)
        att[out, n * SLOT : (n + 1) * SLOT] = nn(weight[i], part_of(color, n, 2)).astype(BF)
        qkv_grad[out, (3 * n) * SLOT : (3 * n + 1) * SLOT] = nn(delta[i], part_of(color, n, 1)).astype(BF)
        qkv_grad[out, (3 * n + 1) * SLOT : (3 * n + 2) * SLOT] = tn(delta[i], part_of(color, n, 0)).astype(BF)
        qkv_grad[out, (3 * n + 2) * SLOT : (3 * n + 3) * SLOT] = tn(weight[i], grad_of(color, n)).astype(BF)
    spread = nt(qkv_grad[here_rows, :], mix[...]) + nt(ups, direct[...]) * part
    spread = spread[:, 0:chans].astype(BF)
    spread_all[here_rows, :] = spread
    fields[...] = spread.reshape(2 * coarse_frames, quart, chans)
    mine = (frame >> 1) * 2
    att_rows, line_rows = [], []
    for color in range(2):
        rows = pl.ds(pl.multiple_of(step * total + color * tokens + mine * quart, 2 * quart), 2 * quart)
        att_rows.append(att[rows, :])
        line_rows.append(pooled[rows, :])
    lifted = nn(jnp.concatenate(att_rows, axis=0), out_mix[...])
    lifted = lifted + nn(jnp.concatenate(line_rows, axis=0), direct[...]) * part
    lifted = lifted.astype(BF).reshape(4, quart, chans)
    for d in range(heads_axis):

        @pl.when(step == d)
        def _():
            for color in range(2):
                for i in range(2):
                    local[d][i, color] = lifted[2 * color + i]
                for i in range(4):
                    at = jnp.clip(mine + i - 1, 0, coarse_frames - 1)
                    local[d][2 + i, color] = fields[color * coarse_frames + at]

    @pl.when(step == heads_axis - 1)
    def _():
        g = tn(pooled[...], qkv_grad[...])
        for i in range(3 * heads):
            grad_mix[:, i * HD : (i + 1) * HD] = g[:, i * SLOT : i * SLOT + HD].astype(BF)
        used = 3 * heads * HD
        grad_mix[:, used:] = jnp.zeros((padded, grad_mix.shape[1] - used), BF)
        a = tn(att[...], upper[...])
        for n in range(heads):
            grad_att[n * HD : (n + 1) * HD, :] = a[n * SLOT : n * SLOT + HD, :].astype(BF)
        s = tn(pooled[...], upper[...]).astype(BF)
        pair = rows_tap.shape[0]
        own = shifted[:, pl.ds(pl.multiple_of((frame >> 1) * pair, pair), pair)]
        rows_tap[:, 0:chans] = tn(own, spread_all[...])
        rows_tap[:, chans:] = jnp.zeros((pair, padded - chans), F32)
        q_win, u_win, o_win, d_win = [jnp.concatenate([ref[...] for ref in group], axis=1) for group in windows]
        down_t = nn(grad_mix[:, 0:used], q_win) + nn(s, u_win) * part
        rows_down[...] = down_t.astype(BF).T.astype(F32)
        up_t = tn(grad_att[...], o_win) + tn(s, d_win) * part
        rows_up[:, 0:chans] = up_t.astype(BF).T.astype(F32)
        rows_up[:, chans:] = jnp.zeros((rows_up.shape[0], padded - chans), F32)
        core = frame & 1
        base = ((frame >> 1) * shift) & (SLOT - 1)
        extra = jnp.zeros((piece - 2 * p1 - r3, padded), F32)
        for dest, which in ((keep, core), (send, 1 - core)):
            for j in range(heads_axis):
                at = pl.ds(pl.multiple_of(base + (which * heads_axis + j) * p1, 8), p1)
                tap = rows_tap[pl.ds(pl.multiple_of((which * heads_axis + j) * r3, r3), r3), :]
                parts = [rows_down[at, :], rows_up[at, :], tap]
                if piece > 2 * p1 + r3:
                    parts.append(extra)
                dest[j] = jnp.concatenate(parts, axis=0).astype(BF)


def order_kernel(me, keep, got, *refs, at, taps):
    parts, outs = refs[:taps], refs[taps:]
    head = me[1]
    rows = parts[0].shape[0] // len(outs)
    chans = parts[0].shape[1]
    for d, out in enumerate(outs):
        value = keep[head ^ d].astype(F32) + got[head ^ d].astype(F32)
        here = pl.ds(pl.multiple_of((head ^ d) * rows, rows), rows)
        tap = value[at : at + rows, 0:chans]
        for ref in parts:
            tap = tap + ref[here, :].astype(F32)
        out[...] = value.astype(BF)
        out[at : at + rows, 0:chans] = tap.astype(BF)


def sum_kernel(*refs):
    acc = refs[0][...].astype(F32)
    for ref in refs[1:-1]:
        acc = acc + ref[...].astype(F32)
    refs[-1][...] = acc.astype(BF)


def local_kernel(me, *refs):
    parts, (mine, send, acc) = refs[:-3], refs[-3:]
    core = me[0] & 1
    for i in range(acc.shape[0]):
        value = parts[0][i].astype(F32)
        for ref in parts[1:]:
            value = value + ref[i].astype(F32)
        acc[i] = value
    for dest, which in ((mine, core), (send, 1 - core)):
        dest[0] = acc[which].astype(BF)
        for i in range(3):
            dest[1 + i] = acc[2 + which + i].astype(BF)


def split_grad_kernel(down, mix_a, mix_b, *refs, late):
    if late:
        _, qkv_out, flipped = refs
    else:
        att_a, att_b, w_up, qkv_out, att_out, flipped = refs

    @pl.when(pl.program_id(0) == 0)
    def _():
        flipped[...] = (mix_a[...].astype(F32) + mix_b[...].astype(F32)).astype(BF).T[0 : flipped.shape[0]]
        if not late:
            att_out[...] = nn((att_a[...].astype(F32) + att_b[...].astype(F32)).astype(BF), w_up[...])

    qkv_out[...] = nn(flipped[...], down[...])


def finish_kernel(me, clip, cot, clip_lo, clip_hi, cot_lo, cot_hi, own, other, w_time, output, grad_clip, wide, grad, rows, *, coarse_frames):
    columns = clip.shape[3]
    cells = 2 * columns
    for t in range(4):
        for r in range(2):
            at = slice((2 * t + r) * columns, (2 * t + r + 1) * columns)
            if t in (0, 3):
                wide[:, at] = (clip_lo if t == 0 else clip_hi)[r]
                grad[:, at] = (cot_lo if t == 0 else cot_hi)[r]
            else:
                wide[:, at] = clip[t - 1, r]
                grad[:, at] = cot[t - 1, r]
    hidden = wide[:, cells : 3 * cells].astype(F32)
    base = grad[:, cells : 3 * cells].astype(F32)
    for tap in range(3):
        hidden = hidden + tn(w_time[tap], wide[:, tap * cells : (tap + 2) * cells])
        base = base + nn(w_time[tap], grad[:, (2 - tap) * cells : (4 - tap) * cells])
    frame = me[0]
    core = frame & 1
    half = own.shape[1]
    for i in range(4):
        rows[i, pl.ds(pl.multiple_of(core * half, half), half), :] = own[i].astype(F32)
        rows[i, pl.ds(pl.multiple_of((1 - core) * half, half), half), :] = other[i].astype(F32)
    lift = pool_matrix(2 * half, columns)
    fine = tn(rows[0].astype(BF), lift)
    for t in range(2):
        for r in range(2):
            at = slice((2 * t + r) * columns, (2 * t + r + 1) * columns)
            output[t, r] = (hidden[:, at] + fine).astype(BF)
    before = (rows[1] * jnp.where(frame == 0, 0.0, 1.0)).astype(BF)
    here = rows[2].astype(BF)
    after = (rows[3] * jnp.where(frame == coarse_frames - 1, 0.0, 1.0)).astype(BF)
    mid = rows[2] + nt(here, w_time[1])
    even = mid + nt(here, w_time[0]) + nt(before, w_time[2])
    odd = mid + nt(after, w_time[0]) + nt(here, w_time[2])
    for t, value in ((0, even), (1, odd)):
        high = value.astype(BF)
        low = (value - high.astype(F32)).astype(BF)
        add = (tn(high, lift) + tn(low, lift)) * 0.125
        for r in range(2):
            at = slice((2 * t + r) * columns, (2 * t + r + 1) * columns)
            grad_clip[t, r] = base[:, at] + add


def gather_kernel(me, embed, *refs, layout, aligned):
    pieces = refs[:8]
    if aligned:
        results, (down_rows, up_rows, time_out, down_out, embed_out, up_out, sems) = refs[8:12], refs[12:]
    else:
        time_out, down_rows, up_rows = refs[8:]
    frame, head = me[0], me[1]
    chips, heads_axis, r1, p1, r3 = layout
    chans = time_out.shape[2]
    devices = 2 * chips * heads_axis
    for core in range(2):
        for idx in range(chips * heads_axis):
            hi, zi = idx // chips, idx % chips
            colors = []
            for color in range(2):
                off = hi if color == 0 else reversed_bits(hi, heads_axis)
                edge = heads_axis // 2
                src = pieces[4 * core + 2 * color + off // edge]
                colors.append(src[off % edge, zi].astype(F32))
            value = jnp.concatenate(colors, axis=0)
            owner = (frame ^ (reversed_bits(zi, chips) * 2 + core)) * heads_axis + (head ^ hi)
            down_rows[owner] = value[0:r1]
            up_rows[owner] = value[p1 : p1 + r1]

            @pl.when(owner < time_out.shape[0])
            def _():
                time_out[owner] = value[2 * p1 : 2 * p1 + r3, 0:chans]

    if aligned:
        buffers = (time_out, down_out, embed_out, up_out)
        copies = [pltpu.make_async_copy(buffers[i], results[i], sems.at[i]) for i in range(4)]
        copies[0].start()
        lanes = down_rows.shape[2]
        eye = (lax.broadcasted_iota(jnp.int32, (lanes, lanes), 0) == lax.broadcasted_iota(jnp.int32, (lanes, lanes), 1))
        eye = eye.astype(F32).astype(BF)
        flipped = nt(eye, down_rows[...].reshape(devices * r1, lanes).astype(BF))
        down_out[...] = flipped[0:chans]
        copies[1].start()
        embed_out[...] = embed[:, 0:1] * flipped[chans : chans + 1]
        copies[2].start()
        up_out[...] = nt(eye[0:chans], up_rows[...].reshape(devices * r1, lanes).astype(BF))
        copies[3].start()
        for copy in copies:
            copy.wait()


def double(x, axis, bits, dim):
    for bit in bits:
        got = swap(x, axis, bit)
        x = jnp.concatenate([x, got], axis=dim)
    return x


def cross(first, second, bits):
    for i, (a, b) in enumerate(zip(bits, reversed(bits))):
        first_in = swap(first, "heads", a)
        second_in = swap(second, "heads", b)
        if i + 1 < len(bits):
            first = jnp.concatenate([first, first_in], axis=0)
            second = jnp.concatenate([second, second_in], axis=0)
    return first, first_in, second, second_in


def body(clip, w_time, w_down, w_embed, w_qkv, w_out, w_up, timestep, cotangent):
    nf = lax.axis_size("frames")
    nh = lax.axis_size("heads")
    f = lax.axis_index("frames")
    h = lax.axis_index("heads")
    me = jnp.stack([f, h]).astype(jnp.int32)
    _, _, columns, chans = clip.shape
    width = w_down.shape[1]
    half_c = columns // 2
    half = half_c // 2
    quart = half // 2
    chips = nf // 2
    padded = round_up(chans + 2, 128)
    pieces = w_qkv.shape[1] // HD
    heads = pieces // 3
    chip_bits = [2 * b for b in reversed(bit_list(chips))]
    head_bits = bit_list(nh)
    devices = nf * nh

    clip_t = clip.transpose(0, 1, 3, 2)
    cot_t = cotangent.transpose(0, 1, 3, 2)
    w_qkv_t = w_qkv.T
    w_up_t = w_up.T

    keep, send = call(
        pool_kernel,
        [sds((2, 3, quart // 2, 2 * chans), BF)] * 2,
        in_specs=[smem(), vmem(), vmem()],
        out_specs=[vmem()] * 2,
        scratch_shapes=[pltpu.VMEM((3, half_c, chans), F32)],
    )(f.astype(jnp.int32).reshape(1), clip_t, cot_t)
    keep_in = swap(send, "frames", 1)
    block = jnp.concatenate([keep, keep_in], axis=1)
    block = double(block, "frames", chip_bits, 1)
    first, second = block[0][None], block[1][None]

    embed = time_embed(timestep, w_embed.shape[0])
    down, mix, out_mix, direct, embed_col = call(
        weight_kernel,
        [
            sds((padded, width), BF),
            sds((padded, pieces * SLOT), BF),
            sds((heads * SLOT, chans), BF),
            sds((padded, chans), BF),
            sds((embed.shape[0], SLOT), F32),
        ],
    )(w_down, w_embed, embed[None, :], w_qkv_t, w_out, w_up_t)

    def halo(x, after):
        head, tail = call(
            edge_kernel,
            [sds((2, chans, columns), BF)] * 2,
            in_specs=[vmem(), pl.BlockSpec(memory_space=pl.ANY)],
            out_specs=[vmem()] * 2,
        )(x, after)
        lo = lax.ppermute(tail, "frames", [(i, i + 1) for i in range(nf - 1)])
        hi = lax.ppermute(head, "frames", [(i + 1, i) for i in range(nf - 1)])
        return lo, hi

    cot_lo, cot_hi = halo(cot_t, keep)
    clip_lo, clip_hi = halo(clip_t, keep)
    tap_rows = round_up(3 * chans, devices * 8)
    tap_keep, tap_send = call(
        fine_kernel,
        [sds((chips, tap_rows // nf, chans), BF)] * 2,
        in_specs=[smem()] + [vmem()] * 4,
        out_specs=[vmem()] * 2,
        scratch_shapes=[
            pltpu.VMEM((chans, 8 * columns), BF),
            pltpu.VMEM((chans, 4 * columns), BF),
            pltpu.VMEM((tap_rows, chans), F32),
        ],
    )(me, clip_t, cot_t, cot_lo, cot_hi)
    share = tap_rows // nf
    tap_got = swap(tap_send, "frames", 1)
    tap_parts = call(
        tap_kernel,
        [sds((share, chans), BF)] * chips,
        in_specs=[smem(), vmem(), vmem()],
        out_specs=[vmem()] * chips,
    )(me, tap_keep, tap_got)
    taps = [tap_parts[0]]
    for d in range(1, chips):
        taps.append(swap(tap_parts[d], "frames", 2 * d))

    chip_rows = 2 * width // nf
    r1 = width // devices
    p1 = round_up(r1, 8)
    r3 = share // nh
    piece_rows = round_up(2 * p1 + r3, 16)
    sides = cross(first, second, head_bits)
    simple = r1 == p1
    if simple:
        panes = -(-(chip_rows + SLOT - math.gcd(chip_rows, SLOT)) // SLOT)
        shift = chip_rows
        cells = (w_qkv_t, w_up_t, w_out, down)
    else:
        panes = -(-(2 * nh * p1) // SLOT)
        shift = 0
        start = (f >> 1) * chip_rows

        def columns_of(x):
            x = lax.dynamic_slice_in_dim(x, start, chip_rows, axis=1).reshape(x.shape[0], 2 * nh, r1)
            x = jnp.pad(x, ((0, 0), (0, 0), (0, p1 - r1))).reshape(x.shape[0], 2 * nh * p1)
            return jnp.pad(x, ((0, 0), (0, panes * SLOT - x.shape[1])))

        cells = tuple(columns_of(x) for x in (w_qkv_t, w_up_t, w_out, down))

    def pane(x, i):
        return pl.BlockSpec((x.shape[0], SLOT), lambda g, m: (0, ((m[0] >> 1) * shift) // SLOT + i))

    edge = nh // 2

    def side(mirrored, late):
        def index(g, m):
            at = reversed_bits(g, nh) if mirrored else g
            at = jnp.maximum(at - edge, 0) if late else jnp.minimum(at, edge - 1)
            return (at, 0, 0, 0)

        return pl.BlockSpec((1, nf * 3, quart // 2, 2 * chans), index)

    side_specs = [side(False, False), side(False, True), side(True, False), side(True, True)]
    total = 2 * nf * quart
    every = nh * total

    def whole(*shape):
        return pl.BlockSpec(shape, lambda *g: (0,) * len(shape))

    w_time2 = w_time.reshape(3 * chans, chans)
    statics = (w_time2, mix, out_mix, direct)
    window = panes * SLOT
    outs = [sds((6, 2, quart, chans), BF)] * nh + [
        sds((padded, round_up(pieces * HD, SLOT)), BF),
        sds((heads * HD, chans), BF),
        sds((nh, piece_rows, padded), BF),
        sds((nh, piece_rows, padded), BF),
    ]
    grid_spec = pltpu.PrefetchScalarGridSpec(
        num_scalar_prefetch=1,
        grid=(nh,),
        in_specs=side_specs + [whole(*x.shape) for x in statics] + [pane(x, i) for x in cells for i in range(panes)],
        out_specs=[whole(*x.shape) for x in outs],
        scratch_shapes=[
            pltpu.VMEM((2, nf * 3, quart // 2, 2 * chans), BF),
            pltpu.VMEM((every, tap_rows), BF),
            pltpu.VMEM((total, chans), F32),
            pltpu.VMEM((every, padded), BF),
            pltpu.VMEM((every, chans), BF),
            pltpu.VMEM((total, pieces * SLOT), BF),
            pltpu.VMEM((total, heads * SLOT), BF),
            pltpu.VMEM((every, heads * SLOT), BF),
            pltpu.VMEM((every, pieces * SLOT), BF),
            pltpu.VMEM((2 * heads, total // 2, total // 2), F32),
            pltpu.VMEM((2 * heads, total // 2, total // 2), F32),
            pltpu.VMEM((2 * heads, total // 2, total // 2), BF),
            pltpu.VMEM((2 * heads, total // 2, total // 2), BF),
            pltpu.VMEM((2 * nf, quart, chans), BF),
            pltpu.VMEM((every, chans), BF),
            pltpu.VMEM((window, padded), F32),
            pltpu.VMEM((window, padded), F32),
            pltpu.VMEM((2 * share, padded), F32),
        ],
    )
    rest = (p1, r3, piece_rows, panes, shift)
    results = call(
        functools.partial(coarse_kernel, coarse_frames=nf, heads_axis=nh, rest=rest),
        outs,
        grid_spec=grid_spec,
    )(me, *sides, *statics, *[x for x in cells for _ in range(panes)])
    local = results[:nh]
    mix_g, att_g, d_keep, d_send = results[nh:]

    d_got = swap(d_send, "frames", 1)
    ordered = call(
        functools.partial(order_kernel, at=2 * p1, taps=chips),
        [sds((piece_rows, padded), BF)] * nh,
        in_specs=[smem()] + [vmem()] * (2 + chips),
        out_specs=[vmem()] * nh,
    )(me, d_keep, d_got, *taps)
    got = []
    for d in range(1, nh):
        got.append(swap(ordered[d], "heads", d))
    piece = call(sum_kernel, sds((piece_rows, padded), BF))(ordered[0], *got)
    piece = piece.reshape(2, 1, piece_rows // 2, padded)
    piece = double(piece, "frames", chip_bits, 1)
    shares = cross(piece[0][None], piece[1][None], head_bits)
    mates = []
    for x in shares:
        mates.append(swap(x, "frames", 1))

    got = []
    for d in range(1, nh):
        got.append(swap(local[d], "heads", d))
    four = sds((4, 2, quart, chans), BF)
    mine4, send4 = call(
        local_kernel,
        [four, four],
        in_specs=[smem()] + [vmem()] * nh,
        out_specs=[vmem()] * 2,
        scratch_shapes=[pltpu.VMEM(local[0].shape, F32)],
    )(me, local[0], *got)
    other4 = swap(send4, "frames", 1)
    mine4 = mine4.reshape(4, half, chans)
    other4 = other4.reshape(4, half, chans)
    output, grad_clip = call(
        functools.partial(finish_kernel, coarse_frames=nf),
        [sds(clip_t.shape, BF), sds(clip_t.shape, F32)],
        in_specs=[smem()] + [vmem()] * 9,
        out_specs=[vmem()] * 2,
        scratch_shapes=[pltpu.VMEM((chans, 8 * columns), BF)] * 2 + [pltpu.VMEM((4, half_c, chans), F32)],
    )(me, clip_t, cot_t, clip_lo, clip_hi, cot_lo, cot_hi, mine4, other4, w_time)

    mix_o = swap(mix_g, "frames", 1)
    att_o = swap(att_g, "frames", 1)
    step = 256
    early = 2
    wide = sds((pieces * HD, width), F32)
    scratch = [pltpu.VMEM((pieces * HD, padded), BF)]
    grad_qkv, grad_out = call(
        functools.partial(split_grad_kernel, late=False),
        [wide, sds((heads * HD, width), F32)],
        grid=(early,),
        in_specs=[
            pl.BlockSpec((padded, step), lambda g: (0, g)),
            whole(*mix_g.shape),
            whole(*mix_g.shape),
            whole(*att_g.shape),
            whole(*att_g.shape),
            whole(*w_up_t.shape),
        ],
        out_specs=[
            pl.BlockSpec((pieces * HD, step), lambda g: (0, g)),
            whole(heads * HD, width),
        ],
        scratch_shapes=scratch,
    )(down, mix_g, mix_o, att_g, att_o, w_up_t)
    grad_qkv = call(
        functools.partial(split_grad_kernel, late=True),
        wide,
        grid=(width // step - early,),
        in_specs=[
            pl.BlockSpec((padded, step), lambda g: (0, g + early)),
            whole(*mix_g.shape),
            whole(*mix_g.shape),
            pl.BlockSpec(memory_space=pl.ANY),
        ],
        out_specs=pl.BlockSpec((pieces * HD, step), lambda g: (0, g + early)),
        scratch_shapes=scratch,
        input_output_aliases={3: 0},
    )(down, mix_g, mix_o, grad_qkv)

    output, grad_clip, grad_qkv, grad_out, mates[3] = lax.optimization_barrier(
        (output, grad_clip, grad_qkv, grad_out, mates[3])
    )
    aligned = r1 % 8 == 0
    layout = (chips, nh, r1, p1, r3)
    outs = [sds((3 * chans // r3, r3, chans), F32)]
    table = (devices, r1, padded)
    scratch = []
    if aligned:
        outs += [sds((chans, width), F32), sds((w_embed.shape[0], width), F32), sds((chans, width), F32)]
        scratch = [pltpu.VMEM(table, F32)] * 2 + [pltpu.VMEM(x.shape, F32) for x in outs]
        scratch.append(pltpu.SemaphoreType.DMA((4,)))
    else:
        outs += [sds(table, F32)] * 2
    got = call(
        functools.partial(gather_kernel, layout=layout, aligned=aligned),
        outs,
        in_specs=[smem()] + [vmem()] * 9,
        out_specs=[pl.BlockSpec(memory_space=pl.ANY) if aligned else vmem()] * len(outs),
        scratch_shapes=scratch,
    )(me, embed_col, *shares, *mates)
    grad_time = got[0].reshape(w_time.shape)
    if aligned:
        grad_down, grad_embed, grad_up = got[1], got[2], got[3].T
    else:
        down_rows = got[1].reshape(width, padded)
        grad_down = down_rows[:, :chans].T
        grad_embed = embed_col[:, 0:1] * down_rows[:, chans][None, :]
        grad_up = got[2].reshape(width, padded)[:, :chans]
    return (
        output.transpose(0, 1, 3, 2),
        grad_clip.transpose(0, 1, 3, 2),
        grad_time,
        grad_down,
        grad_embed,
        grad_qkv.T,
        grad_out,
        grad_up,
    )


def solution(mesh):
    return jax.shard_map(
        body,
        mesh=mesh,
        in_specs=(
            P("frames", "heads", None, None),
            P(),
            P(),
            P(),
            P(None, "heads"),
            P("heads", None),
            P(),
            P(),
            P("frames", "heads", None, None),
        ),
        out_specs=(
            P("frames", "heads", None, None),
            P("frames", "heads", None, None),
            P(),
            P(),
            P(),
            P(None, "heads"),
            P("heads", None),
            P(),
        ),
        check_vma=False,
    )
```

```python
import functools
import math

import jax
import jax.numpy as jnp
from jax import lax
from jax.experimental import pallas as pl
from jax.experimental.pallas import tpu as pltpu
from jax.sharding import PartitionSpec as P


HD = 80
SLOT = 128
BF = jnp.bfloat16
F32 = jnp.float32


def nn(a, b):
    return lax.dot_general(a, b, (((1,), (0,)), ((), ())), preferred_element_type=F32)


def nt(a, b):
    return lax.dot_general(a, b, (((1,), (1,)), ((), ())), preferred_element_type=F32)


def tn(a, b):
    return lax.dot_general(a, b, (((0,), (0,)), ((), ())), preferred_element_type=F32)


def round_up(value, step):
    return -(-value // step) * step


def call(kernel, out_shape, **kw):
    return pl.pallas_call(
        kernel,
        out_shape=out_shape,
        compiler_params=pltpu.CompilerParams(vmem_limit_bytes=56 * 1024 * 1024),
        **kw,
    )


def smem():
    return pl.BlockSpec(memory_space=pltpu.SMEM)


def vmem():
    return pl.BlockSpec(memory_space=pltpu.VMEM)


def sds(shape, dtype):
    return jax.ShapeDtypeStruct(shape, dtype)


def bit_list(count):
    bits = []
    while (1 << len(bits)) < count:
        bits.append(1 << len(bits))
    return bits


def reversed_bits(value, count):
    n = len(bit_list(count))
    out = 0
    for i in range(n):
        out = out + (((value >> i) & 1) << (n - 1 - i))
    return out


def swap(x, axis, bit):
    n = lax.axis_size(axis)
    return lax.ppermute(x, axis, [(i, i ^ bit) for i in range(n)])


def time_embed(timestep, width):
    half = width // 2
    freqs = jnp.exp(-math.log(10000.0) * jnp.arange(half, dtype=F32) / half)
    angle = timestep.astype(F32)[0] * freqs
    return jax.nn.silu(jnp.concatenate([jnp.cos(angle), jnp.sin(angle)])).astype(BF)


def pool_matrix(half_c, columns):
    row = lax.broadcasted_iota(jnp.int32, (half_c, columns), 0)
    col = lax.broadcasted_iota(jnp.int32, (half_c, columns), 1)
    return jnp.where((col >> 1) == row, 1.0, 0.0).astype(BF)


def fold(x):
    half = x.shape[0] // 2
    return jnp.concatenate([x[:half], x[half:]], axis=1).astype(BF)


def unfold(x):
    half = x.shape[1] // 2
    x = x.astype(F32)
    return jnp.concatenate([x[:, :half], x[:, half:]], axis=0)


def pool_kernel(me, clip, cot, keep, send, tmp):
    half_c = tmp.shape[1]
    half = half_c // 2
    quart = half // 2
    pool = pool_matrix(half_c, clip.shape[3])
    for t in range(2):
        tmp[t] = (nt(pool, clip[t, 0]) + nt(pool, clip[t, 1])) * 0.25
    tmp[2] = (nt(pool, cot[0, 0]) + nt(pool, cot[0, 1])) + (nt(pool, cot[1, 0]) + nt(pool, cot[1, 1]))
    core = me[0] & 1
    for color in range(2):
        for item in range(3):
            base = pl.multiple_of(core * half + color * quart, quart)
            keep[color, item] = fold(tmp[item, pl.ds(base, quart), :])
            base = pl.multiple_of((1 - core) * half + color * quart, quart)
            send[color, item] = fold(tmp[item, pl.ds(base, quart), :])


def edge_kernel(cells, after, head, tail):
    del after
    for r in range(2):
        head[r] = cells[0, r]
        tail[r] = cells[1, r]


def weight_kernel(w_down, w_embed, embed, w_qkv, w_out, w_up, down, mix, out_mix, direct, column):
    wide = embed.shape[1]
    eye = lax.broadcasted_iota(jnp.int32, (wide, wide), 0) == lax.broadcasted_iota(jnp.int32, (wide, wide), 1)
    line = jnp.broadcast_to(embed[...].astype(F32), (SLOT, wide)).astype(BF)
    column[...] = nt(eye.astype(F32).astype(BF), line)
    chans = w_down.shape[0]
    padded = down.shape[0]
    shift = nn(embed[...], w_embed[...])
    high = shift.astype(BF)
    low = (shift - high.astype(F32)).astype(BF)
    down[0:chans, :] = w_down[...]
    row = lax.broadcasted_iota(jnp.int32, (padded - chans, shift.shape[1]), 0)
    tail = jnp.where(row == 0, high.astype(F32), jnp.where(row == 1, low.astype(F32), 0.0))
    down[chans:padded, :] = tail.astype(BF)
    full = down[...]
    pieces = w_qkv.shape[0] // HD
    prod = nt(full, w_qkv[...])
    mix[...] = jnp.zeros(mix.shape, BF)
    for i in range(pieces):
        mix[:, i * SLOT : i * SLOT + HD] = prod[:, i * HD : (i + 1) * HD].astype(BF)
    up = w_up[...]
    small = nt(w_out[...], up)
    out_mix[...] = jnp.zeros(out_mix.shape, BF)
    for i in range(pieces // 3):
        out_mix[i * SLOT : i * SLOT + HD, :] = small[i * HD : (i + 1) * HD, :].astype(BF)
    direct[...] = nt(full, up).astype(BF)


def fine_kernel(me, clip, cot, lo, hi, *refs):
    outs, (wide, here, taps) = refs[:-3], refs[-3:]
    chans, columns = clip.shape[2], clip.shape[3]
    cells = 2 * columns
    for t in range(4):
        for r in range(2):
            at = slice((2 * t + r) * columns, (2 * t + r + 1) * columns)
            wide[:, at] = lo[r] if t == 0 else (hi[r] if t == 3 else cot[t - 1, r])
            if t in (1, 2):
                here[:, (2 * t - 2 + r) * columns : (2 * t - 1 + r) * columns] = clip[t - 1, r]
    taps[3 * chans :, :] = jnp.zeros((taps.shape[0] - 3 * chans, chans), F32)
    for tap in range(3):
        taps[tap * chans : (tap + 1) * chans, :] = nt(here[...], wide[:, (2 - tap) * cells : (4 - tap) * cells])
    pair = outs[0].shape[0]
    for d, out in enumerate(outs):
        at = (me[0] >> 1) ^ d
        out[...] = taps[pl.ds(pl.multiple_of(at * pair, pair), pair), :].astype(BF)


def tap_kernel(me, *refs):
    parts, (keep, send) = refs[:-2], refs[-2:]
    share = keep.shape[0]
    core = me[0] & 1
    for dest, which in ((keep, core), (send, 1 - core)):
        rows = pl.ds(pl.multiple_of(which * share, share), share)
        acc = parts[0][rows, :].astype(F32)
        for ref in parts[1:]:
            acc = acc + ref[rows, :].astype(F32)
        dest[...] = acc.astype(BF)


def coarse_kernel(
    me, first_a, first_b, second_a, second_b, w_time, mix, out_mix, direct, *refs,
    coarse_frames, heads_axis, rest,
):
    p1, r3, piece, panes, shift = rest
    windows = [refs[i * panes : (i + 1) * panes] for i in range(4)]
    local = refs[4 * panes : 4 * panes + heads_axis]
    grad_mix, grad_att, keep, send = refs[4 * panes + heads_axis : 4 * panes + heads_axis + 4]
    (
    stage, shifted, centre, pooled, upper, qkv, att_grad, att, qkv_grad, score, slope, weight, delta, fields, spread_all,
    rows_down, rows_up, rows_tap,
    ) = refs[4 * panes + heads_axis + 4 :]
    step = pl.program_id(0)
    frame = me[0]
    quart = 2 * stage.shape[2]
    chans = stage.shape[3] // 2
    padded = pooled.shape[1]
    tokens = coarse_frames * quart
    total = 2 * tokens
    chips = coarse_frames // 2
    heads = att.shape[1] // SLOT
    scale = 1.0 / math.sqrt(HD)
    part = 1.0 / heads_axis
    here_rows = pl.ds(pl.multiple_of(step * total, total), total)

    @pl.when(step == 0)
    def _():
        lane = lax.broadcasted_iota(jnp.int32, (pooled.shape[0], padded - chans), 1)
        pooled[:, chans:padded] = jnp.where(lane < 2, 1.0, 0.0).astype(BF)
        shifted[:, 3 * chans :] = jnp.zeros((shifted.shape[0], shifted.shape[1] - 3 * chans), BF)

    def entry(index):
        gap = index ^ frame
        return (reversed_bits(gap >> 1, chips) * 2 + (gap & 1)) * 3

    for color, sources in ((0, (first_a, first_b)), (1, (second_a, second_b))):
        place = step if color == 0 else reversed_bits(step, heads_axis)
        for late in range(2):

            @pl.when((place >= heads_axis // 2) == bool(late))
            def _():
                stage[color] = sources[late][0]

    for color in range(2):
        before = jnp.zeros((quart, chans), F32)
        here = unfold(stage[color, entry(0)])
        for u in range(coarse_frames):
            at = entry(u)
            last = unfold(stage[color, at + 1])
            after = unfold(stage[color, entry(u + 1)]) if u + 1 < coarse_frames else jnp.zeros((quart, chans), F32)
            offset = color * tokens + u * quart
            rows = pl.ds(pl.multiple_of(step * total + offset, quart), quart)
            mid = 0.5 * (here + last)
            shifted[rows, 0:chans] = (0.5 * (before + here)).astype(BF)
            shifted[rows, chans : 2 * chans] = mid.astype(BF)
            shifted[rows, 2 * chans : 3 * chans] = (0.5 * (last + after)).astype(BF)
            centre[offset : offset + quart, :] = mid
            upper[rows, :] = unfold(stage[color, at + 2]).astype(BF)
            before, here = last, after
    pool = (centre[...] + nn(shifted[here_rows, 0 : 3 * chans], w_time[...])).astype(BF)
    pooled[here_rows, 0:chans] = pool
    lines = pooled[here_rows, :]
    ups = upper[here_rows, :]
    qkv[...] = nn(lines, mix[...]).astype(BF)
    att_grad[...] = nt(ups, out_mix[...]).astype(BF)
    row = lax.broadcasted_iota(jnp.int32, (tokens, tokens), 0)
    col = lax.broadcasted_iota(jnp.int32, (tokens, tokens), 1)
    same = (row & (quart - 1)) == (col & (quart - 1))
    ones = jnp.ones((tokens, tokens), BF)
    cases = [(color, n) for color in range(2) for n in range(heads)]

    def part_of(color, n, which):
        return qkv[color * tokens : (color + 1) * tokens, (3 * n + which) * SLOT : (3 * n + which + 1) * SLOT]

    def grad_of(color, n):
        return att_grad[color * tokens : (color + 1) * tokens, n * SLOT : (n + 1) * SLOT]

    for i, (color, n) in enumerate(cases):
        score[i] = nt(part_of(color, n, 0), part_of(color, n, 1))
        slope[i] = nt(grad_of(color, n), part_of(color, n, 2))
    for i, (color, n) in enumerate(cases):
        scores = jnp.where(same, score[i] * scale, -jnp.inf)
        ex = jnp.exp(scores - jnp.max(scores, axis=1, keepdims=True))
        probs = ex * (1.0 / nn(ex.astype(BF), ones))
        dw = slope[i]
        inner = nn((probs * dw).astype(BF), ones)
        weight[i] = probs.astype(BF)
        delta[i] = (probs * (dw - inner) * scale).astype(BF)
    for i, (color, n) in enumerate(cases):
        out = pl.ds(pl.multiple_of(step * total + color * tokens, tokens), tokens)
        att[out, n * SLOT : (n + 1) * SLOT] = nn(weight[i], part_of(color, n, 2)).astype(BF)
        qkv_grad[out, (3 * n) * SLOT : (3 * n + 1) * SLOT] = nn(delta[i], part_of(color, n, 1)).astype(BF)
        qkv_grad[out, (3 * n + 1) * SLOT : (3 * n + 2) * SLOT] = tn(delta[i], part_of(color, n, 0)).astype(BF)
        qkv_grad[out, (3 * n + 2) * SLOT : (3 * n + 3) * SLOT] = tn(weight[i], grad_of(color, n)).astype(BF)
    spread = nt(qkv_grad[here_rows, :], mix[...]) + nt(ups, direct[...]) * part
    spread = spread[:, 0:chans].astype(BF)
    spread_all[here_rows, :] = spread
    fields[...] = spread.reshape(2 * coarse_frames, quart, chans)
    mine = (frame >> 1) * 2
    att_rows, line_rows = [], []
    for color in range(2):
        rows = pl.ds(pl.multiple_of(step * total + color * tokens + mine * quart, 2 * quart), 2 * quart)
        att_rows.append(att[rows, :])
        line_rows.append(pooled[rows, :])
    lifted = nn(jnp.concatenate(att_rows, axis=0), out_mix[...])
    lifted = lifted + nn(jnp.concatenate(line_rows, axis=0), direct[...]) * part
    lifted = lifted.astype(BF).reshape(4, quart, chans)
    for d in range(heads_axis):

        @pl.when(step == d)
        def _():
            for color in range(2):
                for i in range(2):
                    local[d][i, color] = lifted[2 * color + i]
                for i in range(4):
                    at = jnp.clip(mine + i - 1, 0, coarse_frames - 1)
                    local[d][2 + i, color] = fields[color * coarse_frames + at]

    @pl.when(step == heads_axis - 1)
    def _():
        g = tn(pooled[...], qkv_grad[...])
        for i in range(3 * heads):
            grad_mix[:, i * HD : (i + 1) * HD] = g[:, i * SLOT : i * SLOT + HD].astype(BF)
        used = 3 * heads * HD
        grad_mix[:, used:] = jnp.zeros((padded, grad_mix.shape[1] - used), BF)
        a = tn(att[...], upper[...])
        for n in range(heads):
            grad_att[n * HD : (n + 1) * HD, :] = a[n * SLOT : n * SLOT + HD, :].astype(BF)
        s = tn(pooled[...], upper[...]).astype(BF)
        pair = rows_tap.shape[0]
        own = shifted[:, pl.ds(pl.multiple_of((frame >> 1) * pair, pair), pair)]
        rows_tap[:, 0:chans] = tn(own, spread_all[...])
        rows_tap[:, chans:] = jnp.zeros((pair, padded - chans), F32)
        q_win, u_win, o_win, d_win = [jnp.concatenate([ref[...] for ref in group], axis=1) for group in windows]
        down_t = nn(grad_mix[:, 0:used], q_win) + nn(s, u_win) * part
        rows_down[...] = down_t.astype(BF).T.astype(F32)
        up_t = tn(grad_att[...], o_win) + tn(s, d_win) * part
        rows_up[:, 0:chans] = up_t.astype(BF).T.astype(F32)
        rows_up[:, chans:] = jnp.zeros((rows_up.shape[0], padded - chans), F32)
        core = frame & 1
        base = ((frame >> 1) * shift) & (SLOT - 1)
        extra = jnp.zeros((piece - 2 * p1 - r3, padded), F32)
        for dest, which in ((keep, core), (send, 1 - core)):
            for j in range(heads_axis):
                at = pl.ds(pl.multiple_of(base + (which * heads_axis + j) * p1, 8), p1)
                tap = rows_tap[pl.ds(pl.multiple_of((which * heads_axis + j) * r3, r3), r3), :]
                parts = [rows_down[at, :], rows_up[at, :], tap]
                if piece > 2 * p1 + r3:
                    parts.append(extra)
                dest[j] = jnp.concatenate(parts, axis=0).astype(BF)


def order_kernel(me, keep, got, *refs, at, taps):
    parts, outs = refs[:taps], refs[taps:]
    head = me[1]
    rows = parts[0].shape[0] // len(outs)
    chans = parts[0].shape[1]
    for d, out in enumerate(outs):
        value = keep[head ^ d].astype(F32) + got[head ^ d].astype(F32)
        here = pl.ds(pl.multiple_of((head ^ d) * rows, rows), rows)
        tap = value[at : at + rows, 0:chans]
        for ref in parts:
            tap = tap + ref[here, :].astype(F32)
        out[...] = value.astype(BF)
        out[at : at + rows, 0:chans] = tap.astype(BF)


def sum_kernel(*refs):
    acc = refs[0][...].astype(F32)
    for ref in refs[1:-1]:
        acc = acc + ref[...].astype(F32)
    refs[-1][...] = acc.astype(BF)


def local_kernel(me, *refs):
    parts, (mine, send, acc) = refs[:-3], refs[-3:]
    core = me[0] & 1
    for i in range(acc.shape[0]):
        value = parts[0][i].astype(F32)
        for ref in parts[1:]:
            value = value + ref[i].astype(F32)
        acc[i] = value
    for dest, which in ((mine, core), (send, 1 - core)):
        dest[0] = acc[which].astype(BF)
        for i in range(3):
            dest[1 + i] = acc[2 + which + i].astype(BF)


def split_grad_kernel(down, mix_a, mix_b, *refs, late):
    if late:
        _, qkv_out, flipped = refs
    else:
        att_a, att_b, w_up, qkv_out, att_out, flipped = refs

    @pl.when(pl.program_id(0) == 0)
    def _():
        flipped[...] = (mix_a[...].astype(F32) + mix_b[...].astype(F32)).astype(BF).T[0 : flipped.shape[0]]
        if not late:
            att_out[...] = nn((att_a[...].astype(F32) + att_b[...].astype(F32)).astype(BF), w_up[...])

    qkv_out[...] = nn(flipped[...], down[...])


def finish_kernel(me, clip, cot, clip_lo, clip_hi, cot_lo, cot_hi, own, other, w_time, output, grad_clip, wide, grad, rows, *, coarse_frames):
    columns = clip.shape[3]
    cells = 2 * columns
    for t in range(4):
        for r in range(2):
            at = slice((2 * t + r) * columns, (2 * t + r + 1) * columns)
            if t in (0, 3):
                wide[:, at] = (clip_lo if t == 0 else clip_hi)[r]
                grad[:, at] = (cot_lo if t == 0 else cot_hi)[r]
            else:
                wide[:, at] = clip[t - 1, r]
                grad[:, at] = cot[t - 1, r]
    hidden = wide[:, cells : 3 * cells].astype(F32)
    base = grad[:, cells : 3 * cells].astype(F32)
    for tap in range(3):
        hidden = hidden + tn(w_time[tap], wide[:, tap * cells : (tap + 2) * cells])
        base = base + nn(w_time[tap], grad[:, (2 - tap) * cells : (4 - tap) * cells])
    frame = me[0]
    core = frame & 1
    half = own.shape[1]
    for i in range(4):
        rows[i, pl.ds(pl.multiple_of(core * half, half), half), :] = own[i].astype(F32)
        rows[i, pl.ds(pl.multiple_of((1 - core) * half, half), half), :] = other[i].astype(F32)
    lift = pool_matrix(2 * half, columns)
    fine = tn(rows[0].astype(BF), lift)
    for t in range(2):
        for r in range(2):
            at = slice((2 * t + r) * columns, (2 * t + r + 1) * columns)
            output[t, r] = (hidden[:, at] + fine).astype(BF)
    before = (rows[1] * jnp.where(frame == 0, 0.0, 1.0)).astype(BF)
    here = rows[2].astype(BF)
    after = (rows[3] * jnp.where(frame == coarse_frames - 1, 0.0, 1.0)).astype(BF)
    mid = rows[2] + nt(here, w_time[1])
    even = mid + nt(here, w_time[0]) + nt(before, w_time[2])
    odd = mid + nt(after, w_time[0]) + nt(here, w_time[2])
    for t, value in ((0, even), (1, odd)):
        high = value.astype(BF)
        low = (value - high.astype(F32)).astype(BF)
        add = (tn(high, lift) + tn(low, lift)) * 0.125
        for r in range(2):
            at = slice((2 * t + r) * columns, (2 * t + r + 1) * columns)
            grad_clip[t, r] = base[:, at] + add


def gather_kernel(me, embed, *refs, layout, aligned):
    pieces = refs[:8]
    if aligned:
        results, (down_rows, up_rows, time_out, down_out, embed_out, up_out, sems) = refs[8:12], refs[12:]
    else:
        time_out, down_rows, up_rows = refs[8:]
    frame, head = me[0], me[1]
    chips, heads_axis, r1, p1, r3 = layout
    chans = time_out.shape[2]
    devices = 2 * chips * heads_axis
    for core in range(2):
        for idx in range(chips * heads_axis):
            hi, zi = idx // chips, idx % chips
            colors = []
            for color in range(2):
                off = hi if color == 0 else reversed_bits(hi, heads_axis)
                edge = heads_axis // 2
                src = pieces[4 * core + 2 * color + off // edge]
                colors.append(src[off % edge, zi].astype(F32))
            value = jnp.concatenate(colors, axis=0)
            owner = (frame ^ (reversed_bits(zi, chips) * 2 + core)) * heads_axis + (head ^ hi)
            down_rows[owner] = value[0:r1]
            up_rows[owner] = value[p1 : p1 + r1]

            @pl.when(owner < time_out.shape[0])
            def _():
                time_out[owner] = value[2 * p1 : 2 * p1 + r3, 0:chans]

    if aligned:
        buffers = (time_out, down_out, embed_out, up_out)
        copies = [pltpu.make_async_copy(buffers[i], results[i], sems.at[i]) for i in range(4)]
        copies[0].start()
        lanes = down_rows.shape[2]
        eye = (lax.broadcasted_iota(jnp.int32, (lanes, lanes), 0) == lax.broadcasted_iota(jnp.int32, (lanes, lanes), 1))
        eye = eye.astype(F32).astype(BF)
        flipped = nt(eye, down_rows[...].reshape(devices * r1, lanes).astype(BF))
        down_out[...] = flipped[0:chans]
        copies[1].start()
        embed_out[...] = embed[:, 0:1] * flipped[chans : chans + 1]
        copies[2].start()
        up_out[...] = nt(eye[0:chans], up_rows[...].reshape(devices * r1, lanes).astype(BF))
        copies[3].start()
        for copy in copies:
            copy.wait()


def double(x, axis, bits, dim):
    for bit in bits:
        got = swap(x, axis, bit)
        x = jnp.concatenate([x, got], axis=dim)
    return x


def cross(first, second, bits):
    for i, (a, b) in enumerate(zip(bits, reversed(bits))):
        first_in = swap(first, "heads", a)
        second_in = swap(second, "heads", b)
        if i + 1 < len(bits):
            first = jnp.concatenate([first, first_in], axis=0)
            second = jnp.concatenate([second, second_in], axis=0)
    return first, first_in, second, second_in


def body(clip, w_time, w_down, w_embed, w_qkv, w_out, w_up, timestep, cotangent):
    nf = lax.axis_size("frames")
    nh = lax.axis_size("heads")
    f = lax.axis_index("frames")
    h = lax.axis_index("heads")
    me = jnp.stack([f, h]).astype(jnp.int32)
    _, _, columns, chans = clip.shape
    width = w_down.shape[1]
    half_c = columns // 2
    half = half_c // 2
    quart = half // 2
    chips = nf // 2
    padded = round_up(chans + 2, 128)
    pieces = w_qkv.shape[1] // HD
    heads = pieces // 3
    chip_bits = [2 * b for b in reversed(bit_list(chips))]
    head_bits = bit_list(nh)
    devices = nf * nh

    clip_t = clip.transpose(0, 1, 3, 2)
    cot_t = cotangent.transpose(0, 1, 3, 2)
    w_qkv_t = w_qkv.T
    w_up_t = w_up.T

    keep, send = call(
        pool_kernel,
        [sds((2, 3, quart // 2, 2 * chans), BF)] * 2,
        in_specs=[smem(), vmem(), vmem()],
        out_specs=[vmem()] * 2,
        scratch_shapes=[pltpu.VMEM((3, half_c, chans), F32)],
    )(f.astype(jnp.int32).reshape(1), clip_t, cot_t)
    keep_in = swap(send, "frames", 1)
    block = jnp.concatenate([keep, keep_in], axis=1)
    block = double(block, "frames", chip_bits, 1)
    first, second = block[0][None], block[1][None]

    embed = time_embed(timestep, w_embed.shape[0])
    down, mix, out_mix, direct, embed_col = call(
        weight_kernel,
        [
            sds((padded, width), BF),
            sds((padded, pieces * SLOT), BF),
            sds((heads * SLOT, chans), BF),
            sds((padded, chans), BF),
            sds((embed.shape[0], SLOT), F32),
        ],
    )(w_down, w_embed, embed[None, :], w_qkv_t, w_out, w_up_t)

    def halo(x, after):
        head, tail = call(
            edge_kernel,
            [sds((2, chans, columns), BF)] * 2,
            in_specs=[vmem(), pl.BlockSpec(memory_space=pl.ANY)],
            out_specs=[vmem()] * 2,
        )(x, after)
        lo = lax.ppermute(tail, "frames", [(i, i + 1) for i in range(nf - 1)])
        hi = lax.ppermute(head, "frames", [(i + 1, i) for i in range(nf - 1)])
        return lo, hi

    cot_lo, cot_hi = halo(cot_t, keep)
    clip_lo, clip_hi = halo(clip_t, keep)
    tap_rows = round_up(3 * chans, devices * 8)
    tap_parts = call(
        fine_kernel,
        [sds((2 * tap_rows // nf, chans), BF)] * chips,
        in_specs=[smem()] + [vmem()] * 4,
        out_specs=[vmem()] * chips,
        scratch_shapes=[
            pltpu.VMEM((chans, 8 * columns), BF),
            pltpu.VMEM((chans, 4 * columns), BF),
            pltpu.VMEM((tap_rows, chans), F32),
        ],
    )(me, clip_t, cot_t, cot_lo, cot_hi)
    share = tap_rows // nf
    tap_got = [tap_parts[0]]
    for d in range(1, chips):
        tap_got.append(swap(tap_parts[d], "frames", 2 * d))
    tap_keep, tap_send = call(
        tap_kernel,
        [sds((share, chans), BF)] * 2,
        in_specs=[smem()] + [vmem()] * chips,
        out_specs=[vmem()] * 2,
    )(me, *tap_got)
    taps = (tap_keep, swap(tap_send, "frames", 1))

    chip_rows = 2 * width // nf
    r1 = width // devices
    p1 = round_up(r1, 8)
    r3 = share // nh
    piece_rows = round_up(2 * p1 + r3, 16)
    sides = cross(first, second, head_bits)
    simple = r1 == p1
    if simple:
        panes = -(-(chip_rows + SLOT - math.gcd(chip_rows, SLOT)) // SLOT)
        shift = chip_rows
        cells = (w_qkv_t, w_up_t, w_out, down)
    else:
        panes = -(-(2 * nh * p1) // SLOT)
        shift = 0
        start = (f >> 1) * chip_rows

        def columns_of(x):
            x = lax.dynamic_slice_in_dim(x, start, chip_rows, axis=1).reshape(x.shape[0], 2 * nh, r1)
            x = jnp.pad(x, ((0, 0), (0, 0), (0, p1 - r1))).reshape(x.shape[0], 2 * nh * p1)
            return jnp.pad(x, ((0, 0), (0, panes * SLOT - x.shape[1])))

        cells = tuple(columns_of(x) for x in (w_qkv_t, w_up_t, w_out, down))

    def pane(x, i):
        return pl.BlockSpec((x.shape[0], SLOT), lambda g, m: (0, ((m[0] >> 1) * shift) // SLOT + i))

    edge = nh // 2

    def side(mirrored, late):
        def index(g, m):
            at = reversed_bits(g, nh) if mirrored else g
            at = jnp.maximum(at - edge, 0) if late else jnp.minimum(at, edge - 1)
            return (at, 0, 0, 0)

        return pl.BlockSpec((1, nf * 3, quart // 2, 2 * chans), index)

    side_specs = [side(False, False), side(False, True), side(True, False), side(True, True)]
    total = 2 * nf * quart
    every = nh * total

    def whole(*shape):
        return pl.BlockSpec(shape, lambda *g: (0,) * len(shape))

    w_time2 = w_time.reshape(3 * chans, chans)
    statics = (w_time2, mix, out_mix, direct)
    window = panes * SLOT
    outs = [sds((6, 2, quart, chans), BF)] * nh + [
        sds((padded, round_up(pieces * HD, SLOT)), BF),
        sds((heads * HD, chans), BF),
        sds((nh, piece_rows, padded), BF),
        sds((nh, piece_rows, padded), BF),
    ]
    grid_spec = pltpu.PrefetchScalarGridSpec(
        num_scalar_prefetch=1,
        grid=(nh,),
        in_specs=side_specs + [whole(*x.shape) for x in statics] + [pane(x, i) for x in cells for i in range(panes)],
        out_specs=[whole(*x.shape) for x in outs],
        scratch_shapes=[
            pltpu.VMEM((2, nf * 3, quart // 2, 2 * chans), BF),
            pltpu.VMEM((every, tap_rows), BF),
            pltpu.VMEM((total, chans), F32),
            pltpu.VMEM((every, padded), BF),
            pltpu.VMEM((every, chans), BF),
            pltpu.VMEM((total, pieces * SLOT), BF),
            pltpu.VMEM((total, heads * SLOT), BF),
            pltpu.VMEM((every, heads * SLOT), BF),
            pltpu.VMEM((every, pieces * SLOT), BF),
            pltpu.VMEM((2 * heads, total // 2, total // 2), F32),
            pltpu.VMEM((2 * heads, total // 2, total // 2), F32),
            pltpu.VMEM((2 * heads, total // 2, total // 2), BF),
            pltpu.VMEM((2 * heads, total // 2, total // 2), BF),
            pltpu.VMEM((2 * nf, quart, chans), BF),
            pltpu.VMEM((every, chans), BF),
            pltpu.VMEM((window, padded), F32),
            pltpu.VMEM((window, padded), F32),
            pltpu.VMEM((2 * share, padded), F32),
        ],
    )
    rest = (p1, r3, piece_rows, panes, shift)
    results = call(
        functools.partial(coarse_kernel, coarse_frames=nf, heads_axis=nh, rest=rest),
        outs,
        grid_spec=grid_spec,
    )(me, *sides, *statics, *[x for x in cells for _ in range(panes)])
    local = results[:nh]
    mix_g, att_g, d_keep, d_send = results[nh:]

    d_got = swap(d_send, "frames", 1)
    ordered = call(
        functools.partial(order_kernel, at=2 * p1, taps=2),
        [sds((piece_rows, padded), BF)] * nh,
        in_specs=[smem()] + [vmem()] * 4,
        out_specs=[vmem()] * nh,
    )(me, d_keep, d_got, *taps)
    got = []
    for d in range(1, nh):
        got.append(swap(ordered[d], "heads", d))
    piece = call(sum_kernel, sds((piece_rows, padded), BF))(ordered[0], *got)
    piece = piece.reshape(2, 1, piece_rows // 2, padded)
    piece = double(piece, "frames", chip_bits, 1)
    shares = cross(piece[0][None], piece[1][None], head_bits)
    mates = []
    for x in shares:
        mates.append(swap(x, "frames", 1))

    got = []
    for d in range(1, nh):
        got.append(swap(local[d], "heads", d))
    four = sds((4, 2, quart, chans), BF)
    mine4, send4 = call(
        local_kernel,
        [four, four],
        in_specs=[smem()] + [vmem()] * nh,
        out_specs=[vmem()] * 2,
        scratch_shapes=[pltpu.VMEM(local[0].shape, F32)],
    )(me, local[0], *got)
    other4 = swap(send4, "frames", 1)
    mine4 = mine4.reshape(4, half, chans)
    other4 = other4.reshape(4, half, chans)
    output, grad_clip = call(
        functools.partial(finish_kernel, coarse_frames=nf),
        [sds(clip_t.shape, BF), sds(clip_t.shape, F32)],
        in_specs=[smem()] + [vmem()] * 9,
        out_specs=[vmem()] * 2,
        scratch_shapes=[pltpu.VMEM((chans, 8 * columns), BF)] * 2 + [pltpu.VMEM((4, half_c, chans), F32)],
    )(me, clip_t, cot_t, clip_lo, clip_hi, cot_lo, cot_hi, mine4, other4, w_time)

    mix_o = swap(mix_g, "frames", 1)
    att_o = swap(att_g, "frames", 1)
    step = 256
    early = 2
    wide = sds((pieces * HD, width), F32)
    scratch = [pltpu.VMEM((pieces * HD, padded), BF)]
    grad_qkv, grad_out = call(
        functools.partial(split_grad_kernel, late=False),
        [wide, sds((heads * HD, width), F32)],
        grid=(early,),
        in_specs=[
            pl.BlockSpec((padded, step), lambda g: (0, g)),
            whole(*mix_g.shape),
            whole(*mix_g.shape),
            whole(*att_g.shape),
            whole(*att_g.shape),
            whole(*w_up_t.shape),
        ],
        out_specs=[
            pl.BlockSpec((pieces * HD, step), lambda g: (0, g)),
            whole(heads * HD, width),
        ],
        scratch_shapes=scratch,
    )(down, mix_g, mix_o, att_g, att_o, w_up_t)
    grad_qkv = call(
        functools.partial(split_grad_kernel, late=True),
        wide,
        grid=(width // step - early,),
        in_specs=[
            pl.BlockSpec((padded, step), lambda g: (0, g + early)),
            whole(*mix_g.shape),
            whole(*mix_g.shape),
            pl.BlockSpec(memory_space=pl.ANY),
        ],
        out_specs=pl.BlockSpec((pieces * HD, step), lambda g: (0, g + early)),
        scratch_shapes=scratch,
        input_output_aliases={3: 0},
    )(down, mix_g, mix_o, grad_qkv)

    output, grad_clip, grad_qkv, grad_out, mates[3] = lax.optimization_barrier(
        (output, grad_clip, grad_qkv, grad_out, mates[3])
    )
    aligned = r1 % 8 == 0
    layout = (chips, nh, r1, p1, r3)
    outs = [sds((3 * chans // r3, r3, chans), F32)]
    table = (devices, r1, padded)
    scratch = []
    if aligned:
        outs += [sds((chans, width), F32), sds((w_embed.shape[0], width), F32), sds((chans, width), F32)]
        scratch = [pltpu.VMEM(table, F32)] * 2 + [pltpu.VMEM(x.shape, F32) for x in outs]
        scratch.append(pltpu.SemaphoreType.DMA((4,)))
    else:
        outs += [sds(table, F32)] * 2
    got = call(
        functools.partial(gather_kernel, layout=layout, aligned=aligned),
        outs,
        in_specs=[smem()] + [vmem()] * 9,
        out_specs=[pl.BlockSpec(memory_space=pl.ANY) if aligned else vmem()] * len(outs),
        scratch_shapes=scratch,
    )(me, embed_col, *shares, *mates)
    grad_time = got[0].reshape(w_time.shape)
    if aligned:
        grad_down, grad_embed, grad_up = got[1], got[2], got[3].T
    else:
        down_rows = got[1].reshape(width, padded)
        grad_down = down_rows[:, :chans].T
        grad_embed = embed_col[:, 0:1] * down_rows[:, chans][None, :]
        grad_up = got[2].reshape(width, padded)[:, :chans]
    return (
        output.transpose(0, 1, 3, 2),
        grad_clip.transpose(0, 1, 3, 2),
        grad_time,
        grad_down,
        grad_embed,
        grad_qkv.T,
        grad_out,
        grad_up,
    )


def solution(mesh):
    return jax.shard_map(
        body,
        mesh=mesh,
        in_specs=(
            P("frames", "heads", None, None),
            P(),
            P(),
            P(),
            P(None, "heads"),
            P("heads", None),
            P(),
            P(),
            P("frames", "heads", None, None),
        ),
        out_specs=(
            P("frames", "heads", None, None),
            P("frames", "heads", None, None),
            P(),
            P(),
            P(),
            P(None, "heads"),
            P("heads", None),
            P(),
        ),
        check_vma=False,
    )
```
